32 devices in a mesh: dp: 8 (over y, x, core), tensor: 4 (over z).
Axes of the slice: x: 2, y: 2, z: 4, core: 2. Of those that a mesh axis runs over, the one named last changes fastest.
Arguments:
- inputs: bfloat16 [4096, 1024], P(('dp', 'tensor')), may hold values from -6 to 6
- segments: int32 [4096], P('dp'), may hold values from 0 to 7, never falling along the last dimension, each value on 1 to 2000 neighbouring positions
- mixers_norm_gain: float32 [1024], replicated, may hold values from 0.5 to 1.5
- query_weight: bfloat16 [1024, 512], P(None, 'tensor'), may hold values from -0.1875 to 0.1875
- key_weight: bfloat16 [1024, 128], replicated, may hold values from -0.1875 to 0.1875
- value_weight: bfloat16 [1024, 128], replicated, may hold values from -0.1875 to 0.1875
- attention_out: bfloat16 [512, 1024], P('tensor'), may hold values from -2 to 2
- mamba_gate: bfloat16 [1024, 1536], P(None, 'tensor'), may hold values from -0.1875 to 0.1875
- mamba_input: bfloat16 [1024, 1536], P(None, 'tensor'), may hold values from -0.1875 to 0.1875
- state_weight: bfloat16 [1024, 256], replicated, may hold values from -0.1875 to 0.1875
- step_weight: bfloat16 [1024, 24], P(None, 'tensor'), may hold values from -0.1875 to 0.1875
- kernel_input: float32 [4, 1536], P(None, 'tensor'), may hold values from -3 to 3
- kernel_state: float32 [4, 256], replicated, may hold values from -3 to 3
- offset_input: float32 [1536], P('tensor'), may hold values from -3 to 3
- offset_state: float32 [256], replicated, may hold values from -3 to 3
- step_bias: float32 [24], P('tensor'), may hold values from -6 to -1
- decay_log: float32 [24], P('tensor'), may hold values from -3 to 1.5
- skip_gain: float32 [24], P('tensor'), may hold values from 0.5 to 2
- mamba_out: bfloat16 [1536, 1024], P('tensor'), may hold values from -0.15625 to 0.15625
- feedforward_norm_gain: float32 [1024], replicated, may hold values from 0.5 to 1.5
- gate_weight: bfloat16 [1024, 2048], P(None, 'tensor'), may hold values from -0.1875 to 0.1875
- up_weight: bfloat16 [1024, 2048], P(None, 'tensor'), may hold values from -0.1875 to 0.1875
- down_weight: bfloat16 [2048, 1024], P('tensor'), may hold values from -0.125 to 0.125
- cotangent: bfloat16 [4096, 1024], P(('dp', 'tensor')), may hold values from -6 to 6
Outputs:
- output: bfloat16 [4096, 1024], P(('dp', 'tensor'))
- block_input_gradient: float32 [4096, 1024], P(('dp', 'tensor'))
- grad_mixer_gain: float32 [1024], replicated
- grad_query_weight: float32 [1024, 512], P(None, 'tensor')
- grad_key_weight: float32 [1024, 128], replicated
- grad_value_weight: float32 [1024, 128], replicated
- grad_attention_out: float32 [512, 1024], P('tensor')
- grad_mamba_gate: float32 [1024, 1536], P(None, 'tensor')
- grad_mamba_input: float32 [1024, 1536], P(None, 'tensor')
- grad_state_weight: float32 [1024, 256], replicated
- grad_step_weight: float32 [1024, 24], P(None, 'tensor')
- grad_kernel_input: float32 [4, 1536], P(None, 'tensor')
- grad_kernel_state: float32 [4, 256], replicated
- grad_offset_input: float32 [1536], P('tensor')
- grad_offset_state: float32 [256], replicated
- grad_step_bias: float32 [24], P('tensor')
- grad_decay_log: float32 [24], P('tensor')
- grad_skip_gain: float32 [24], P('tensor')
- grad_mamba_out: float32 [1536, 1024], P('tensor')
- grad_feed_gain: float32 [1024], replicated
- grad_gate_weight: float32 [1024, 2048], P(None, 'tensor')
- grad_up_weight: float32 [1024, 2048], P(None, 'tensor')
- grad_down_weight: float32 [2048, 1024], P('tensor')
The draws below stay inside these ranges and needn't reach their ends.
Inputs may be any that keep to these rules, and one draw needn't show every extreme that they name: `segments`: segment numbers never fall along the tokens; each segment holds 1 to 2000 tokens and one holds exactly 2000.
All inputs are finite; a program needn't handle non-finite values.
Results may differ from the reference program's by a relative error of at most 0.018.
Values may be sent and summed in bfloat16 or wider, within the bound.
No kernel may reach another device: no remote copies, remote signals or barrier semaphores. Data moves between devices by JAX's collectives and lax.ppermute only.
A program may use at most 192 MiB of HBM per device.

```python
import math
import jax
import jax.numpy as jnp
import numpy as np
from jax import lax

D = 1024
QH = 8
KVH = 2
HD = 64
MH = 24
MP = 64
NS = 128
KC = 4
FF = 2048
L = 512
TOKENS = 4096
SEGS = 8
N_DP = 8


def steps_of(own_key, extent, cuts, least, high):
    level, own = 1.0, jax.random.fold_in(own_key, 6)
    for axis_at, parts in cuts:
        draws = jnp.exp(jax.random.uniform(jax.random.fold_in(own, axis_at), (parts,), jnp.float32, least / len(cuts), high / len(cuts)))
        level = level * jnp.repeat(draws, extent[axis_at] // parts).reshape([-1 if axis == axis_at else 1 for axis in range(len(extent))])
    return level


def split_up(number_of, total, bound, lean):
    weights = [(1 << 20) // math.isqrt(standing ** lean) + 1 for standing in range(2, number_of + 1)]
    surplus, counts = total - bound - (number_of - 1), [1] * (number_of - 1)
    while surplus > 0:
        free = [i for i in range(number_of - 1) if counts[i] < bound]
        pool, left = sum([weights[i] for i in free]), surplus
        for i in free:
            addition = min(bound - counts[i], max(1, left * weights[i] // pool), surplus)
            counts[i] = counts[i] + addition
            surplus = surplus - addition
    return np.array([bound] + counts)


def uneven_parts(own_key, count, total, limit, lean):
    if count == 2:
        one = jax.random.randint(own_key, (), max(1, total - limit), min(limit, total - 1) + 1)
        return jnp.stack([one, total - one])
    lengths = jnp.asarray(split_up(count, total, limit, lean), jnp.int32)
    twos = (count - 1) // 2
    giver, taker = lengths[1:1 + 2 * twos:2], lengths[2:2 + 2 * twos:2]
    slack = jnp.minimum(giver - 1, limit - taker)
    moved = jax.random.randint(jax.random.fold_in(own_key, 1), (twos,), 0, 1 << 20) % (slack + 1)
    lengths = lengths.at[1:1 + 2 * twos:2].set(giver - moved).at[2:2 + 2 * twos:2].set(taker + moved)
    return lengths[jax.random.permutation(jax.random.fold_in(own_key, 2), count)]


def centred(stream_key, extent, scale, most, shards=(), kind=jnp.bfloat16):
    factor_of = steps_of(stream_key, extent, shards, -0.22, 0.18) if shards else 1.0
    values = jax.random.normal(stream_key, extent, jnp.float32) * scale * factor_of
    return jnp.minimum(jnp.maximum(values, -most), most).astype(kind)


def setup_inputs(seed: int = 0) -> dict:
    arg_keys = jax.random.split(jax.random.key(seed), 25)
    inputs = centred(arg_keys[0], (TOKENS, D), 1.0, 6.0, ((0, 32),))
    segments = jnp.searchsorted(jnp.cumsum(uneven_parts(arg_keys[1], SEGS, TOKENS, 2000, 1)), jnp.arange(TOKENS), side="right").astype(jnp.int32)
    mixers_norm_gain = jnp.clip(1.0 + 0.1 * jax.random.normal(arg_keys[2], (D,), jnp.float32), 0.5, 1.5)
    query_weight = centred(arg_keys[3], (D, QH * HD), D ** -0.5, 0.1875, ((1, 4),))
    key_weight = centred(arg_keys[4], (D, KVH * HD), D ** -0.5, 0.1875)
    value_weight = centred(arg_keys[5], (D, KVH * HD), D ** -0.5, 0.1875)
    attention_out = centred(arg_keys[6], (QH * HD, D), (QH * HD // 64) ** -0.5, 2.0, ((0, 4),))
    mamba_gate = centred(arg_keys[7], (D, MH * MP), D ** -0.5, 0.1875, ((1, 4),))
    mamba_input = centred(arg_keys[8], (D, MH * MP), D ** -0.5, 0.1875, ((1, 4),))
    state_weight = centred(arg_keys[9], (D, 2 * NS), D ** -0.5, 0.1875)
    step_weight = centred(arg_keys[10], (D, MH), D ** -0.5, 0.1875, ((1, 4),))
    kernel_input = centred(arg_keys[11], (KC, MH * MP), KC ** -0.5, 3.0, ((1, 4),), jnp.float32)
    kernel_state = centred(arg_keys[12], (KC, 2 * NS), KC ** -0.5, 3.0, (), jnp.float32)
    offset_input = centred(arg_keys[13], (MH * MP,), 0.5, 3.0, ((0, 4),), jnp.float32)
    offset_state = centred(arg_keys[14], (2 * NS,), 0.5, 3.0, (), jnp.float32)
    step_bias = jnp.clip(-6.0 + 5.0 * jax.random.uniform(arg_keys[15], (MH,), jnp.float32) ** steps_of(arg_keys[15], (MH,), ((0, 4),), -0.2, 0.2), -6.0, -1.0)
    decay_log = jnp.clip(-3.0 + 4.5 * jax.random.uniform(arg_keys[16], (MH,), jnp.float32) ** steps_of(arg_keys[16], (MH,), ((0, 4),), -0.2, 0.2), -3.0, 1.5)
    skip_gain = jnp.clip(0.5 + 1.5 * jax.random.uniform(arg_keys[17], (MH,), jnp.float32) ** steps_of(arg_keys[17], (MH,), ((0, 4),), -0.2, 0.2), 0.5, 2.0)
    mamba_out = centred(arg_keys[18], (MH * MP, D), (MH * MP) ** -0.5, 0.15625, ((0, 4),))
    feedforward_norm_gain = jnp.clip(1.0 + 0.1 * jax.random.normal(arg_keys[19], (D,), jnp.float32), 0.5, 1.5)
    gate_weight = centred(arg_keys[20], (D, FF), D ** -0.5, 0.1875, ((1, 4),))
    up_weight = centred(arg_keys[21], (D, FF), D ** -0.5, 0.1875, ((1, 4),))
    down_weight = centred(arg_keys[22], (FF, D), FF ** -0.5, 0.125, ((0, 4),))
    cotangent = centred(arg_keys[23], (TOKENS, D), 1.0, 6.0, ((0, 32),))
    return {"inputs": inputs, "segments": segments, "mixers_norm_gain": mixers_norm_gain, "query_weight": query_weight, "key_weight": key_weight, "value_weight": value_weight, "attention_out": attention_out, "mamba_gate": mamba_gate, "mamba_input": mamba_input, "state_weight": state_weight, "step_weight": step_weight, "kernel_input": kernel_input, "kernel_state": kernel_state, "offset_input": offset_input, "offset_state": offset_state, "step_bias": step_bias, "decay_log": decay_log, "skip_gain": skip_gain, "mamba_out": mamba_out, "feedforward_norm_gain": feedforward_norm_gain, "gate_weight": gate_weight, "up_weight": up_weight, "down_weight": down_weight, "cotangent": cotangent}


eps = 1e-05
att_block = 512
ssd_block = 256
big_negative = -1e+30

def tdot(left, right):
    return lax.dot_general(left, right, (((0,), (0,)), ((), ())), preferred_element_type=jnp.float32)

def dot_t(left, right):
    return lax.dot_general(left, right, (((1,), (1,)), ((), ())), preferred_element_type=jnp.float32)

def tdot_high(left, right):
    return lax.dot_general(left, right, (((0,), (0,)), ((), ())), precision=lax.Precision.HIGHEST, preferred_element_type=jnp.float32)

def dot_t_high(left, right):
    return lax.dot_general(left, right, (((1,), (1,)), ((), ())), precision=lax.Precision.HIGHEST, preferred_element_type=jnp.float32)

def conv_silu(signal, taps, offset, segment):
    acc = offset[None, :] + taps[0][None, :] * signal
    for shift_by in range(1, taps.shape[0]):
        shifted = jnp.concatenate([jnp.zeros((shift_by, signal.shape[1]), signal.dtype), signal[:-shift_by]], 0)
        seg_back = jnp.concatenate([jnp.full((shift_by,), -1, jnp.int32), segment[:-shift_by]], 0)
        linked = (seg_back == segment).astype(signal.dtype)[:, None]
        acc = acc + taps[shift_by][None, :] * shifted * linked
    return jax.nn.silu(acc)

def mamba_core(xin, bcst, step_raw, kernel_input, kernel_state, offset_input, offset_state, step_bias, decay_log, skip_gain, segment):
    head_count = step_raw.shape[1]
    width = xin.shape[1]
    head_size = width // head_count
    state_size = bcst.shape[1] // 2
    length = xin.shape[0]
    act = conv_silu(jnp.concatenate([xin, bcst], 1), jnp.concatenate([kernel_input, kernel_state], 1), jnp.concatenate([offset_input, offset_state], 0), segment)
    xconv = act[:, :width].reshape(length, head_count, head_size)
    bstate = act[:, width:width + state_size]
    cstate = act[:, width + state_size:]
    delta_t = jax.nn.softplus(step_raw + step_bias[None, :])
    log_decay = delta_t * (-jnp.exp(decay_log))[None, :]
    block = min(ssd_block, length)
    blocks = length // block
    before = jnp.concatenate([jnp.full((1,), -1, jnp.int32), segment[block - 1::block][:-1]], 0)
    items = (xconv.reshape(blocks, block, head_count, head_size), bstate.reshape(blocks, block, state_size), cstate.reshape(blocks, block, state_size), delta_t.reshape(blocks, block, head_count), log_decay.reshape(blocks, block, head_count), segment.reshape(blocks, block), before)
    lower = jnp.arange(block, dtype=jnp.int32)[:, None] >= jnp.arange(block, dtype=jnp.int32)[None, :]

    def advance(state, pieces):
        x_rows, b_rows, c_rows, dt_rows, decay_rows, seg_rows, seg_before = pieces
        running = jnp.cumsum(decay_rows, axis=0)
        linked = lower & (seg_rows[:, None] == seg_rows[None, :])
        spread = running[:, None, :] - running[None, :, :]
        weights = jnp.exp(jnp.where(linked[:, :, None], spread, 0.0)) * linked.astype(jnp.float32)[:, :, None]
        inner_cb = jnp.dot(c_rows, b_rows.T, precision=lax.Precision.HIGHEST)
        mixing = weights * inner_cb[:, :, None] * dt_rows[None, :, :]
        inner = jnp.einsum('tsh,shp->thp', mixing, x_rows, precision=lax.Precision.HIGHEST)
        alive = (seg_rows == seg_before).astype(jnp.float32)[:, None] * jnp.exp(running)
        carried = jnp.einsum('tn,hpn->thp', c_rows, state, precision=lax.Precision.HIGHEST) * alive[:, :, None]
        y_rows = inner + carried + skip_gain[None, :, None] * x_rows
        end_live = (seg_rows == seg_rows[-1]).astype(jnp.float32)[:, None]
        end_weight = jnp.exp(running[-1][None, :] - running) * end_live * dt_rows
        keep_all = jnp.exp(running[-1]) * (seg_rows[-1] == seg_before).astype(jnp.float32)
        fresh = jnp.einsum('sh,shp,sn->hpn', end_weight, x_rows, b_rows, precision=lax.Precision.HIGHEST)
        return (state * keep_all[:, None, None] + fresh, y_rows)
    start_state = jnp.zeros((head_count, head_size, state_size), jnp.float32)
    _, outputs = lax.scan(advance, start_state, items)
    return outputs.reshape(length, width)

def score_block(query, keys, segment, index):
    length = keys.shape[0]
    scale = query.shape[-1] ** (-0.5)
    start = index * att_block
    q_rows = lax.dynamic_slice_in_dim(query, start, att_block, 0)
    row_pos = start + jnp.arange(att_block, dtype=jnp.int32)
    row_seg = lax.dynamic_slice_in_dim(segment, start, att_block, 0)
    positions = jnp.arange(length, dtype=jnp.int32)
    scores = jnp.einsum('qhd,khd->hqk', q_rows.astype(jnp.float32), keys.astype(jnp.float32)) * scale
    allowed = (row_pos[:, None] >= positions[None, :]) & (row_seg[:, None] == segment[None, :])
    return (jnp.where(allowed[None], scores, big_negative), q_rows)

def attend_forward(query, keys, values, segment):
    length, head_count, head_size = query.shape
    blocks = length // att_block

    def one_block(index):
        scores, _ = score_block(query, keys, segment, index)
        top = lax.optimization_barrier(jnp.max(scores, axis=-1))
        expo = jnp.exp(scores - top[:, :, None])
        total = lax.optimization_barrier(jnp.sum(expo, axis=-1))
        probs = (expo / total[:, :, None]).astype(jnp.bfloat16)
        outs = jnp.einsum('hqk,khd->qhd', probs.astype(jnp.float32), values.astype(jnp.float32))
        return (outs.astype(jnp.bfloat16), top + jnp.log(total))
    outs, logsum = lax.map(one_block, jnp.arange(blocks, dtype=jnp.int32))
    return (outs.reshape(length, head_count, head_size), logsum)

def attend_backward(query, keys, values, attention, logsum, dattention, segment):
    length, head_count, head_size = query.shape
    scale = head_size ** (-0.5)
    blocks = length // att_block
    delta = lax.optimization_barrier(jnp.sum(dattention.astype(jnp.float32) * attention.astype(jnp.float32), axis=-1))

    def one_block(carry, index):
        dkey, dvalue = carry
        scores, q_rows = score_block(query, keys, segment, index)
        start = index * att_block
        d_rows = lax.dynamic_slice_in_dim(dattention, start, att_block, 0)
        delta_rows = lax.dynamic_slice_in_dim(delta, start, att_block, 0)
        probs = jnp.exp(scores - logsum[index][:, :, None])
        dprob = jnp.einsum('qhd,khd->hqk', d_rows.astype(jnp.float32), values.astype(jnp.float32))
        dscore = (probs * (dprob - delta_rows.T[:, :, None]) * scale).astype(jnp.bfloat16)
        dq_rows = jnp.einsum('hqk,khd->qhd', dscore.astype(jnp.float32), keys.astype(jnp.float32))
        dkey = dkey + jnp.einsum('hqk,qhd->khd', dscore.astype(jnp.float32), q_rows.astype(jnp.float32))
        dvalue = dvalue + jnp.einsum('hqk,qhd->khd', probs.astype(jnp.bfloat16).astype(jnp.float32), d_rows.astype(jnp.float32))
        return ((dkey, dvalue), dq_rows)
    empty = jnp.zeros((length, head_count, head_size), jnp.float32)
    (dkey, dvalue), dquery = lax.scan(one_block, (empty, empty), jnp.arange(blocks, dtype=jnp.int32))
    return (dquery.reshape(length, head_count, head_size).astype(jnp.bfloat16), dkey.astype(jnp.bfloat16), dvalue.astype(jnp.bfloat16))

def rms_recip(values):
    return lax.rsqrt(lax.optimization_barrier(jnp.mean(values * values, axis=-1, keepdims=True)) + eps)

def sequence_pass(seq_inputs, seq_cotangent, segment, params):
    mixers_norm_gain, query_weight, key_weight, value_weight, attention_out, mamba_gate, mamba_input, state_weight, step_weight, kernel_input, kernel_state, offset_input, offset_state, step_bias, decay_log, skip_gain, mamba_out, feedforward_norm_gain, gate_weight, up_weight, down_weight = params
    length = seq_inputs.shape[0]
    group = QH // KVH
    inputs_float = seq_inputs.astype(jnp.float32)
    reciprocal_first = rms_recip(inputs_float)
    unit_input_first = inputs_float * reciprocal_first
    normed_first = (unit_input_first * mixers_norm_gain[None, :]).astype(jnp.bfloat16)
    query = jnp.dot(normed_first, query_weight, preferred_element_type=jnp.float32).astype(jnp.bfloat16).reshape(length, QH, HD)
    keys = jnp.dot(normed_first, key_weight, preferred_element_type=jnp.float32).astype(jnp.bfloat16).reshape(length, KVH, HD)
    values = jnp.dot(normed_first, value_weight, preferred_element_type=jnp.float32).astype(jnp.bfloat16).reshape(length, KVH, HD)
    keys_rep = jnp.repeat(keys, group, axis=1)
    values_rep = jnp.repeat(values, group, axis=1)
    attention, logsum = attend_forward(query, keys_rep, values_rep, segment)
    attention_flat = attention.reshape(length, QH * HD)
    zgate = jnp.dot(normed_first, mamba_gate, preferred_element_type=jnp.float32)
    xin = jnp.dot(normed_first, mamba_input, preferred_element_type=jnp.float32)
    bcst = jnp.dot(normed_first, state_weight, preferred_element_type=jnp.float32)
    step_raw = jnp.dot(normed_first, step_weight, preferred_element_type=jnp.float32)

    def core(xin_, bcst_, step_, kin, kst, oin, ost, sbias, dlog, skip):
        return mamba_core(xin_, bcst_, step_, kin, kst, oin, ost, sbias, dlog, skip, segment)
    ssm_y, core_vjp = jax.vjp(core, xin, bcst, step_raw, kernel_input, kernel_state, offset_input, offset_state, step_bias, decay_log, skip_gain)
    zsig = jax.nn.sigmoid(zgate)
    gated = (ssm_y * zgate * zsig).astype(jnp.bfloat16)
    mixed = jnp.dot(attention_flat, attention_out, preferred_element_type=jnp.float32) + jnp.dot(gated, mamba_out, preferred_element_type=jnp.float32)
    hidden_first = inputs_float + mixed
    reciprocal_second = rms_recip(hidden_first)
    unit_input_second = hidden_first * reciprocal_second
    normed_second = (unit_input_second * feedforward_norm_gain[None, :]).astype(jnp.bfloat16)
    gate_pre = jnp.dot(normed_second, gate_weight, preferred_element_type=jnp.float32)
    up_pre = jnp.dot(normed_second, up_weight, preferred_element_type=jnp.float32)
    gsig = jax.nn.sigmoid(gate_pre)
    hidden = (gate_pre * gsig * up_pre).astype(jnp.bfloat16)
    output = (hidden_first + jnp.dot(hidden, down_weight, preferred_element_type=jnp.float32)).astype(jnp.bfloat16)
    cotangent_float = seq_cotangent.astype(jnp.float32)
    grad_down = tdot(hidden, seq_cotangent)
    dhidden = dot_t(seq_cotangent, down_weight)
    dup = (dhidden * gate_pre * gsig).astype(jnp.bfloat16)
    dgate = (dhidden * up_pre * gsig * (1.0 + gate_pre * (1.0 - gsig))).astype(jnp.bfloat16)
    grad_gate = tdot(normed_second, dgate)
    grad_up = tdot(normed_second, dup)
    grad_normed_second = dot_t(dgate, gate_weight) + dot_t(dup, up_weight)
    feedforward_grad = lax.optimization_barrier(jnp.sum(grad_normed_second * unit_input_second, axis=0))
    scaled_second = grad_normed_second * feedforward_norm_gain[None, :]
    grad_hidden_first = cotangent_float + reciprocal_second * (scaled_second - unit_input_second * lax.optimization_barrier(jnp.mean(scaled_second * unit_input_second, axis=-1, keepdims=True)))
    dmixed = grad_hidden_first.astype(jnp.bfloat16)
    grad_attn_out = tdot(attention_flat, dmixed)
    dattention = dot_t(dmixed, attention_out).astype(jnp.bfloat16).reshape(length, QH, HD)
    dquery, dkey, dvalue = attend_backward(query, keys_rep, values_rep, attention, logsum, dattention, segment)
    dquery_flat = dquery.reshape(length, QH * HD)
    dkey_flat = dkey.reshape(length, QH * HD)
    dvalue_flat = dvalue.reshape(length, QH * HD)
    grad_query = tdot(normed_first, dquery_flat)
    grad_key = tdot(normed_first, dkey_flat).reshape(D, KVH, group, HD).sum(axis=2).reshape(D, KVH * HD)
    grad_value = tdot(normed_first, dvalue_flat).reshape(D, KVH, group, HD).sum(axis=2).reshape(D, KVH * HD)
    key_rep_w = jnp.repeat(key_weight.reshape(D, KVH, HD), group, axis=1).reshape(D, QH * HD)
    value_rep_w = jnp.repeat(value_weight.reshape(D, KVH, HD), group, axis=1).reshape(D, QH * HD)
    grad_normed_first = dot_t(dquery_flat, query_weight) + dot_t(dkey_flat, key_rep_w) + dot_t(dvalue_flat, value_rep_w)
    grad_mamba_out = tdot(gated, dmixed)
    dgated = dot_t(dmixed, mamba_out)
    dssm = dgated * zgate * zsig
    dzgate = (dgated * ssm_y * zsig * (1.0 + zgate * (1.0 - zsig))).astype(jnp.bfloat16)
    core_grads = core_vjp(dssm)
    dxin = core_grads[0].astype(jnp.bfloat16)
    dbcst = core_grads[1]
    dstep = core_grads[2].astype(jnp.bfloat16)
    grad_mgate = tdot(normed_first, dzgate)
    grad_minput = tdot(normed_first, dxin)
    grad_step = tdot(normed_first, dstep)
    grad_state = tdot_high(normed_first.astype(jnp.float32), dbcst)
    grad_normed_first = grad_normed_first + dot_t(dzgate, mamba_gate) + dot_t(dxin, mamba_input) + dot_t(dstep, step_weight)
    grad_normed_first = grad_normed_first + dot_t_high(dbcst, state_weight.astype(jnp.float32))
    mixers_grad = lax.optimization_barrier(jnp.sum(grad_normed_first * unit_input_first, axis=0))
    scaled_first = grad_normed_first * mixers_norm_gain[None, :]
    block_input_gradient = grad_hidden_first + reciprocal_first * (scaled_first - unit_input_first * lax.optimization_barrier(jnp.mean(scaled_first * unit_input_first, axis=-1, keepdims=True)))
    grads = (mixers_grad, grad_query, grad_key, grad_value, grad_attn_out, grad_mgate, grad_minput, grad_state, grad_step, core_grads[3], core_grads[4], core_grads[5], core_grads[6], core_grads[7], core_grads[8], core_grads[9], grad_mamba_out, feedforward_grad, grad_gate, grad_up, grad_down)
    return (output, block_input_gradient, grads)

def reference(inputs, segments, mixers_norm_gain, query_weight, key_weight, value_weight, attention_out, mamba_gate, mamba_input, state_weight, step_weight, kernel_input, kernel_state, offset_input, offset_state, step_bias, decay_log, skip_gain, mamba_out, feedforward_norm_gain, gate_weight, up_weight, down_weight, cotangent):
    params = (mixers_norm_gain, query_weight, key_weight, value_weight, attention_out, mamba_gate, mamba_input, state_weight, step_weight, kernel_input, kernel_state, offset_input, offset_state, step_bias, decay_log, skip_gain, mamba_out, feedforward_norm_gain, gate_weight, up_weight, down_weight)
    items = (inputs.reshape(N_DP, L, D), cotangent.reshape(N_DP, L, D), segments.reshape(N_DP, L))
    start = tuple((jnp.zeros(param.shape, jnp.float32) for param in params))

    def advance(totals, pieces):
        output, block_input_gradient, grads = sequence_pass(pieces[0], pieces[1], pieces[2], params)
        return (tuple((total + grad for total, grad in zip(totals, grads))), (output, block_input_gradient))
    grads, (outputs, input_grads) = lax.scan(advance, start, items)
    return (outputs.reshape(TOKENS, D), input_grads.reshape(TOKENS, D), grads[0], grads[1], grads[2], grads[3], grads[4], grads[5], grads[6], grads[7], grads[8], grads[9], grads[10], grads[11], grads[12], grads[13], grads[14], grads[15], grads[16], grads[17], grads[18], grads[19], grads[20])
```

```python
import functools

import jax
import jax.numpy as jnp
from jax import lax
from jax.experimental import pallas as pl
from jax.experimental.pallas import tpu as pltpu
from jax.sharding import PartitionSpec as P


QH = 8
KVH = 2
HD = 64
LANES = 128

eps = 1e-05
big_negative = -1e30
f32 = jnp.float32
bf16 = jnp.bfloat16


def dot(left, right):
    return jnp.dot(left, right, preferred_element_type=f32)


def tdot(left, right):
    return lax.dot_general(left, right, (((0,), (0,)), ((), ())), preferred_element_type=f32)


def dot_t(left, right):
    return lax.dot_general(left, right, (((1,), (1,)), ((), ())), preferred_element_type=f32)


def split3(value):
    high = value.astype(bf16)
    rest = value - high.astype(f32)
    mid = rest.astype(bf16)
    return high, mid, (rest - mid.astype(f32)).astype(bf16)


def exact_left(mask, value):
    high, mid, low = split3(value)
    return dot(mask, high) + (dot(mask, mid) + dot(mask, low))


def rms_recip(values):
    return lax.rsqrt(jnp.mean(values * values, axis=-1, keepdims=True) + eps)


def sigmoid(value):
    return 1.0 / (1.0 + jnp.exp(-value))


def lane_ids(rows, width):
    return lax.broadcasted_iota(jnp.int32, (rows, width), 1)


def pair_columns(values, pair, lanes):
    first = values[:, 2 * pair : 2 * pair + 1]
    second = values[:, 2 * pair + 1 : 2 * pair + 2]
    return jnp.where(lanes < HD, first, second)


def fwd_body(widths, taps_count, heads, tensor, *refs):
    (t_ref,) = refs[:1]
    parts = refs[1 : 1 + tensor]
    (
        seg_ref,
        gain_ref,
        query_w_ref,
        kv_w_ref,
        gate_w_ref,
        input_w_ref,
        state_w_ref,
        step_w_ref,
        taps_ref,
        offs_ref,
        bias_ref,
        nega_ref,
        skip_ref,
        att_w_ref,
        mam_w_ref,
        n1_ref,
        qkv_ref,
        att_ref,
        stat_ref,
        z_ref,
        u_ref,
        acc_ref,
        ysum_ref,
        gated_ref,
        raw_ref,
        mask_ref,
        g_ref,
        run_ref,
        run_t_ref,
        dt_ref,
        link_ref,
        *mixed_refs,
        mixed_ref,
        query_v,
        att_v,
        mam_v,
        sems,
    ) = refs[1 + tensor :]
    wq, _, _, wx, wbc, _ = widths
    copies = Copies(sems)
    for source, target in (
        (query_w_ref, query_v),
        (att_w_ref, att_v),
        (mam_w_ref, mam_v),
    ):
        copies.start(source, target)
    t = t_ref[0]
    rows = parts[0].shape[0]
    length = rows * tensor
    state = wbc // 2
    for k in range(tensor):
        xf = parts[k][...].astype(f32)
        normed = (xf * rms_recip(xf) * gain_ref[...]).astype(bf16)
        n1_ref[pl.ds(pl.multiple_of((t ^ k) * rows, rows), rows), :] = normed
    n1 = n1_ref[...]
    seg_row = seg_ref[0:1, :].astype(f32)
    seg_col = jnp.broadcast_to(seg_row, (LANES, length)).T
    row_pos = lax.broadcasted_iota(jnp.int32, (length, length), 0)
    col_pos = lax.broadcasted_iota(jnp.int32, (length, length), 1)
    allowed = (row_pos >= col_pos) & (seg_col[:, 0:1] == seg_row)
    mask_ref[...] = jnp.where(allowed, 0.0, big_negative)
    copies.wait(0, 1)
    query = dot(n1, query_v[...]).astype(bf16)
    kv = dot(n1, kv_w_ref[...])
    lanes = lane_ids(length, LANES)
    kv_swap = pltpu.roll(kv, HD, 1)
    keys2 = jnp.where(lanes < HD, kv, kv_swap).astype(bf16)
    values2 = jnp.where(lanes < HD, kv_swap, kv).astype(bf16)
    qkv_ref[:, 0:wq] = query
    qkv_ref[:, wq : wq + LANES] = keys2
    qkv_ref[:, wq + LANES :] = values2
    z_ref[...] = dot(n1, gate_w_ref[...])
    u_ref[:, :wx] = dot(n1, input_w_ref[...])
    u_ref[:, wx:] = dot(n1, state_w_ref[...])
    raw = dot_t(n1, step_w_ref[...]) + bias_ref[...]
    raw_ref[...] = raw

    lane_lo = lanes < HD
    scale = HD ** (-0.5)
    half = length // 2
    for block in range(2):
        lo, hi = block * half, (block + 1) * half
        out = jnp.zeros((half, LANES), f32)
        stats = []
        for head in range(2):
            keep = lane_lo[:half] if head == 0 else ~lane_lo[:half]
            keep_v = lane_lo[:hi] if head == 0 else ~lane_lo[:hi]
            q_rows = jnp.where(keep, query[lo:hi].astype(f32), 0.0).astype(bf16)
            scores = dot_t(q_rows, keys2[:hi]) * scale + mask_ref[lo:hi, 0:hi]
            top = jnp.max(scores, axis=-1, keepdims=True)
            expo = jnp.exp(scores - top)
            total = jnp.sum(expo, axis=-1, keepdims=True)
            probs = (expo / total).astype(bf16)
            v_rows = jnp.where(keep_v, values2[:hi].astype(f32), 0.0).astype(bf16)
            out = out + dot(probs, v_rows)
            stats.append(top + jnp.log(total))
        att_ref[lo:hi, :] = out.astype(bf16)
        stat_ref[lo:hi, :] = jnp.where(lane_lo[:half], stats[0], stats[1])

    u = u_ref[...]
    acc = offs_ref[...] + taps_ref[0:1, :] * u
    spots = lax.broadcasted_iota(jnp.int32, (length, LANES), 0)
    for shift_by in range(1, taps_count):
        linked = (pltpu.roll(seg_col, shift_by, 0) == seg_col) & (spots >= shift_by)
        linked = jnp.where(linked, 1.0, 0.0)
        link_ref[shift_by - 1] = linked
        acc = acc + taps_ref[shift_by : shift_by + 1, :] * (
            linked[:, 0:1] * pltpu.roll(u, shift_by, 0)
        )
    acc_ref[...] = acc

    dt = jnp.maximum(raw, 0.0) + jnp.log1p(jnp.exp(-jnp.abs(raw)))
    tri = (row_pos >= col_pos).astype(f32).astype(bf16)
    run = exact_left(tri, dt * nega_ref[...])
    run_t = run.T
    dt_ref[...] = dt
    run_ref[...] = run
    run_t_ref[...] = run_t
    bc = acc_ref[:, wx:]
    bc = (bc * sigmoid(bc)).astype(bf16)
    g_ref[...] = dot_t(bc[:, state:], bc[:, :state])
    for pair in range(heads // 2):
        cols = slice(pair * LANES, (pair + 1) * LANES)
        xa = acc_ref[:, cols]
        xc = xa * sigmoid(xa)
        uu = xc * pair_columns(dt, pair, lanes)
        u_lo = jnp.where(lane_lo, uu, 0.0).astype(bf16)
        u_hi = jnp.where(lane_lo, 0.0, uu).astype(bf16)
        for block in range(2):
            lo, hi = block * half, (block + 1) * half
            total = jnp.zeros((half, LANES), f32)
            for side, masked in ((0, u_lo), (1, u_hi)):
                head = 2 * pair + side
                spread = run[lo:hi, head : head + 1] - run_t[head : head + 1, 0:hi]
                weight = jnp.exp(spread + mask_ref[lo:hi, 0:hi])
                mixing = (weight * g_ref[lo:hi, 0:hi]).astype(bf16)
                total = total + dot(mixing, masked[:hi])
            ysum_ref[lo:hi, cols] = total
        y = ysum_ref[:, cols] + skip_ref[0:1, cols] * xc
        z = z_ref[:, cols]
        gated_ref[:, cols] = (y * z * sigmoid(z)).astype(bf16)
    copies.wait(1)
    mixed = dot(att_ref[...], att_v[...]) + dot(gated_ref[...], mam_v[...])
    mixed_ref[...] = mixed.astype(bf16)
    for k in range(tensor):
        mixed_refs[k][...] = mixed_ref[pl.ds(pl.multiple_of((t ^ k) * rows, rows), rows), :]


def attention_bwd_body(widths, heads, tensor, *refs):
    t_ref = refs[0]
    dparts = refs[1 : 1 + tensor]
    (
        skip_ref,
        att_w_ref,
        mam_w_ref,
        mask_ref,
        qkv_ref,
        att_ref,
        stat_ref,
        z_ref,
        acc_ref,
        ysum_ref,
        gated_ref,
        n1_ref,
        d_ref,
        dssm_ref,
        keep_ref,
        send_ref,
        dmixed_ref,
    ) = refs[1 + tensor :]
    wq, wkv, _, wx, _, _ = widths
    t = t_ref[0]
    rows = dparts[0].shape[0]
    length = rows * tensor
    for k in range(tensor):
        dmixed_ref[pl.ds(pl.multiple_of((t ^ k) * rows, rows), rows), :] = dparts[k][...]
    dmixed = dmixed_ref[...]
    lane_lo = lane_ids(length, LANES) < HD
    half = length // 2
    scale = HD ** (-0.5)

    datt = dot_t(dmixed, att_w_ref[...]).astype(bf16)
    datt_f = datt.astype(f32)
    prod = datt_f * att_ref[...].astype(f32)
    query = qkv_ref[:, 0:wq]
    keys2 = qkv_ref[:, wq : wq + LANES]
    values2 = qkv_ref[:, wq + LANES :]
    stat = stat_ref[...]
    dq = [jnp.zeros((half, LANES), f32) for _ in range(2)]
    dk = [jnp.zeros((half, LANES), f32) for _ in range(2)]
    dv = [jnp.zeros((half, LANES), f32) for _ in range(2)]
    for head in range(2):
        keep = lane_lo if head == 0 else ~lane_lo
        q_m = jnp.where(keep, query.astype(f32), 0.0).astype(bf16)
        k_m = jnp.where(keep, keys2.astype(f32), 0.0).astype(bf16)
        d_m = jnp.where(keep, datt_f, 0.0).astype(bf16)
        delta = jnp.sum(jnp.where(keep, prod, 0.0), axis=-1, keepdims=True)
        logsum = stat[:, head * HD : head * HD + 1]
        for block in range(2):
            lo, hi = block * half, (block + 1) * half
            scores = dot_t(q_m[lo:hi], keys2[:hi]) * scale + mask_ref[lo:hi, 0:hi]
            probs = jnp.exp(scores - logsum[lo:hi])
            dprob = dot_t(d_m[lo:hi], values2[:hi])
            dscore = (probs * (dprob - delta[lo:hi]) * scale).astype(bf16)
            dq[block] = dq[block] + dot(dscore, k_m[:hi])
            dk_add = tdot(dscore, q_m[lo:hi])
            dv_add = tdot(probs.astype(bf16), d_m[lo:hi])
            for part in range(block + 1):
                dk[part] = dk[part] + dk_add[part * half : (part + 1) * half]
                dv[part] = dv[part] + dv_add[part * half : (part + 1) * half]
    for block in range(2):
        lo, hi = block * half, (block + 1) * half
        d_ref[lo:hi, 0:wq] = dq[block].astype(bf16)
        dk_sum = dk[block] + pltpu.roll(dk[block], HD, 1)
        dv_sum = dv[block] + pltpu.roll(dv[block], HD, 1)
        d_ref[lo:hi, wq : wq + wkv] = jnp.where(lane_lo[:half], dk_sum, dv_sum).astype(bf16)

    base = wq + wkv
    for pair in range(heads // 2):
        cols = slice(pair * LANES, (pair + 1) * LANES)
        xa = acc_ref[:, cols]
        xc = xa * sigmoid(xa)
        z = z_ref[:, cols]
        zs = sigmoid(z)
        dgated = dot_t(dmixed, mam_w_ref[cols, :])
        dssm_ref[:, cols] = dgated * z * zs
        y = ysum_ref[:, cols] + skip_ref[0:1, cols] * xc
        dz = dgated * y * zs * (1.0 + z * (1.0 - zs))
        d_ref[:, base + pair * LANES : base + (pair + 1) * LANES] = dz.astype(bf16)
    upper = t_ref[1] % 2
    n1 = n1_ref[...]
    gz = tdot(d_ref[:, base:], n1)
    split_store(upper, tdot(att_ref[...], dmixed), gz[wx - wq :], keep_ref, send_ref, 0)
    second = jnp.concatenate([gz[: wx - wq], tdot(d_ref[:, :wq], n1)], 0)
    split_store(upper, tdot(gated_ref[...], dmixed), second, keep_ref, send_ref, wq)


def state_bwd_body(widths, taps_count, heads, tensor, *refs):
    (
        t_ref,
        gain_ref,
        query_w_ref,
        kv_w_ref,
        gate_w_ref,
        input_w_ref,
        state_w_ref,
        step_w_ref,
        taps_ref,
        nega_ref,
        skip_ref,
        mask_ref,
        g_ref,
        run_ref,
        run_t_ref,
        dt_ref,
        link_ref,
        n1_ref,
        u_ref,
        acc_ref,
        ysum_ref,
        raw_ref,
        d1_ref,
        dssm_ref,
        gfeed_ref,
    ) = refs[:25]
    (
        keep_ref,
        send_ref,
        *dn1_refs,
        d2_ref,
        small_ref,
        dn1_ref,
        dg_ref,
        dact_ref,
        rows_ref,
    ) = refs[25:]
    wq, wkv, _, wx, wbc, _ = widths
    t = t_ref[0]
    length = n1_ref.shape[0]
    rows = length // tensor
    state = wbc // 2
    lanes = lane_ids(length, LANES)
    lane_lo = lanes < HD
    half = length // 2

    raw = raw_ref[...]
    dt = dt_ref[...]
    ld = dt * nega_ref[...]
    run = run_ref[...]
    run_t = run_t_ref[...]
    bc_acc = acc_ref[:, wx:]
    bc = (bc_acc * sigmoid(bc_acc)).astype(bf16)
    dg_ref[...] = jnp.zeros((length, length), f32)
    drun = jnp.zeros((length, LANES), f32)
    ddt = jnp.zeros((length, LANES), f32)
    skip_row = jnp.zeros((1, LANES), f32)
    small_ref[...] = jnp.zeros(small_ref.shape, f32)
    for pair in range(heads // 2):
        cols = slice(pair * LANES, (pair + 1) * LANES)
        xa = acc_ref[:, cols]
        xc = xa * sigmoid(xa)
        skip = skip_ref[0:1, cols]
        ysum = ysum_ref[:, cols]
        dssm = dssm_ref[:, cols]
        dskip = jnp.sum(dssm * xc, axis=0, keepdims=True)
        for side in range(2):
            keep = lane_lo[0:1] if side == 0 else ~lane_lo[0:1]
            head_sum = jnp.sum(jnp.where(keep, dskip, 0.0), axis=-1, keepdims=True)
            skip_row = jnp.where(lanes[0:1] == 2 * pair + side, head_sum, skip_row)
        dt_pair = pair_columns(dt, pair, lanes)
        u_b = (xc * dt_pair).astype(bf16)
        dy_b = dssm.astype(bf16)
        u_f = u_b.astype(f32)
        dy_f = dy_b.astype(f32)
        du = [jnp.zeros((half, LANES), f32) for _ in range(2)]
        for side in range(2):
            head = 2 * pair + side
            keep = lane_lo if side == 0 else ~lane_lo
            dy_m = jnp.where(keep, dy_f, 0.0).astype(bf16)
            for block in range(2):
                lo, hi = block * half, (block + 1) * half
                spread = run[lo:hi, head : head + 1] - run_t[head : head + 1, 0:hi]
                weight = jnp.exp(spread + mask_ref[lo:hi, 0:hi])
                mixing = (weight * g_ref[lo:hi, 0:hi]).astype(bf16)
                dmix = dot_t(dy_m[lo:hi], u_b[:hi])
                dg_ref[lo:hi, 0:hi] += weight * dmix
                du_add = tdot(mixing, dy_m[lo:hi])
                for part in range(block + 1):
                    du[part] = du[part] + du_add[part * half : (part + 1) * half]
        du = jnp.concatenate(du, 0)
        balance = dy_f * ysum - u_f * du
        weighted = du * xc
        for side in range(2):
            head = 2 * pair + side
            keep = lane_lo if side == 0 else ~lane_lo
            here = lanes == head
            drun = jnp.where(
                here, jnp.sum(jnp.where(keep, balance, 0.0), axis=-1, keepdims=True), drun
            )
            ddt = jnp.where(
                here, jnp.sum(jnp.where(keep, weighted, 0.0), axis=-1, keepdims=True), ddt
            )
        dact_ref[:, cols] = du * dt_pair + skip * dssm
    dg = dg_ref[...].astype(bf16)
    dact_ref[:, wx : wx + state] = tdot(dg, bc[:, state:])
    dact_ref[:, wx + state :] = dot(dg, bc[:, :state])
    linked = jnp.where(mask_ref[...] == 0.0, 1.0, 0.0).astype(bf16)
    high, mid, low = split3(drun)
    dld = tdot(linked, high) + (tdot(linked, mid) + tdot(linked, low))
    ddt = ddt + dld * nega_ref[...]
    dstep = ddt * sigmoid(raw)
    d2_ref[:, wx + wbc :] = dstep.astype(bf16)

    acc = acc_ref[...]
    sig = sigmoid(acc)
    dconv = dact_ref[...] * sig * (1.0 + acc * (1.0 - sig))
    u = u_ref[...]
    small_ref[0:1, :] = jnp.sum(dconv * u, axis=0, keepdims=True)
    small_ref[taps_count : taps_count + 1, :] = jnp.sum(dconv, axis=0, keepdims=True)
    du_in = dconv * taps_ref[0:1, :]
    for shift_by in range(1, taps_count):
        masked = dconv * link_ref[shift_by - 1, :, 0:1]
        small_ref[shift_by : shift_by + 1, :] = jnp.sum(
            masked * pltpu.roll(u, shift_by, 0), axis=0, keepdims=True
        )
        du_in = du_in + taps_ref[shift_by : shift_by + 1, :] * pltpu.roll(
            masked, length - shift_by, 0
        )
    d2_ref[:, 0 : wx + wbc] = du_in.astype(bf16)
    small_ref[taps_count + 1 : taps_count + 2, 0:LANES] = skip_row
    small_ref[taps_count + 2 : taps_count + 3, 0:LANES] = jnp.sum(dstep, axis=0, keepdims=True)
    small_ref[taps_count + 3 : taps_count + 4, 0:LANES] = jnp.sum(dld * ld, axis=0, keepdims=True)
    dn1 = dot_t(d1_ref[:, :wq], query_w_ref[...]) + dot_t(d1_ref[:, wq : wq + wkv], kv_w_ref[...])
    dn1 = dn1 + dot_t(d1_ref[:, wq + wkv :], gate_w_ref[...])
    dn1 = dn1 + dot_t(d2_ref[:, :wx], input_w_ref[...])
    dn1 = dn1 + dot_t(d2_ref[:, wx : wx + wbc], state_w_ref[...])
    dn1 = dn1 + dot(d2_ref[:, wx + wbc :], step_w_ref[...])
    dn1_ref[...] = dn1.astype(bf16)
    for k in range(tensor):
        dn1_refs[k][...] = dn1_ref[pl.ds(pl.multiple_of((t ^ k) * rows, rows), rows), :]
    gmix = jnp.sum(dn1 * n1_ref[...].astype(f32), axis=0, keepdims=True) / gain_ref[...]
    late_grads(
        widths, heads, t_ref[1] % 2, n1_ref, d1_ref, d2_ref, small_ref, gmix, gfeed_ref[...],
        keep_ref, send_ref, rows_ref,
    )


def feed_body(tensor, *refs):
    parts = refs[:tensor]
    dhidden_ref, gate_ref, up_ref, n2_ref, hidden_ref, dgu_ref = refs[tensor : tensor + 6]
    dn2_refs = refs[tensor + 6 :]
    rows = parts[0].shape[0]
    units = gate_ref.shape[1]
    for k in range(tensor):
        n2_ref[k * rows : (k + 1) * rows, :] = parts[k][...]
    n2 = n2_ref[...]
    gate_pre = dot(n2, gate_ref[...])
    up_pre = dot(n2, up_ref[...])
    gsig = sigmoid(gate_pre)
    gate_act = gate_pre * gsig
    dhidden = dhidden_ref[...]
    dgate = (dhidden * up_pre * gsig * (1.0 + gate_pre * (1.0 - gsig))).astype(bf16)
    dup = (dhidden * gate_act).astype(bf16)
    dn2 = (dot_t(dgate, gate_ref[...]) + dot_t(dup, up_ref[...])).astype(bf16)
    for k in range(tensor):
        dn2_refs[k][...] = dn2[k * rows : (k + 1) * rows]
    hidden_ref[...] = (gate_act * up_pre).astype(bf16)
    dgu_ref[:, :units] = dgate
    dgu_ref[:, units:] = dup


def split_store(upper, first, second, keep_ref, send_ref, at):
    size = first.shape[0]
    low = upper == 0
    keep_ref[at : at + size, :] = jnp.where(low, first, second).astype(bf16)
    send_ref[at : at + size, :] = jnp.where(low, second, first).astype(bf16)


def feed_grads_body(groups, u_ref, n2_ref, dgu_ref, hidden_ref, cot_ref, keep_ref, send_ref):
    upper = u_ref[1] % 2
    dgu = dgu_ref[...]
    cot = cot_ref[...]
    half_wide = n2_ref.shape[1] // 2
    half_tall = hidden_ref.shape[1] // 2
    wide, tall = half_wide // groups, half_tall // groups
    low = upper == 0
    for source, other, half, size, skip in (
        (n2_ref, dgu, half_wide, wide, 0),
        (hidden_ref, cot, half_tall, tall, wide),
    ):
        first = tdot(source[:, :half], other)
        second = tdot(source[:, half:], other)
        keep = jnp.where(low, first, second).astype(bf16)
        send = jnp.where(low, second, first).astype(bf16)
        for q in range(groups):
            at = q * (wide + tall) + skip
            keep_ref[at : at + size, :] = keep[q * size : (q + 1) * size]
            send_ref[at : at + size, :] = send[q * size : (q + 1) * size]


def late_grads(
    widths, heads, upper, n1_ref, d1_ref, d2_ref, small_ref, gmix, gfeed,
    keep_ref, send_ref, rows_ref,
):
    wq, wkv, _, wx, wbc, wst = widths
    count = small_ref.shape[0]
    width = n1_ref.shape[1]
    half = width // 2
    rows_ref[...] = jnp.zeros(rows_ref.shape, f32)
    at = heads
    rows_ref[at : at + count, 0:wx] = small_ref[:, :wx]
    at += count
    rows_ref[at : at + 1, :] = gmix
    rows_ref[at + 1 : at + 2, :] = gfeed
    at += 2
    rows_ref[at : at + count, 0:wbc] = small_ref[:, wx:]
    extra = rows_ref[...].T
    low = upper == 0
    for source, columns, where_to in (
        (d1_ref, (wq, wq + wkv), 0),
        (d2_ref, (wx, wx + wbc), wkv),
        (d2_ref, (wx + wbc, wx + wbc + wst), wkv + wbc),
        (d2_ref, (0, wx), wkv + wbc + wst),
    ):
        grads = tdot(n1_ref[...], source[:, columns[0] : columns[1]])
        if columns[0] == wx + wbc:
            grads = grads + extra
        first, second = grads[:half], grads[half:]
        span = slice(where_to, where_to + columns[1] - columns[0])
        keep_ref[:, span] = jnp.where(low, first, second).astype(bf16)
        send_ref[:, span] = jnp.where(low, second, first).astype(bf16)


def combine_body(widths, heads, counts, local_heads, t_ref, own_ref, sum_ref, other_ref, out_ref):
    _, wkv, _, _, wbc, wst = widths
    t = t_ref[0]
    group = QH // KVH
    picked = wkv + wbc + wst
    lanes = lane_ids(own_ref.shape[0], LANES)
    first = t * local_heads // group == 0
    own = own_ref[:, :picked].astype(f32)
    mine = sum_ref[...].astype(f32)
    other = other_ref[...].astype(f32)
    low = jnp.where(first, mine[:, :wkv], other[:, :wkv])
    high = jnp.where(first, other[:, :wkv], mine[:, :wkv])
    out_ref[:, :LANES] = jnp.where(lanes < HD, low, pltpu.roll(high, HD, 1)).astype(bf16)
    out_ref[:, LANES : 2 * LANES] = jnp.where(lanes < HD, pltpu.roll(low, HD, 1), high).astype(
        bf16
    )
    total = mine[:, wkv:] + other[:, wkv:]
    at = 2 * LANES
    out_ref[:, at : at + wbc] = total[:, :wbc].astype(bf16)
    at += wbc
    extra = jnp.where(lanes < heads + counts, own[:, wkv + wbc :], total[:, wbc:])
    out_ref[:, at : at + wst] = extra.astype(bf16)
    at += wst
    out_ref[:, at:] = own_ref[:, picked:]


def piece_places(d, groups):
    for side in range(2):
        half = d % 2 if side == 0 else 1 - d % 2
        for j in range(groups):
            yield side * groups + j, half, (d // 2) ^ j


def merge_rows(d, groups, pieces, full_ref):
    rows = pieces[0].shape[0]
    for at, half, group in piece_places(d, groups):
        where_to = pl.multiple_of((half * groups + group) * rows, rows)
        full_ref[pl.ds(where_to, rows), :] = pieces[at][...]


def feed_out_body(groups, d_ref, *refs):
    pieces = refs[: 2 * groups]
    gate_ref, up_ref, down_ref, gate_stage, up_stage, down_stage, sems = refs[2 * groups :]
    width, units = gate_ref.shape
    wide, tall = width // (2 * groups), units // (2 * groups)
    copies = Copies(sems)
    for at, half, group in piece_places(d_ref[1], groups):
        piece = pieces[at]
        place = half * groups + group
        rows = pl.ds(pl.multiple_of(place * wide, wide), wide)
        gate_stage[rows, :] = piece[:wide, :units].astype(f32)
        copies.start(gate_stage.at[rows, :], gate_ref.at[rows, :])
        up_stage[rows, :] = piece[:wide, units:].astype(f32)
        copies.start(up_stage.at[rows, :], up_ref.at[rows, :])
        rows = pl.ds(pl.multiple_of(place * tall, tall), tall)
        down_stage[rows, :] = piece[wide:, :].astype(f32)
        copies.start(down_stage.at[rows, :], down_ref.at[rows, :])
    copies.wait()


def mid_out_body(widths, groups, d_ref, *refs):
    wq, _, _, wx, _, _ = widths
    outs = refs[2 * groups : 2 * groups + 4]
    stages = refs[2 * groups + 4 : 2 * groups + 8]
    full_ref, sems = refs[2 * groups + 8 :]
    att_stage, mam_stage, gate_stage, query_stage = stages
    merge_rows(d_ref[1], groups, refs[: 2 * groups], full_ref)
    copies = Copies(sems)
    mam_stage[...] = full_ref[wq : wq + wx, :].astype(f32)
    copies.start(mam_stage, outs[1])
    att_stage[...] = full_ref[:wq, :].astype(f32)
    copies.start(att_stage, outs[0])
    at = wq + wx
    gate_stage[:, wx - wq :] = full_ref[at : at + wq, :].astype(f32).T
    gate_stage[:, : wx - wq] = full_ref[at + wq : at + wx, :].astype(f32).T
    copies.start(gate_stage, outs[2])
    query_stage[...] = full_ref[at + wx :, :].astype(f32).T
    copies.start(query_stage, outs[3])
    copies.wait()


def late_out_body(widths, heads, taps_count, groups, d_ref, *refs):
    _, _, _, wx, wbc, wst = widths
    big = refs[2 * groups : 2 * groups + 4]
    (
        step_ref, tap_in_ref, off_in_ref, skip_ref, bias_ref, decay_ref,
        mix_ref, feed_ref, tap_st_ref, off_st_ref,
    ) = refs[2 * groups + 4 : 2 * groups + 14]
    *stages, full_ref, rows_ref, sems = refs[2 * groups + 14 :]
    merge_rows(d_ref[1], groups, refs[: 2 * groups], full_ref)
    copies = Copies(sems)
    sizes = (KVH * HD, KVH * HD, wbc, wx)
    starts = (0, KVH * HD, 2 * KVH * HD, 2 * KVH * HD + wbc + wst)
    for out_ref, stage, size, at in zip(big, stages, sizes, starts):
        stage[...] = full_ref[:, at : at + size].astype(f32)
        copies.start(stage, out_ref)
    at = 2 * KVH * HD + wbc
    rows_ref[...] = full_ref[:, at : at + wst].astype(f32).T
    step_ref[...] = rows_ref[:heads, :]
    at = heads
    tap_in_ref[...] = rows_ref[at : at + taps_count, :wx]
    at += taps_count
    off_in_ref[...] = rows_ref[at : at + 1, :wx]
    skip_ref[...] = rows_ref[at + 1 : at + 2, :heads]
    bias_ref[...] = rows_ref[at + 2 : at + 3, :heads]
    decay_ref[...] = rows_ref[at + 3 : at + 4, :heads]
    at += taps_count
    mix_ref[...] = rows_ref[at : at + 1, :]
    feed_ref[...] = rows_ref[at + 1 : at + 2, :]
    at += 2
    tap_st_ref[...] = rows_ref[at : at + taps_count, :wbc]
    off_st_ref[...] = rows_ref[at + taps_count : at + taps_count + 1, :wbc]
    copies.wait()


def add_split_body(groups, d_ref, keep_ref, came_ref, *outs):
    group = d_ref[1] // 2
    rows = keep_ref.shape[0] // groups
    for j in range(groups):
        at = pl.ds(pl.multiple_of((group ^ j) * rows, rows), rows)
        outs[j][...] = (keep_ref[at, :].astype(f32) + came_ref[at, :].astype(f32)).astype(bf16)


def add_body(groups, picked, d_ref, *refs):
    total = refs[0][...].astype(f32)
    for j in range(1, groups):
        total = total + refs[j][...].astype(f32)
    total = total.astype(bf16)
    refs[groups][...] = total
    if picked:
        refs[groups + 1][...] = total[:, :picked]


def call_kernel(body, scalar, operands, out_shapes, scratch=(), leaves=False, far=(), far_outs=0):
    spec = pl.BlockSpec(memory_space=pltpu.VMEM)
    hbm = pl.BlockSpec(memory_space=pltpu.HBM)
    shape_of = jax.ShapeDtypeStruct if leaves else pltpu.VMEM
    placed = [
        pltpu.with_memory_space_constraint(value, pltpu.HBM if at in far else pltpu.VMEM)
        for at, value in enumerate(operands)
    ]
    return pl.pallas_call(
        body,
        in_specs=[pl.BlockSpec(memory_space=pltpu.SMEM)]
        + [hbm if at in far else spec for at in range(len(operands))],
        out_specs=[hbm if at < far_outs else spec for at in range(len(out_shapes))],
        out_shape=[shape_of(shape, kind) for shape, kind in out_shapes],
        scratch_shapes=[
            shape if kind is None else pltpu.VMEM(shape, kind) for shape, kind in scratch
        ],
        compiler_params=pltpu.CompilerParams(vmem_limit_bytes=24 * 1024 * 1024),
    )(scalar, *placed)


class Copies:
    def __init__(self, sems):
        self.sems = sems
        self.started = []

    def start(self, source, target):
        copy = pltpu.make_async_copy(source, target, self.sems.at[len(self.started)])
        copy.start()
        self.started.append(copy)

    def wait(self, first=0, last=None):
        for copy in self.started[first:last]:
            copy.wait()


def xor_pairs(size, bit):
    return [(at, at ^ bit) for at in range(size)]


def swap(value, axis, size, bit):
    return lax.ppermute(value, axis, xor_pairs(size, bit))


def lowest_bit(number):
    return number & -number


def gather_parts(value, size):
    got = {0: value}
    for k in range(size - 1, 0, -1):
        if lowest_bit(k) == k:
            got[k] = swap(value, "tensor", size, k)
    for k in range(1, size):
        low = lowest_bit(k)
        if k != low:
            got[k] = swap(got[k ^ low], "tensor", size, low)
    return [got[k] for k in range(size)]


def scatter_parts(blocks, size):
    held = list(blocks)
    for k in range(size - 1, 0, -1):
        low = lowest_bit(k)
        if k != low:
            came = swap(held[k], "tensor", size, low)
            held[k ^ low] = (held[k ^ low].astype(f32) + came.astype(f32)).astype(bf16)
    total = held[0].astype(f32)
    for k in range(size - 1, 0, -1):
        if lowest_bit(k) == k:
            total = total + swap(held[k], "tensor", size, k).astype(f32)
    return total


def sum_over_dp(keep, send, size, index, between=None, picked=0):
    groups = size // 2
    rows, width = keep.shape[0] // groups, keep.shape[1]
    came = swap(send, "dp", size, 1)
    pieces = call_kernel(
        functools.partial(add_split_body, groups),
        index,
        (keep, came),
        [((rows, width), bf16)] * groups,
    )
    came = [swap(pieces[j], "dp", size, 2 * j) for j in range(1, groups)]
    outs = [((rows, width), bf16)]
    if picked:
        outs = outs + [((rows, picked), bf16)]
    total, *rest = call_kernel(
        functools.partial(add_body, groups, picked), index, (pieces[0], *came), outs
    )
    if between is not None:
        total = between(total, *rest)
    mine = [total]
    mine = mine + [swap(total, "dp", size, 2 * j) for j in range(1, groups)]
    return mine + [swap(piece, "dp", size, 1) for piece in mine]


def block(
    inputs,
    segments,
    mixers_norm_gain,
    query_weight,
    key_weight,
    value_weight,
    attention_out,
    mamba_gate,
    mamba_input,
    state_weight,
    step_weight,
    kernel_input,
    kernel_state,
    offset_input,
    offset_state,
    step_bias,
    decay_log,
    skip_gain,
    mamba_out,
    feedforward_norm_gain,
    gate_weight,
    up_weight,
    down_weight,
    cotangent,
    *,
    dp,
    tensor,
):
    local_heads = query_weight.shape[1] // HD
    group = QH // KVH
    assert tensor == 4 and KVH * HD == LANES and 2 * local_heads == group
    rows, width = inputs.shape
    length = rows * tensor
    heads = step_weight.shape[1]
    wq = query_weight.shape[1]
    wkv = 2 * HD
    wx = mamba_input.shape[1]
    wbc = state_weight.shape[1]
    wst = LANES
    units = gate_weight.shape[1]
    kc = kernel_input.shape[0]
    widths = (wq, wkv, wx, wx, wbc, wst)
    t_index = lax.axis_index("tensor")
    t_array = jnp.where(
        lax.iota(jnp.int32, 2) == 0, t_index, lax.axis_index("dp")
    ).astype(jnp.int32)

    parts = gather_parts(inputs, tensor)
    cot_parts = gather_parts(cotangent, tensor)

    kv_index = t_index * local_heads // group
    key_slice = lax.dynamic_slice_in_dim(key_weight, kv_index * HD, HD, 1)
    value_slice = lax.dynamic_slice_in_dim(value_weight, kv_index * HD, HD, 1)
    step_pad = jnp.pad(step_weight.T, ((0, LANES - heads), (0, 0)))
    kv_weight = jnp.concatenate([key_slice, value_slice], 1)
    weights = (query_weight, kv_weight, mamba_gate, mamba_input, state_weight, step_pad)
    taps = jnp.concatenate([kernel_input, kernel_state], 1)
    offs = jnp.concatenate([offset_input, offset_state], 0)[None, :]
    bias = jnp.pad(step_bias, (0, LANES - heads))[None, :]
    nega = jnp.pad(-jnp.exp(decay_log), (0, LANES - heads))[None, :]
    skip = jnp.repeat(skip_gain, wx // heads)[None, :]
    seg_row = segments[None, :]
    gain1 = mixers_norm_gain[None, :]

    full = (length, width)
    blocks = [((rows, width), bf16)] * tensor
    square = ((length, length), f32)
    (n1, qkv, att, stat, z, u, acc, ysum, gated, raw, *held) = call_kernel(
        functools.partial(fwd_body, widths, kc, heads, tensor),
        t_array,
        (*parts, seg_row, gain1, *weights, taps, offs, bias, nega, skip, attention_out, mamba_out),
        [
            (full, bf16),
            ((length, wq + 2 * LANES), bf16),
            ((length, LANES), bf16),
            ((length, LANES), f32),
            ((length, wx), f32),
            ((length, wx + wbc), f32),
            ((length, wx + wbc), f32),
            ((length, wx), f32),
            ((length, wx), bf16),
            ((length, wst), f32),
            square,
            square,
            ((length, wst), f32),
            ((wst, length), f32),
            ((length, wst), f32),
            ((kc - 1, length, LANES), f32),
            *blocks,
        ],
        [
            (full, bf16),
            (query_weight.shape, bf16),
            (attention_out.shape, bf16),
            (mamba_out.shape, bf16),
            (pltpu.SemaphoreType.DMA((3,)), None),
        ],
        far=(tensor + 2, tensor + 13, tensor + 14),
    )
    mask, g, run, run_t, dt, link, *mixed_blocks = held

    inputs_float = inputs.astype(f32)
    reciprocal_first = rms_recip(inputs_float)
    unit_first = inputs_float * reciprocal_first
    hidden_first = inputs_float + scatter_parts(mixed_blocks, tensor)
    reciprocal_second = rms_recip(hidden_first)
    unit_second = hidden_first * reciprocal_second
    local_normed_second = (unit_second * feedforward_norm_gain[None, :]).astype(bf16)
    n2_parts = gather_parts(local_normed_second, tensor)

    cot_rows = jnp.concatenate(cot_parts, 0)
    dhidden = dot_t(cot_rows, down_weight)
    n2, hidden, dgu, *dn2_blocks = call_kernel(
        lambda scalar, *refs: feed_body(tensor, *refs),
        t_array,
        (*n2_parts, dhidden, gate_weight, up_weight),
        [(full, bf16), ((length, units), bf16), ((length, 2 * units), bf16), *blocks],
    )
    dn2 = scatter_parts(dn2_blocks, tensor)
    scaled_second = dn2 * feedforward_norm_gain[None, :]
    grad_hidden = cotangent.astype(f32) + reciprocal_second * (
        scaled_second - unit_second * jnp.mean(scaled_second * unit_second, axis=-1, keepdims=True)
    )
    feed_grad = jnp.sum(dn2 * unit_second, axis=0)
    dparts = gather_parts(grad_hidden.astype(bf16), tensor)

    span = width // 2 + units // 2
    feed_keep, feed_send = call_kernel(
        functools.partial(feed_grads_body, dp // 2),
        t_array,
        (n2, dgu, hidden, cot_rows),
        [((span, width), bf16)] * 2,
    )
    feed_sum = sum_over_dp(feed_keep, feed_send, dp, t_array)

    mid_rows = wq + wx
    d1, dssm, mid_keep, mid_send = call_kernel(
        functools.partial(attention_bwd_body, widths, heads, tensor),
        t_array,
        (
            *dparts, skip, attention_out, mamba_out, mask,
            qkv, att, stat, z, acc, ysum, gated, n1,
        ),
        [
            ((length, wq + wkv + wx), bf16),
            ((length, wx), f32),
            ((mid_rows, width), bf16),
            ((mid_rows, width), bf16),
        ],
        [(full, bf16)],
    )
    mid_sum = sum_over_dp(mid_keep, mid_send, dp, t_array)

    feed_part = dot(hidden, down_weight).astype(bf16)
    feed_blocks = [feed_part[k * rows : (k + 1) * rows] for k in range(tensor)]
    feed_total = scatter_parts(feed_blocks, tensor)
    hidden_held, feed_total = lax.optimization_barrier((hidden_first, feed_total))
    output = (hidden_held + feed_total).astype(bf16)

    wl = wkv + wbc + wst + wx
    late_keep, late_send, *dn1_blocks = call_kernel(
        functools.partial(state_bwd_body, widths, kc, heads, tensor),
        t_array,
        (
            gain1, *weights, taps, nega, skip, mask, g, run, run_t, dt, link,
            n1, u, acc, ysum, raw, d1, dssm, feed_grad[None, :],
        ),
        [((width // 2, wl), bf16), ((width // 2, wl), bf16), *blocks],
        [
            ((length, wx + wbc + wst), bf16),
            ((2 * kc, wx + wbc), f32),
            (full, bf16),
            square,
            ((length, wx + wbc), f32),
            ((LANES, width), f32),
        ],
    )
    dn1 = scatter_parts(dn1_blocks, tensor)
    scaled_first = dn1 * mixers_norm_gain[None, :]
    block_input_gradient = grad_hidden + reciprocal_first * (
        scaled_first - unit_first * jnp.mean(scaled_first * unit_first, axis=-1, keepdims=True)
    )

    picked = wkv + wbc + wst
    wide = 2 * KVH * HD + wbc + wst + wx

    def combine(own, shared):
        pair = shared + swap(shared, "tensor", tensor, 1)
        (out,) = call_kernel(
            functools.partial(combine_body, widths, heads, 2 * kc, local_heads),
            t_array,
            (own, pair, swap(pair, "tensor", tensor, 2)),
            [((own.shape[0], wide), bf16)],
        )
        return out

    late_sum = sum_over_dp(late_keep, late_send, dp, t_array, combine, picked)

    groups = dp // 2
    feed_shapes = [((width, units), f32), ((width, units), f32), ((units, width), f32)]
    grad_gate, grad_up, grad_down = call_kernel(
        functools.partial(feed_out_body, groups),
        t_array,
        feed_sum,
        feed_shapes,
        [*feed_shapes, (pltpu.SemaphoreType.DMA((6 * groups,)), None)],
        leaves=True,
        far_outs=3,
    )
    mid_shapes = [((wq, width), f32), ((wx, width), f32), ((width, wx), f32), ((width, wq), f32)]
    grad_attn_out, grad_mamba_out, grad_mgate, grad_query = call_kernel(
        functools.partial(mid_out_body, widths, groups),
        t_array,
        mid_sum,
        mid_shapes,
        [*mid_shapes, ((2 * (wq + wx), width), bf16), (pltpu.SemaphoreType.DMA((4,)), None)],
        leaves=True,
        far_outs=4,
    )
    late_shapes = [
        ((width, KVH * HD), f32),
        ((width, KVH * HD), f32),
        ((width, wbc), f32),
        ((width, wx), f32),
    ]
    (
        grad_key,
        grad_value,
        grad_state,
        grad_minput,
        grad_step,
        grad_kinput,
        grad_oinput,
        grad_skip,
        grad_sbias,
        grad_dlog,
        mixers_grad,
        feedforward_grad,
        grad_kstate,
        grad_ostate,
    ) = call_kernel(
        functools.partial(late_out_body, widths, heads, kc, groups),
        t_array,
        late_sum,
        [
            *late_shapes,
            ((heads, width), f32),
            ((kc, wx), f32),
            ((1, wx), f32),
            ((1, heads), f32),
            ((1, heads), f32),
            ((1, heads), f32),
            ((1, width), f32),
            ((1, width), f32),
            ((kc, wbc), f32),
            ((1, wbc), f32),
        ],
        [
            *late_shapes,
            ((width, wide), bf16),
            ((LANES, width), f32),
            (pltpu.SemaphoreType.DMA((4,)), None),
        ],
        leaves=True,
        far_outs=4,
    )
    grad_step = grad_step.T
    grad_oinput, grad_skip, grad_sbias, grad_dlog, mixers_grad, feedforward_grad, grad_ostate = (
        value[0]
        for value in (
            grad_oinput, grad_skip, grad_sbias, grad_dlog, mixers_grad, feedforward_grad, grad_ostate
        )
    )
    return (
        output,
        block_input_gradient,
        mixers_grad,
        grad_query,
        grad_key,
        grad_value,
        grad_attn_out,
        grad_mgate,
        grad_minput,
        grad_state,
        grad_step,
        grad_kinput,
        grad_kstate,
        grad_oinput,
        grad_ostate,
        grad_sbias,
        grad_dlog,
        grad_skip,
        grad_mamba_out,
        feedforward_grad,
        grad_gate,
        grad_up,
        grad_down,
    )


def solution(mesh):
    in_specs = (
        P(("dp", "tensor"), None),
        P("dp"),
        P(),
        P(None, "tensor"),
        P(),
        P(),
        P("tensor", None),
        P(None, "tensor"),
        P(None, "tensor"),
        P(),
        P(None, "tensor"),
        P(None, "tensor"),
        P(),
        P("tensor"),
        P(),
        P("tensor"),
        P("tensor"),
        P("tensor"),
        P("tensor", None),
        P(),
        P(None, "tensor"),
        P(None, "tensor"),
        P("tensor", None),
        P(("dp", "tensor"), None),
    )
    out_specs = (
        P(("dp", "tensor"), None),
        P(("dp", "tensor"), None),
        P(),
        P(None, "tensor"),
        P(),
        P(),
        P("tensor", None),
        P(None, "tensor"),
        P(None, "tensor"),
        P(),
        P(None, "tensor"),
        P(None, "tensor"),
        P(),
        P("tensor"),
        P(),
        P("tensor"),
        P("tensor"),
        P("tensor"),
        P("tensor", None),
        P(),
        P(None, "tensor"),
        P(None, "tensor"),
        P("tensor", None),
    )
    body = functools.partial(block, dp=mesh.shape["dp"], tensor=mesh.shape["tensor"])
    return jax.shard_map(body, mesh=mesh, in_specs=in_specs, out_specs=out_specs, check_vma=False)
```

```python
import functools

import jax
import jax.numpy as jnp
from jax import lax
from jax.experimental import pallas as pl
from jax.experimental.pallas import tpu as pltpu
from jax.sharding import PartitionSpec as P


QH = 8
KVH = 2
HD = 64
LANES = 128

eps = 1e-05
big_negative = -1e30
f32 = jnp.float32
bf16 = jnp.bfloat16

DP = "dp"
TP = "tensor"


def dot(left, right):
    return jnp.dot(left, right, preferred_element_type=f32)


def tdot(left, right):
    return lax.dot_general(left, right, (((0,), (0,)), ((), ())), preferred_element_type=f32)


def dot_t(left, right):
    return lax.dot_general(left, right, (((1,), (1,)), ((), ())), preferred_element_type=f32)


def split3(value):
    high = value.astype(bf16)
    rest = value - high.astype(f32)
    mid = rest.astype(bf16)
    return high, mid, (rest - mid.astype(f32)).astype(bf16)


def exact_left(mask, value):
    high, mid, low = split3(value)
    return dot(mask, high) + (dot(mask, mid) + dot(mask, low))


def rms_recip(values):
    return lax.rsqrt(jnp.mean(values * values, axis=-1, keepdims=True) + eps)


def sigmoid(value):
    return 1.0 / (1.0 + jnp.exp(-value))


def lane_ids(rows, width):
    return lax.broadcasted_iota(jnp.int32, (rows, width), 1)


def pair_columns(values, pair, lanes):
    first = values[:, 2 * pair : 2 * pair + 1]
    second = values[:, 2 * pair + 1 : 2 * pair + 2]
    return jnp.where(lanes < HD, first, second)


def fwd_body(widths, taps_count, heads, tensor, *refs):
    (t_ref,) = refs[:1]
    parts = refs[1 : 1 + tensor]
    (
        seg_ref,
        gain_ref,
        query_w_ref,
        kv_w_ref,
        gate_w_ref,
        input_w_ref,
        state_w_ref,
        step_w_ref,
        taps_ref,
        offs_ref,
        bias_ref,
        nega_ref,
        skip_ref,
        att_w_ref,
        mam_w_ref,
        n1_ref,
        qkv_ref,
        att_ref,
        stat_ref,
        z_ref,
        u_ref,
        acc_ref,
        ysum_ref,
        gated_ref,
        raw_ref,
        mask_ref,
        g_ref,
        run_ref,
        run_t_ref,
        dt_ref,
        link_ref,
        *mixed_refs,
        mixed_ref,
        query_v,
        att_v,
        mam_v,
        sems,
    ) = refs[1 + tensor :]
    wq, _, _, wx, wbc, _ = widths
    copies = Copies(sems)
    for source, target in (
        (query_w_ref, query_v),
        (att_w_ref, att_v),
        (mam_w_ref, mam_v),
    ):
        copies.start(source, target)
    t = t_ref[0]
    rows = parts[0].shape[0]
    length = rows * tensor
    state = wbc // 2
    for k in range(tensor):
        xf = parts[k][...].astype(f32)
        normed = (xf * rms_recip(xf) * gain_ref[...]).astype(bf16)
        n1_ref[pl.ds(pl.multiple_of((t ^ k) * rows, rows), rows), :] = normed
    n1 = n1_ref[...]
    seg_row = seg_ref[0:1, :].astype(f32)
    seg_col = jnp.broadcast_to(seg_row, (LANES, length)).T
    row_pos = lax.broadcasted_iota(jnp.int32, (length, length), 0)
    col_pos = lax.broadcasted_iota(jnp.int32, (length, length), 1)
    allowed = (row_pos >= col_pos) & (seg_col[:, 0:1] == seg_row)
    mask_ref[...] = jnp.where(allowed, 0.0, big_negative)
    copies.wait(0, 1)
    query = dot(n1, query_v[...]).astype(bf16)
    kv = dot(n1, kv_w_ref[...])
    lanes = lane_ids(length, LANES)
    kv_swap = pltpu.roll(kv, HD, 1)
    keys2 = jnp.where(lanes < HD, kv, kv_swap).astype(bf16)
    values2 = jnp.where(lanes < HD, kv_swap, kv).astype(bf16)
    qkv_ref[:, 0:wq] = query
    qkv_ref[:, wq : wq + LANES] = keys2
    qkv_ref[:, wq + LANES :] = values2
    z_ref[...] = dot(n1, gate_w_ref[...])
    u_ref[:, :wx] = dot(n1, input_w_ref[...])
    u_ref[:, wx:] = dot(n1, state_w_ref[...])
    raw = dot_t(n1, step_w_ref[...]) + bias_ref[...]
    raw_ref[...] = raw

    lane_lo = lanes < HD
    scale = HD ** (-0.5)
    half = length // 2
    for block in range(2):
        lo, hi = block * half, (block + 1) * half
        out = jnp.zeros((half, LANES), f32)
        stats = []
        for head in range(2):
            keep = lane_lo[:half] if head == 0 else ~lane_lo[:half]
            keep_v = lane_lo[:hi] if head == 0 else ~lane_lo[:hi]
            q_rows = jnp.where(keep, query[lo:hi].astype(f32), 0.0).astype(bf16)
            scores = dot_t(q_rows, keys2[:hi]) * scale + mask_ref[lo:hi, 0:hi]
            top = jnp.max(scores, axis=-1, keepdims=True)
            expo = jnp.exp(scores - top)
            total = jnp.sum(expo, axis=-1, keepdims=True)
            probs = (expo / total).astype(bf16)
            v_rows = jnp.where(keep_v, values2[:hi].astype(f32), 0.0).astype(bf16)
            out = out + dot(probs, v_rows)
            stats.append(top + jnp.log(total))
        att_ref[lo:hi, :] = out.astype(bf16)
        stat_ref[lo:hi, :] = jnp.where(lane_lo[:half], stats[0], stats[1])

    u = u_ref[...]
    acc = offs_ref[...] + taps_ref[0:1, :] * u
    spots = lax.broadcasted_iota(jnp.int32, (length, LANES), 0)
    for shift_by in range(1, taps_count):
        linked = (pltpu.roll(seg_col, shift_by, 0) == seg_col) & (spots >= shift_by)
        linked = jnp.where(linked, 1.0, 0.0)
        link_ref[shift_by - 1] = linked
        acc = acc + taps_ref[shift_by : shift_by + 1, :] * (
            linked[:, 0:1] * pltpu.roll(u, shift_by, 0)
        )
    acc_ref[...] = acc

    dt = jnp.maximum(raw, 0.0) + jnp.log1p(jnp.exp(-jnp.abs(raw)))
    tri = (row_pos >= col_pos).astype(f32).astype(bf16)
    run = exact_left(tri, dt * nega_ref[...])
    run_t = run.T
    dt_ref[...] = dt
    run_ref[...] = run
    run_t_ref[...] = run_t
    bc = acc_ref[:, wx:]
    bc = (bc * sigmoid(bc)).astype(bf16)
    g_ref[...] = dot_t(bc[:, state:], bc[:, :state])
    for pair in range(heads // 2):
        cols = slice(pair * LANES, (pair + 1) * LANES)
        xa = acc_ref[:, cols]
        xc = xa * sigmoid(xa)
        uu = xc * pair_columns(dt, pair, lanes)
        u_lo = jnp.where(lane_lo, uu, 0.0).astype(bf16)
        u_hi = jnp.where(lane_lo, 0.0, uu).astype(bf16)
        for block in range(2):
            lo, hi = block * half, (block + 1) * half
            total = jnp.zeros((half, LANES), f32)
            for side, masked in ((0, u_lo), (1, u_hi)):
                head = 2 * pair + side
                spread = run[lo:hi, head : head + 1] - run_t[head : head + 1, 0:hi]
                weight = jnp.exp(spread + mask_ref[lo:hi, 0:hi])
                mixing = (weight * g_ref[lo:hi, 0:hi]).astype(bf16)
                total = total + dot(mixing, masked[:hi])
            ysum_ref[lo:hi, cols] = total
        y = ysum_ref[:, cols] + skip_ref[0:1, cols] * xc
        z = z_ref[:, cols]
        gated_ref[:, cols] = (y * z * sigmoid(z)).astype(bf16)
    copies.wait(1)
    mixed = dot(att_ref[...], att_v[...]) + dot(gated_ref[...], mam_v[...])
    mixed_ref[...] = mixed.astype(bf16)
    for k in range(tensor):
        mixed_refs[k][...] = mixed_ref[pl.ds(pl.multiple_of((t ^ k) * rows, rows), rows), :]


def attention_bwd_body(widths, heads, tensor, *refs):
    t_ref = refs[0]
    dparts = refs[1 : 1 + tensor]
    (
        skip_ref,
        att_w_ref,
        mam_w_ref,
        mask_ref,
        qkv_ref,
        att_ref,
        stat_ref,
        z_ref,
        acc_ref,
        ysum_ref,
        gated_ref,
        n1_ref,
        d_ref,
        dssm_ref,
        keep_ref,
        send_ref,
        dmixed_ref,
    ) = refs[1 + tensor :]
    wq, wkv, _, wx, _, _ = widths
    t = t_ref[0]
    rows = dparts[0].shape[0]
    length = rows * tensor
    for k in range(tensor):
        dmixed_ref[pl.ds(pl.multiple_of((t ^ k) * rows, rows), rows), :] = dparts[k][...]
    dmixed = dmixed_ref[...]
    lane_lo = lane_ids(length, LANES) < HD
    half = length // 2
    scale = HD ** (-0.5)

    datt = dot_t(dmixed, att_w_ref[...]).astype(bf16)
    datt_f = datt.astype(f32)
    prod = datt_f * att_ref[...].astype(f32)
    query = qkv_ref[:, 0:wq]
    keys2 = qkv_ref[:, wq : wq + LANES]
    values2 = qkv_ref[:, wq + LANES :]
    stat = stat_ref[...]
    dq = [jnp.zeros((half, LANES), f32) for _ in range(2)]
    dk = [jnp.zeros((half, LANES), f32) for _ in range(2)]
    dv = [jnp.zeros((half, LANES), f32) for _ in range(2)]
    for head in range(2):
        keep = lane_lo if head == 0 else ~lane_lo
        q_m = jnp.where(keep, query.astype(f32), 0.0).astype(bf16)
        k_m = jnp.where(keep, keys2.astype(f32), 0.0).astype(bf16)
        d_m = jnp.where(keep, datt_f, 0.0).astype(bf16)
        delta = jnp.sum(jnp.where(keep, prod, 0.0), axis=-1, keepdims=True)
        logsum = stat[:, head * HD : head * HD + 1]
        for block in range(2):
            lo, hi = block * half, (block + 1) * half
            scores = dot_t(q_m[lo:hi], keys2[:hi]) * scale + mask_ref[lo:hi, 0:hi]
            probs = jnp.exp(scores - logsum[lo:hi])
            dprob = dot_t(d_m[lo:hi], values2[:hi])
            dscore = (probs * (dprob - delta[lo:hi]) * scale).astype(bf16)
            dq[block] = dq[block] + dot(dscore, k_m[:hi])
            dk_add = tdot(dscore, q_m[lo:hi])
            dv_add = tdot(probs.astype(bf16), d_m[lo:hi])
            for part in range(block + 1):
                dk[part] = dk[part] + dk_add[part * half : (part + 1) * half]
                dv[part] = dv[part] + dv_add[part * half : (part + 1) * half]
    for block in range(2):
        lo, hi = block * half, (block + 1) * half
        d_ref[lo:hi, 0:wq] = dq[block].astype(bf16)
        dk_sum = dk[block] + pltpu.roll(dk[block], HD, 1)
        dv_sum = dv[block] + pltpu.roll(dv[block], HD, 1)
        d_ref[lo:hi, wq : wq + wkv] = jnp.where(lane_lo[:half], dk_sum, dv_sum).astype(bf16)

    base = wq + wkv
    for pair in range(heads // 2):
        cols = slice(pair * LANES, (pair + 1) * LANES)
        xa = acc_ref[:, cols]
        xc = xa * sigmoid(xa)
        z = z_ref[:, cols]
        zs = sigmoid(z)
        dgated = dot_t(dmixed, mam_w_ref[cols, :])
        dssm_ref[:, cols] = dgated * z * zs
        y = ysum_ref[:, cols] + skip_ref[0:1, cols] * xc
        dz = dgated * y * zs * (1.0 + z * (1.0 - zs))
        d_ref[:, base + pair * LANES : base + (pair + 1) * LANES] = dz.astype(bf16)
    upper = t_ref[1] % 2
    n1 = n1_ref[...]
    gz = tdot(d_ref[:, base:], n1)
    split_store(upper, tdot(att_ref[...], dmixed), gz[wx - wq :], keep_ref, send_ref, 0)
    second = jnp.concatenate([gz[: wx - wq], tdot(d_ref[:, :wq], n1)], 0)
    split_store(upper, tdot(gated_ref[...], dmixed), second, keep_ref, send_ref, wq)


def state_bwd_body(widths, taps_count, heads, tensor, *refs):
    (
        t_ref,
        gain_ref,
        query_w_ref,
        kv_w_ref,
        gate_w_ref,
        input_w_ref,
        state_w_ref,
        step_w_ref,
        taps_ref,
        nega_ref,
        skip_ref,
        mask_ref,
        g_ref,
        run_ref,
        run_t_ref,
        dt_ref,
        link_ref,
        n1_ref,
        u_ref,
        acc_ref,
        ysum_ref,
        raw_ref,
        d1_ref,
        dssm_ref,
        gfeed_ref,
    ) = refs[:25]
    (
        keep_ref,
        send_ref,
        *dn1_refs,
        d2_ref,
        small_ref,
        dn1_ref,
        dg_ref,
        dact_ref,
        rows_ref,
    ) = refs[25:]
    wq, wkv, _, wx, wbc, _ = widths
    t = t_ref[0]
    length = n1_ref.shape[0]
    rows = length // tensor
    state = wbc // 2
    lanes = lane_ids(length, LANES)
    lane_lo = lanes < HD
    half = length // 2

    raw = raw_ref[...]
    dt = dt_ref[...]
    ld = dt * nega_ref[...]
    run = run_ref[...]
    run_t = run_t_ref[...]
    bc_acc = acc_ref[:, wx:]
    bc = (bc_acc * sigmoid(bc_acc)).astype(bf16)
    dg_ref[...] = jnp.zeros((length, length), f32)
    drun = jnp.zeros((length, LANES), f32)
    ddt = jnp.zeros((length, LANES), f32)
    skip_row = jnp.zeros((1, LANES), f32)
    small_ref[...] = jnp.zeros(small_ref.shape, f32)
    for pair in range(heads // 2):
        cols = slice(pair * LANES, (pair + 1) * LANES)
        xa = acc_ref[:, cols]
        xc = xa * sigmoid(xa)
        skip = skip_ref[0:1, cols]
        ysum = ysum_ref[:, cols]
        dssm = dssm_ref[:, cols]
        dskip = jnp.sum(dssm * xc, axis=0, keepdims=True)
        for side in range(2):
            keep = lane_lo[0:1] if side == 0 else ~lane_lo[0:1]
            head_sum = jnp.sum(jnp.where(keep, dskip, 0.0), axis=-1, keepdims=True)
            skip_row = jnp.where(lanes[0:1] == 2 * pair + side, head_sum, skip_row)
        dt_pair = pair_columns(dt, pair, lanes)
        u_b = (xc * dt_pair).astype(bf16)
        dy_b = dssm.astype(bf16)
        u_f = u_b.astype(f32)
        dy_f = dy_b.astype(f32)
        du = [jnp.zeros((half, LANES), f32) for _ in range(2)]
        for side in range(2):
            head = 2 * pair + side
            keep = lane_lo if side == 0 else ~lane_lo
            dy_m = jnp.where(keep, dy_f, 0.0).astype(bf16)
            for block in range(2):
                lo, hi = block * half, (block + 1) * half
                spread = run[lo:hi, head : head + 1] - run_t[head : head + 1, 0:hi]
                weight = jnp.exp(spread + mask_ref[lo:hi, 0:hi])
                mixing = (weight * g_ref[lo:hi, 0:hi]).astype(bf16)
                dmix = dot_t(dy_m[lo:hi], u_b[:hi])
                dg_ref[lo:hi, 0:hi] += weight * dmix
                du_add = tdot(mixing, dy_m[lo:hi])
                for part in range(block + 1):
                    du[part] = du[part] + du_add[part * half : (part + 1) * half]
        du = jnp.concatenate(du, 0)
        balance = dy_f * ysum - u_f * du
        weighted = du * xc
        for side in range(2):
            head = 2 * pair + side
            keep = lane_lo if side == 0 else ~lane_lo
            here = lanes == head
            drun = jnp.where(
                here, jnp.sum(jnp.where(keep, balance, 0.0), axis=-1, keepdims=True), drun
            )
            ddt = jnp.where(
                here, jnp.sum(jnp.where(keep, weighted, 0.0), axis=-1, keepdims=True), ddt
            )
        dact_ref[:, cols] = du * dt_pair + skip * dssm
    dg = dg_ref[...].astype(bf16)
    dact_ref[:, wx : wx + state] = tdot(dg, bc[:, state:])
    dact_ref[:, wx + state :] = dot(dg, bc[:, :state])
    linked = jnp.where(mask_ref[...] == 0.0, 1.0, 0.0).astype(bf16)
    high, mid, low = split3(drun)
    dld = tdot(linked, high) + (tdot(linked, mid) + tdot(linked, low))
    ddt = ddt + dld * nega_ref[...]
    dstep = ddt * sigmoid(raw)
    d2_ref[:, wx + wbc :] = dstep.astype(bf16)

    acc = acc_ref[...]
    sig = sigmoid(acc)
    dconv = dact_ref[...] * sig * (1.0 + acc * (1.0 - sig))
    u = u_ref[...]
    small_ref[0:1, :] = jnp.sum(dconv * u, axis=0, keepdims=True)
    small_ref[taps_count : taps_count + 1, :] = jnp.sum(dconv, axis=0, keepdims=True)
    du_in = dconv * taps_ref[0:1, :]
    for shift_by in range(1, taps_count):
        masked = dconv * link_ref[shift_by - 1, :, 0:1]
        small_ref[shift_by : shift_by + 1, :] = jnp.sum(
            masked * pltpu.roll(u, shift_by, 0), axis=0, keepdims=True
        )
        du_in = du_in + taps_ref[shift_by : shift_by + 1, :] * pltpu.roll(
            masked, length - shift_by, 0
        )
    d2_ref[:, 0 : wx + wbc] = du_in.astype(bf16)
    small_ref[taps_count + 1 : taps_count + 2, 0:LANES] = skip_row
    small_ref[taps_count + 2 : taps_count + 3, 0:LANES] = jnp.sum(dstep, axis=0, keepdims=True)
    small_ref[taps_count + 3 : taps_count + 4, 0:LANES] = jnp.sum(dld * ld, axis=0, keepdims=True)
    dn1 = dot_t(d1_ref[:, :wq], query_w_ref[...]) + dot_t(d1_ref[:, wq : wq + wkv], kv_w_ref[...])
    dn1 = dn1 + dot_t(d1_ref[:, wq + wkv :], gate_w_ref[...])
    dn1 = dn1 + dot_t(d2_ref[:, :wx], input_w_ref[...])
    dn1 = dn1 + dot_t(d2_ref[:, wx : wx + wbc], state_w_ref[...])
    dn1 = dn1 + dot(d2_ref[:, wx + wbc :], step_w_ref[...])
    dn1_ref[...] = dn1.astype(bf16)
    for k in range(tensor):
        dn1_refs[k][...] = dn1_ref[pl.ds(pl.multiple_of((t ^ k) * rows, rows), rows), :]
    gmix = jnp.sum(dn1 * n1_ref[...].astype(f32), axis=0, keepdims=True) / gain_ref[...]
    late_grads(
        widths, heads, t_ref[1] % 2, n1_ref, d1_ref, d2_ref, small_ref, gmix, gfeed_ref[...],
        keep_ref, send_ref, rows_ref,
    )


def feed_body(tensor, *refs):
    parts = refs[:tensor]
    dhidden_ref, gate_ref, up_ref, n2_ref, hidden_ref, dgu_ref = refs[tensor : tensor + 6]
    dn2_refs = refs[tensor + 6 :]
    rows = parts[0].shape[0]
    units = gate_ref.shape[1]
    for k in range(tensor):
        n2_ref[k * rows : (k + 1) * rows, :] = parts[k][...]
    n2 = n2_ref[...]
    gate_pre = dot(n2, gate_ref[...])
    up_pre = dot(n2, up_ref[...])
    gsig = sigmoid(gate_pre)
    gate_act = gate_pre * gsig
    dhidden = dhidden_ref[...]
    dgate = (dhidden * up_pre * gsig * (1.0 + gate_pre * (1.0 - gsig))).astype(bf16)
    dup = (dhidden * gate_act).astype(bf16)
    dn2 = (dot_t(dgate, gate_ref[...]) + dot_t(dup, up_ref[...])).astype(bf16)
    for k in range(tensor):
        dn2_refs[k][...] = dn2[k * rows : (k + 1) * rows]
    hidden_ref[...] = (gate_act * up_pre).astype(bf16)
    dgu_ref[:, :units] = dgate
    dgu_ref[:, units:] = dup


def split_store(upper, first, second, keep_ref, send_ref, at):
    size = first.shape[0]
    low = upper == 0
    keep_ref[at : at + size, :] = jnp.where(low, first, second).astype(bf16)
    send_ref[at : at + size, :] = jnp.where(low, second, first).astype(bf16)


def feed_grads_body(groups, u_ref, n2_ref, dgu_ref, hidden_ref, cot_ref, keep_ref, send_ref):
    upper = u_ref[1] % 2
    dgu = dgu_ref[...]
    cot = cot_ref[...]
    half_wide = n2_ref.shape[1] // 2
    half_tall = hidden_ref.shape[1] // 2
    wide, tall = half_wide // groups, half_tall // groups
    low = upper == 0
    for source, other, half, size, skip in (
        (n2_ref, dgu, half_wide, wide, 0),
        (hidden_ref, cot, half_tall, tall, wide),
    ):
        first = tdot(source[:, :half], other)
        second = tdot(source[:, half:], other)
        keep = jnp.where(low, first, second).astype(bf16)
        send = jnp.where(low, second, first).astype(bf16)
        for q in range(groups):
            at = q * (wide + tall) + skip
            keep_ref[at : at + size, :] = keep[q * size : (q + 1) * size]
            send_ref[at : at + size, :] = send[q * size : (q + 1) * size]


def late_grads(
    widths, heads, upper, n1_ref, d1_ref, d2_ref, small_ref, gmix, gfeed,
    keep_ref, send_ref, rows_ref,
):
    wq, wkv, _, wx, wbc, wst = widths
    count = small_ref.shape[0]
    width = n1_ref.shape[1]
    half = width // 2
    rows_ref[...] = jnp.zeros(rows_ref.shape, f32)
    at = heads
    rows_ref[at : at + count, 0:wx] = small_ref[:, :wx]
    at += count
    rows_ref[at : at + 1, :] = gmix
    rows_ref[at + 1 : at + 2, :] = gfeed
    at += 2
    rows_ref[at : at + count, 0:wbc] = small_ref[:, wx:]
    extra = rows_ref[...].T
    low = upper == 0
    for source, columns, where_to in (
        (d1_ref, (wq, wq + wkv), 0),
        (d2_ref, (wx, wx + wbc), wkv),
        (d2_ref, (wx + wbc, wx + wbc + wst), wkv + wbc),
        (d2_ref, (0, wx), wkv + wbc + wst),
    ):
        grads = tdot(n1_ref[...], source[:, columns[0] : columns[1]])
        if columns[0] == wx + wbc:
            grads = grads + extra
        first, second = grads[:half], grads[half:]
        span = slice(where_to, where_to + columns[1] - columns[0])
        keep_ref[:, span] = jnp.where(low, first, second).astype(bf16)
        send_ref[:, span] = jnp.where(low, second, first).astype(bf16)


def combine_body(widths, heads, counts, local_heads, t_ref, own_ref, sum_ref, other_ref, out_ref):
    _, wkv, _, _, wbc, wst = widths
    t = t_ref[0]
    group = QH // KVH
    picked = wkv + wbc + wst
    lanes = lane_ids(own_ref.shape[0], LANES)
    first = t * local_heads // group == 0
    own = own_ref[:, :picked].astype(f32)
    mine = sum_ref[...].astype(f32)
    other = other_ref[...].astype(f32)
    low = jnp.where(first, mine[:, :wkv], other[:, :wkv])
    high = jnp.where(first, other[:, :wkv], mine[:, :wkv])
    out_ref[:, :LANES] = jnp.where(lanes < HD, low, pltpu.roll(high, HD, 1)).astype(bf16)
    out_ref[:, LANES : 2 * LANES] = jnp.where(lanes < HD, pltpu.roll(low, HD, 1), high).astype(
        bf16
    )
    total = mine[:, wkv:] + other[:, wkv:]
    at = 2 * LANES
    out_ref[:, at : at + wbc] = total[:, :wbc].astype(bf16)
    at += wbc
    extra = jnp.where(lanes < heads + counts, own[:, wkv + wbc :], total[:, wbc:])
    out_ref[:, at : at + wst] = extra.astype(bf16)
    at += wst
    out_ref[:, at:] = own_ref[:, picked:]


def input_grad_body(t_ref, *refs):
    *hops, inputs_ref, dhidden_ref, gain_ref, out_ref = refs
    xf = inputs_ref[...].astype(f32)
    recip = rms_recip(xf)
    unit = xf * recip
    scaled = sum_of([hop[...] for hop in hops]) * gain_ref[...]
    mean = jnp.mean(scaled * unit, axis=-1, keepdims=True)
    out_ref[...] = dhidden_ref[...] + recip * (scaled - unit * mean)


def piece_places(d, groups):
    for side in range(2):
        half = d % 2 if side == 0 else 1 - d % 2
        for j in range(groups):
            yield side * groups + j, half, (d // 2) ^ j


def merge_rows(d, groups, pieces, full_ref):
    rows = pieces[0].shape[0]
    for at, half, group in piece_places(d, groups):
        where_to = pl.multiple_of((half * groups + group) * rows, rows)
        full_ref[pl.ds(where_to, rows), :] = pieces[at][...]


def feed_out_body(groups, d_ref, *refs):
    pieces = refs[: 2 * groups]
    gate_ref, up_ref, down_ref, gate_stage, up_stage, down_stage, sems = refs[2 * groups :]
    width, units = gate_ref.shape
    wide, tall = width // (2 * groups), units // (2 * groups)
    copies = Copies(sems)
    for at, half, group in piece_places(d_ref[1], groups):
        piece = pieces[at]
        place = half * groups + group
        rows = pl.ds(pl.multiple_of(place * wide, wide), wide)
        gate_stage[rows, :] = piece[:wide, :units].astype(f32)
        copies.start(gate_stage.at[rows, :], gate_ref.at[rows, :])
        up_stage[rows, :] = piece[:wide, units:].astype(f32)
        copies.start(up_stage.at[rows, :], up_ref.at[rows, :])
        rows = pl.ds(pl.multiple_of(place * tall, tall), tall)
        down_stage[rows, :] = piece[wide:, :].astype(f32)
        copies.start(down_stage.at[rows, :], down_ref.at[rows, :])
    copies.wait()


def mid_out_body(widths, groups, d_ref, *refs):
    wq, _, _, wx, _, _ = widths
    outs = refs[2 * groups : 2 * groups + 4]
    stages = refs[2 * groups + 4 : 2 * groups + 8]
    full_ref, sems = refs[2 * groups + 8 :]
    att_stage, mam_stage, gate_stage, query_stage = stages
    merge_rows(d_ref[1], groups, refs[: 2 * groups], full_ref)
    copies = Copies(sems)
    mam_stage[...] = full_ref[wq : wq + wx, :].astype(f32)
    copies.start(mam_stage, outs[1])
    att_stage[...] = full_ref[:wq, :].astype(f32)
    copies.start(att_stage, outs[0])
    at = wq + wx
    gate_stage[:, wx - wq :] = full_ref[at : at + wq, :].astype(f32).T
    gate_stage[:, : wx - wq] = full_ref[at + wq : at + wx, :].astype(f32).T
    copies.start(gate_stage, outs[2])
    query_stage[...] = full_ref[at + wx :, :].astype(f32).T
    copies.start(query_stage, outs[3])
    copies.wait()


def late_out_body(widths, heads, taps_count, groups, d_ref, *refs):
    _, _, _, wx, wbc, wst = widths
    big = refs[2 * groups : 2 * groups + 4]
    (
        step_ref, tap_in_ref, off_in_ref, skip_ref, bias_ref, decay_ref,
        mix_ref, feed_ref, tap_st_ref, off_st_ref,
    ) = refs[2 * groups + 4 : 2 * groups + 14]
    *stages, full_ref, rows_ref, sems = refs[2 * groups + 14 :]
    merge_rows(d_ref[1], groups, refs[: 2 * groups], full_ref)
    copies = Copies(sems)
    sizes = (KVH * HD, KVH * HD, wbc, wx)
    starts = (0, KVH * HD, 2 * KVH * HD, 2 * KVH * HD + wbc + wst)
    for out_ref, stage, size, at in zip(big, stages, sizes, starts):
        stage[...] = full_ref[:, at : at + size].astype(f32)
        copies.start(stage, out_ref)
    at = 2 * KVH * HD + wbc
    rows_ref[...] = full_ref[:, at : at + wst].astype(f32).T
    step_ref[...] = rows_ref[:heads, :]
    at = heads
    tap_in_ref[...] = rows_ref[at : at + taps_count, :wx]
    at += taps_count
    off_in_ref[...] = rows_ref[at : at + 1, :wx]
    skip_ref[...] = rows_ref[at + 1 : at + 2, :heads]
    bias_ref[...] = rows_ref[at + 2 : at + 3, :heads]
    decay_ref[...] = rows_ref[at + 3 : at + 4, :heads]
    at += taps_count
    mix_ref[...] = rows_ref[at : at + 1, :]
    feed_ref[...] = rows_ref[at + 1 : at + 2, :]
    at += 2
    tap_st_ref[...] = rows_ref[at : at + taps_count, :wbc]
    off_st_ref[...] = rows_ref[at + taps_count : at + taps_count + 1, :wbc]
    copies.wait()


def add_split_body(groups, d_ref, keep_ref, came_ref, *outs):
    group = d_ref[1] // 2
    rows = keep_ref.shape[0] // groups
    for j in range(groups):
        at = pl.ds(pl.multiple_of((group ^ j) * rows, rows), rows)
        outs[j][...] = (keep_ref[at, :].astype(f32) + came_ref[at, :].astype(f32)).astype(bf16)


def add_body(groups, picked, d_ref, *refs):
    total = refs[0][...].astype(f32)
    for j in range(1, groups):
        total = total + refs[j][...].astype(f32)
    total = total.astype(bf16)
    refs[groups][...] = total
    if picked:
        refs[groups + 1][...] = total[:, :picked]


def call_kernel(body, scalar, operands, out_shapes, scratch=(), leaves=False, far=(), far_outs=0):
    spec = pl.BlockSpec(memory_space=pltpu.VMEM)
    hbm = pl.BlockSpec(memory_space=pltpu.HBM)
    shape_of = jax.ShapeDtypeStruct if leaves else pltpu.VMEM
    placed = [
        pltpu.with_memory_space_constraint(value, pltpu.HBM if at in far else pltpu.VMEM)
        for at, value in enumerate(operands)
    ]
    return pl.pallas_call(
        body,
        in_specs=[pl.BlockSpec(memory_space=pltpu.SMEM)]
        + [hbm if at in far else spec for at in range(len(operands))],
        out_specs=[hbm if at < far_outs else spec for at in range(len(out_shapes))],
        out_shape=[shape_of(shape, kind) for shape, kind in out_shapes],
        scratch_shapes=[
            shape if kind is None else pltpu.VMEM(shape, kind) for shape, kind in scratch
        ],
        compiler_params=pltpu.CompilerParams(vmem_limit_bytes=24 * 1024 * 1024),
    )(scalar, *placed)


class Copies:
    def __init__(self, sems):
        self.sems = sems
        self.started = []

    def start(self, source, target):
        copy = pltpu.make_async_copy(source, target, self.sems.at[len(self.started)])
        copy.start()
        self.started.append(copy)

    def wait(self, first=0, last=None):
        for copy in self.started[first:last]:
            copy.wait()


def xor_pairs(size, bit):
    return [(at, at ^ bit) for at in range(size)]


def swap(value, axis, size, bit):
    return lax.ppermute(value, axis, xor_pairs(size, bit))


def lowest_bit(number):
    return number & -number


def gather_parts(value, size):
    got = {0: value}
    for k in range(size - 1, 0, -1):
        if lowest_bit(k) == k:
            got[k] = swap(value, TP, size, k)
    for k in range(1, size):
        low = lowest_bit(k)
        if k != low:
            got[k] = swap(got[k ^ low], TP, size, low)
    return [got[k] for k in range(size)]


def scatter_parts(blocks, size, total=True):
    held = list(blocks)
    for k in range(size - 1, 0, -1):
        low = lowest_bit(k)
        if k != low:
            came = swap(held[k], TP, size, low)
            held[k ^ low] = (held[k ^ low].astype(f32) + came.astype(f32)).astype(bf16)
    hops = [held[0]]
    for k in range(size - 1, 0, -1):
        if lowest_bit(k) == k:
            hops.append(swap(held[k], TP, size, k))
    return sum_of(hops) if total else hops


def sum_of(arrays):
    total = arrays[0].astype(f32)
    for value in arrays[1:]:
        total = total + value.astype(f32)
    return total


def sum_over_dp(keep, send, size, index, between=None, picked=0):
    groups = size // 2
    rows, width = keep.shape[0] // groups, keep.shape[1]
    came = swap(send, DP, size, 1)
    pieces = call_kernel(
        functools.partial(add_split_body, groups),
        index,
        (keep, came),
        [((rows, width), bf16)] * groups,
    )
    came = [swap(pieces[j], DP, size, 2 * j) for j in range(1, groups)]
    outs = [((rows, width), bf16)]
    if picked:
        outs = outs + [((rows, picked), bf16)]
    total, *rest = call_kernel(
        functools.partial(add_body, groups, picked), index, (pieces[0], *came), outs
    )
    if between is not None:
        total = between(total, *rest)
    mine = [total]
    mine = mine + [swap(total, DP, size, 2 * j) for j in range(1, groups)]
    return mine + [swap(piece, DP, size, 1) for piece in mine]


def block(
    inputs,
    segments,
    mixers_norm_gain,
    query_weight,
    key_weight,
    value_weight,
    attention_out,
    mamba_gate,
    mamba_input,
    state_weight,
    step_weight,
    kernel_input,
    kernel_state,
    offset_input,
    offset_state,
    step_bias,
    decay_log,
    skip_gain,
    mamba_out,
    feedforward_norm_gain,
    gate_weight,
    up_weight,
    down_weight,
    cotangent,
    *,
    dp,
    tensor,
):
    local_heads = query_weight.shape[1] // HD
    group = QH // KVH
    assert tensor == 4 and KVH * HD == LANES and 2 * local_heads == group
    rows, width = inputs.shape
    length = rows * tensor
    heads = step_weight.shape[1]
    wq = query_weight.shape[1]
    wkv = 2 * HD
    wx = mamba_input.shape[1]
    wbc = state_weight.shape[1]
    wst = LANES
    units = gate_weight.shape[1]
    kc = kernel_input.shape[0]
    widths = (wq, wkv, wx, wx, wbc, wst)
    t_index = lax.axis_index(TP)
    t_array = jnp.where(
        lax.iota(jnp.int32, 2) == 0, t_index, lax.axis_index(DP)
    ).astype(jnp.int32)

    parts = gather_parts(inputs, tensor)
    cot_parts = gather_parts(cotangent, tensor)

    kv_index = t_index * local_heads // group
    key_slice = lax.dynamic_slice_in_dim(key_weight, kv_index * HD, HD, 1)
    value_slice = lax.dynamic_slice_in_dim(value_weight, kv_index * HD, HD, 1)
    step_pad = jnp.pad(step_weight.T, ((0, LANES - heads), (0, 0)))
    kv_weight = jnp.concatenate([key_slice, value_slice], 1)
    weights = (query_weight, kv_weight, mamba_gate, mamba_input, state_weight, step_pad)
    taps = jnp.concatenate([kernel_input, kernel_state], 1)
    offs = jnp.concatenate([offset_input, offset_state], 0)[None, :]
    bias = jnp.pad(step_bias, (0, LANES - heads))[None, :]
    nega = jnp.pad(-jnp.exp(decay_log), (0, LANES - heads))[None, :]
    skip = jnp.repeat(skip_gain, wx // heads)[None, :]
    seg_row = segments[None, :]
    gain1 = mixers_norm_gain[None, :]

    full = (length, width)
    blocks = [((rows, width), bf16)] * tensor
    square = ((length, length), f32)
    (n1, qkv, att, stat, z, u, acc, ysum, gated, raw, *held) = call_kernel(
        functools.partial(fwd_body, widths, kc, heads, tensor),
        t_array,
        (*parts, seg_row, gain1, *weights, taps, offs, bias, nega, skip, attention_out, mamba_out),
        [
            (full, bf16),
            ((length, wq + 2 * LANES), bf16),
            ((length, LANES), bf16),
            ((length, LANES), f32),
            ((length, wx), f32),
            ((length, wx + wbc), f32),
            ((length, wx + wbc), f32),
            ((length, wx), f32),
            ((length, wx), bf16),
            ((length, wst), f32),
            square,
            square,
            ((length, wst), f32),
            ((wst, length), f32),
            ((length, wst), f32),
            ((kc - 1, length, LANES), f32),
            *blocks,
        ],
        [
            (full, bf16),
            (query_weight.shape, bf16),
            (attention_out.shape, bf16),
            (mamba_out.shape, bf16),
            (pltpu.SemaphoreType.DMA((3,)), None),
        ],
        far=(tensor + 2, tensor + 13, tensor + 14),
    )
    mask, g, run, run_t, dt, link, *mixed_blocks = held

    inputs_float = inputs.astype(f32)
    hidden_first = inputs_float + scatter_parts(mixed_blocks, tensor)
    reciprocal_second = rms_recip(hidden_first)
    unit_second = hidden_first * reciprocal_second
    local_normed_second = (unit_second * feedforward_norm_gain[None, :]).astype(bf16)
    n2_parts = gather_parts(local_normed_second, tensor)

    cot_rows = jnp.concatenate(cot_parts, 0)
    dhidden = dot_t(cot_rows, down_weight)
    n2, hidden, dgu, *dn2_blocks = call_kernel(
        lambda scalar, *refs: feed_body(tensor, *refs),
        t_array,
        (*n2_parts, dhidden, gate_weight, up_weight),
        [(full, bf16), ((length, units), bf16), ((length, 2 * units), bf16), *blocks],
    )
    dn2 = scatter_parts(dn2_blocks, tensor)
    scaled_second = dn2 * feedforward_norm_gain[None, :]
    grad_hidden = cotangent.astype(f32) + reciprocal_second * (
        scaled_second - unit_second * jnp.mean(scaled_second * unit_second, axis=-1, keepdims=True)
    )
    feed_grad = jnp.sum(dn2 * unit_second, axis=0)
    dparts = gather_parts(grad_hidden.astype(bf16), tensor)

    span = width // 2 + units // 2
    feed_keep, feed_send = call_kernel(
        functools.partial(feed_grads_body, dp // 2),
        t_array,
        (n2, dgu, hidden, cot_rows),
        [((span, width), bf16)] * 2,
    )
    feed_sum = sum_over_dp(feed_keep, feed_send, dp, t_array)

    mid_rows = wq + wx
    d1, dssm, mid_keep, mid_send = call_kernel(
        functools.partial(attention_bwd_body, widths, heads, tensor),
        t_array,
        (
            *dparts, skip, attention_out, mamba_out, mask,
            qkv, att, stat, z, acc, ysum, gated, n1,
        ),
        [
            ((length, wq + wkv + wx), bf16),
            ((length, wx), f32),
            ((mid_rows, width), bf16),
            ((mid_rows, width), bf16),
        ],
        [(full, bf16)],
    )
    mid_sum = sum_over_dp(mid_keep, mid_send, dp, t_array)

    feed_part = dot(hidden, down_weight).astype(bf16)
    feed_blocks = [feed_part[k * rows : (k + 1) * rows] for k in range(tensor)]
    feed_total = scatter_parts(feed_blocks, tensor)
    hidden_held, feed_total = lax.optimization_barrier((hidden_first, feed_total))
    output = (hidden_held + feed_total).astype(bf16)

    wl = wkv + wbc + wst + wx
    late_keep, late_send, *dn1_blocks = call_kernel(
        functools.partial(state_bwd_body, widths, kc, heads, tensor),
        t_array,
        (
            gain1, *weights, taps, nega, skip, mask, g, run, run_t, dt, link,
            n1, u, acc, ysum, raw, d1, dssm, feed_grad[None, :],
        ),
        [((width // 2, wl), bf16), ((width // 2, wl), bf16), *blocks],
        [
            ((length, wx + wbc + wst), bf16),
            ((2 * kc, wx + wbc), f32),
            (full, bf16),
            square,
            ((length, wx + wbc), f32),
            ((LANES, width), f32),
        ],
    )
    dn1_hops = scatter_parts(dn1_blocks, tensor, total=False)
    picked = wkv + wbc + wst
    wide = 2 * KVH * HD + wbc + wst + wx

    def combine(own, shared):
        pair = shared + swap(shared, TP, tensor, 1)
        (out,) = call_kernel(
            functools.partial(combine_body, widths, heads, 2 * kc, local_heads),
            t_array,
            (own, pair, swap(pair, TP, tensor, 2)),
            [((own.shape[0], wide), bf16)],
        )
        return out

    late_sum = sum_over_dp(late_keep, late_send, dp, t_array, combine, picked)

    (dn1_hops, _) = lax.optimization_barrier((dn1_hops, late_sum[len(late_sum) // 2 :]))
    (block_input_gradient,) = call_kernel(
        input_grad_body,
        t_array,
        (*dn1_hops, inputs, grad_hidden, gain1),
        [((rows, width), f32)],
        leaves=True,
    )
    groups = dp // 2
    feed_shapes = [((width, units), f32), ((width, units), f32), ((units, width), f32)]
    grad_gate, grad_up, grad_down = call_kernel(
        functools.partial(feed_out_body, groups),
        t_array,
        feed_sum,
        feed_shapes,
        [*feed_shapes, (pltpu.SemaphoreType.DMA((6 * groups,)), None)],
        leaves=True,
        far_outs=3,
    )
    mid_shapes = [((wq, width), f32), ((wx, width), f32), ((width, wx), f32), ((width, wq), f32)]
    grad_attn_out, grad_mamba_out, grad_mgate, grad_query = call_kernel(
        functools.partial(mid_out_body, widths, groups),
        t_array,
        mid_sum,
        mid_shapes,
        [*mid_shapes, ((2 * (wq + wx), width), bf16), (pltpu.SemaphoreType.DMA((4,)), None)],
        leaves=True,
        far_outs=4,
    )
    late_shapes = [
        ((width, KVH * HD), f32),
        ((width, KVH * HD), f32),
        ((width, wbc), f32),
        ((width, wx), f32),
    ]
    (
        grad_key,
        grad_value,
        grad_state,
        grad_minput,
        grad_step,
        grad_kinput,
        grad_oinput,
        grad_skip,
        grad_sbias,
        grad_dlog,
        mixers_grad,
        feedforward_grad,
        grad_kstate,
        grad_ostate,
    ) = call_kernel(
        functools.partial(late_out_body, widths, heads, kc, groups),
        t_array,
        late_sum,
        [
            *late_shapes,
            ((heads, width), f32),
            ((kc, wx), f32),
            ((1, wx), f32),
            ((1, heads), f32),
            ((1, heads), f32),
            ((1, heads), f32),
            ((1, width), f32),
            ((1, width), f32),
            ((kc, wbc), f32),
            ((1, wbc), f32),
        ],
        [
            *late_shapes,
            ((width, wide), bf16),
            ((LANES, width), f32),
            (pltpu.SemaphoreType.DMA((4,)), None),
        ],
        leaves=True,
        far_outs=4,
    )
    grad_step = grad_step.T
    grad_oinput, grad_skip, grad_sbias, grad_dlog, mixers_grad, feedforward_grad, grad_ostate = (
        value[0]
        for value in (
            grad_oinput, grad_skip, grad_sbias, grad_dlog, mixers_grad, feedforward_grad, grad_ostate
        )
    )
    return (
        output,
        block_input_gradient,
        mixers_grad,
        grad_query,
        grad_key,
        grad_value,
        grad_attn_out,
        grad_mgate,
        grad_minput,
        grad_state,
        grad_step,
        grad_kinput,
        grad_kstate,
        grad_oinput,
        grad_ostate,
        grad_sbias,
        grad_dlog,
        grad_skip,
        grad_mamba_out,
        feedforward_grad,
        grad_gate,
        grad_up,
        grad_down,
    )


def solution(mesh):
    in_specs = (
        P((DP, TP), None),
        P(DP),
        P(),
        P(None, TP),
        P(),
        P(),
        P(TP, None),
        P(None, TP),
        P(None, TP),
        P(),
        P(None, TP),
        P(None, TP),
        P(),
        P(TP),
        P(),
        P(TP),
        P(TP),
        P(TP),
        P(TP, None),
        P(),
        P(None, TP),
        P(None, TP),
        P(TP, None),
        P((DP, TP), None),
    )
    out_specs = (
        P((DP, TP), None),
        P((DP, TP), None),
        P(),
        P(None, TP),
        P(),
        P(),
        P(TP, None),
        P(None, TP),
        P(None, TP),
        P(),
        P(None, TP),
        P(None, TP),
        P(),
        P(TP),
        P(),
        P(TP),
        P(TP),
        P(TP),
        P(TP, None),
        P(),
        P(None, TP),
        P(None, TP),
        P(TP, None),
    )
    body = functools.partial(block, dp=mesh.shape[DP], tensor=mesh.shape[TP])
    return jax.shard_map(body, mesh=mesh, in_specs=in_specs, out_specs=out_specs, check_vma=False)
```

```python
import functools

import jax
import jax.numpy as jnp
from jax import lax
from jax.experimental import pallas as pl
from jax.experimental.pallas import tpu as pltpu
from jax.sharding import PartitionSpec as P


QH = 8
KVH = 2
HD = 64
LANES = 128
BLOCKS = 4

eps = 1e-05
big_negative = -1e30
f32 = jnp.float32
bf16 = jnp.bfloat16

DP = "dp"
TP = "tensor"


def dot(left, right):
    return jnp.dot(left, right, preferred_element_type=f32)


def tdot(left, right):
    return lax.dot_general(left, right, (((0,), (0,)), ((), ())), preferred_element_type=f32)


def dot_t(left, right):
    return lax.dot_general(left, right, (((1,), (1,)), ((), ())), preferred_element_type=f32)


def split3(value):
    high = value.astype(bf16)
    rest = value - high.astype(f32)
    mid = rest.astype(bf16)
    return high, mid, (rest - mid.astype(f32)).astype(bf16)


def exact_left(mask, value):
    high, mid, low = split3(value)
    return dot(mask, high) + (dot(mask, mid) + dot(mask, low))


def rms_recip(values):
    return lax.rsqrt(jnp.mean(values * values, axis=-1, keepdims=True) + eps)


def sigmoid(value):
    return 1.0 / (1.0 + jnp.exp(-value))


def lane_ids(rows, width):
    return lax.broadcasted_iota(jnp.int32, (rows, width), 1)


def pair_columns(values, pair, lanes):
    first = values[:, 2 * pair : 2 * pair + 1]
    second = values[:, 2 * pair + 1 : 2 * pair + 2]
    return jnp.where(lanes < HD, first, second)


def masks_body(taps_count, t_ref, seg_ref, mask_ref, tri_ref, link_ref):
    length = mask_ref.shape[0]
    seg_row = seg_ref[0:1, :].astype(f32)
    seg_col = jnp.broadcast_to(seg_row, (LANES, length)).T
    row_pos = lax.broadcasted_iota(jnp.int32, (length, length), 0)
    col_pos = lax.broadcasted_iota(jnp.int32, (length, length), 1)
    allowed = (row_pos >= col_pos) & (seg_col[:, 0:1] == seg_row)
    mask_ref[...] = jnp.where(allowed, 0.0, big_negative)
    tri_ref[...] = (row_pos >= col_pos).astype(f32).astype(bf16)
    spots = lax.broadcasted_iota(jnp.int32, (length, LANES), 0)
    for shift_by in range(1, taps_count):
        linked = (pltpu.roll(seg_col, shift_by, 0) == seg_col) & (spots >= shift_by)
        link_ref[shift_by - 1] = jnp.where(linked, 1.0, 0.0)


def ahead_body(
    widths, taps_count, heads, t_ref, mask_ref, link_ref, qkv_ref, stat_ref, u_ref, acc_ref,
    g_ref, run_ref, run_t_ref, dt_ref,
    probs_ref, weight_ref, mixing_ref, slope_ref, xc_ref, ub_ref, moved_ref, linked_ref,
):
    wq, _, _, _, _, _ = widths
    length = acc_ref.shape[0]
    lanes = lane_ids(length, LANES)
    lane_lo = lanes < HD
    half = length // BLOCKS
    scale = HD ** (-0.5)
    keys2 = qkv_ref[:, wq : wq + LANES]
    for head in range(2):
        keep = lane_lo if head == 0 else ~lane_lo
        q_m = jnp.where(keep, qkv_ref[:, 0:wq].astype(f32), 0.0).astype(bf16)
        logsum = stat_ref[:, head * HD : head * HD + 1]
        for block in range(BLOCKS):
            lo, hi = block * half, (block + 1) * half
            scores = dot_t(q_m[lo:hi], keys2[:hi]) * scale + mask_ref[lo:hi, 0:hi]
            probs_ref[head, lo:hi, 0:hi] = jnp.exp(scores - logsum[lo:hi])
    run = run_ref[...]
    run_t = run_t_ref[...]
    for head in range(heads):
        for block in range(BLOCKS):
            lo, hi = block * half, (block + 1) * half
            spread = run[lo:hi, head : head + 1] - run_t[head : head + 1, 0:hi]
            weight = jnp.exp(spread + mask_ref[lo:hi, 0:hi])
            weight_ref[head, lo:hi, 0:hi] = weight
            mixing_ref[head, lo:hi, 0:hi] = (weight * g_ref[lo:hi, 0:hi]).astype(bf16)
    acc = acc_ref[...]
    sig = sigmoid(acc)
    slope_ref[...] = sig * (1.0 + acc * (1.0 - sig))
    for pair in range(heads // 2):
        cols = slice(pair * LANES, (pair + 1) * LANES)
        xc = acc[:, cols] * sig[:, cols]
        xc_ref[:, cols] = xc
        ub_ref[:, cols] = (xc * pair_columns(dt_ref[...], pair, lanes)).astype(bf16)
    u = u_ref[...]
    for shift_by in range(1, taps_count):
        moved_ref[shift_by - 1] = link_ref[shift_by - 1, :, 0:1] * pltpu.roll(u, shift_by, 0)
    linked_ref[...] = jnp.where(mask_ref[...] == 0.0, 1.0, 0.0).astype(bf16)


def fwd_body(widths, taps_count, heads, tensor, *refs):
    (t_ref,) = refs[:1]
    parts = refs[1 : 1 + tensor]
    (
        mask_ref,
        tri_ref,
        link_ref,
        gain_ref,
        query_w_ref,
        kv_w_ref,
        gate_w_ref,
        input_w_ref,
        state_w_ref,
        step_w_ref,
        taps_ref,
        offs_ref,
        bias_ref,
        nega_ref,
        skip_ref,
        att_w_ref,
        mam_w_ref,
        n1_ref,
        qkv_ref,
        att_ref,
        stat_ref,
        z_ref,
        u_ref,
        acc_ref,
        ysum_ref,
        gated_ref,
        raw_ref,
        g_ref,
        run_ref,
        run_t_ref,
        dt_ref,
        *mixed_refs,
        mixed_ref,
        query_v,
        state_v,
        att_v,
        mam_v,
        sems,
    ) = refs[1 + tensor :]
    wq, _, _, wx, wbc, _ = widths
    copies = Copies(sems)
    for source, target in (
        (query_w_ref, query_v),
        (state_w_ref, state_v),
        (att_w_ref, att_v),
        (mam_w_ref, mam_v),
    ):
        copies.start(source, target)
    t = t_ref[0]
    rows = parts[0].shape[0]
    length = rows * tensor
    state = wbc // 2
    for k in range(tensor):
        xf = parts[k][...].astype(f32)
        normed = (xf * rms_recip(xf) * gain_ref[...]).astype(bf16)
        n1_ref[pl.ds(pl.multiple_of((t ^ k) * rows, rows), rows), :] = normed
    n1 = n1_ref[...]
    copies.wait(0, 1)
    query = dot(n1, query_v[...]).astype(bf16)
    kv = dot(n1, kv_w_ref[...])
    lanes = lane_ids(length, LANES)
    kv_swap = pltpu.roll(kv, HD, 1)
    keys2 = jnp.where(lanes < HD, kv, kv_swap).astype(bf16)
    values2 = jnp.where(lanes < HD, kv_swap, kv).astype(bf16)
    qkv_ref[:, 0:wq] = query
    qkv_ref[:, wq : wq + LANES] = keys2
    qkv_ref[:, wq + LANES :] = values2
    z_ref[...] = dot(n1, gate_w_ref[...])
    u_ref[:, :wx] = dot(n1, input_w_ref[...])
    copies.wait(1, 2)
    u_ref[:, wx:] = dot(n1, state_v[...])
    raw = dot_t(n1, step_w_ref[...]) + bias_ref[...]
    raw_ref[...] = raw

    lane_lo = lanes < HD
    scale = HD ** (-0.5)
    half = length // BLOCKS
    for block in range(BLOCKS):
        lo, hi = block * half, (block + 1) * half
        out = jnp.zeros((half, LANES), f32)
        stats = []
        for head in range(2):
            keep = lane_lo[:half] if head == 0 else ~lane_lo[:half]
            keep_v = lane_lo[:hi] if head == 0 else ~lane_lo[:hi]
            q_rows = jnp.where(keep, query[lo:hi].astype(f32), 0.0).astype(bf16)
            scores = dot_t(q_rows, keys2[:hi]) * scale + mask_ref[lo:hi, 0:hi]
            top = jnp.max(scores, axis=-1, keepdims=True)
            expo = jnp.exp(scores - top)
            total = jnp.sum(expo, axis=-1, keepdims=True)
            probs = (expo / total).astype(bf16)
            v_rows = jnp.where(keep_v, values2[:hi].astype(f32), 0.0).astype(bf16)
            out = out + dot(probs, v_rows)
            stats.append(top + jnp.log(total))
        att_ref[lo:hi, :] = out.astype(bf16)
        stat_ref[lo:hi, :] = jnp.where(lane_lo[:half], stats[0], stats[1])

    u = u_ref[...]
    acc = offs_ref[...] + taps_ref[0:1, :] * u
    for shift_by in range(1, taps_count):
        acc = acc + taps_ref[shift_by : shift_by + 1, :] * (
            link_ref[shift_by - 1, :, 0:1] * pltpu.roll(u, shift_by, 0)
        )
    acc_ref[...] = acc

    dt = jnp.maximum(raw, 0.0) + jnp.log1p(jnp.exp(-jnp.abs(raw)))
    run = exact_left(tri_ref[...], dt * nega_ref[...])
    run_t = run.T
    dt_ref[...] = dt
    run_ref[...] = run
    run_t_ref[...] = run_t
    bc = acc_ref[:, wx:]
    bc = (bc * sigmoid(bc)).astype(bf16)
    g_ref[...] = dot_t(bc[:, state:], bc[:, :state])
    for pair in range(heads // 2):
        cols = slice(pair * LANES, (pair + 1) * LANES)
        xa = acc_ref[:, cols]
        xc = xa * sigmoid(xa)
        uu = xc * pair_columns(dt, pair, lanes)
        u_lo = jnp.where(lane_lo, uu, 0.0).astype(bf16)
        u_hi = jnp.where(lane_lo, 0.0, uu).astype(bf16)
        for block in range(BLOCKS):
            lo, hi = block * half, (block + 1) * half
            total = jnp.zeros((half, LANES), f32)
            for side, masked in ((0, u_lo), (1, u_hi)):
                head = 2 * pair + side
                spread = run[lo:hi, head : head + 1] - run_t[head : head + 1, 0:hi]
                weight = jnp.exp(spread + mask_ref[lo:hi, 0:hi])
                mixing = (weight * g_ref[lo:hi, 0:hi]).astype(bf16)
                total = total + dot(mixing, masked[:hi])
            ysum_ref[lo:hi, cols] = total
        y = ysum_ref[:, cols] + skip_ref[0:1, cols] * xc
        z = z_ref[:, cols]
        gated_ref[:, cols] = (y * z * sigmoid(z)).astype(bf16)
    copies.wait(2)
    mixed = dot(att_ref[...], att_v[...]) + dot(gated_ref[...], mam_v[...])
    mixed_ref[...] = mixed.astype(bf16)
    for k in range(tensor):
        mixed_refs[k][...] = mixed_ref[pl.ds(pl.multiple_of((t ^ k) * rows, rows), rows), :]


def attention_bwd_body(widths, heads, tensor, *refs):
    t_ref = refs[0]
    dparts = refs[1 : 1 + tensor]
    (
        skip_ref,
        att_w_ref,
        mam_w_ref,
        probs_ref,
        xc_ref,
        qkv_ref,
        att_ref,
        z_ref,
        ysum_ref,
        gated_ref,
        n1_ref,
        d_ref,
        dssm_ref,
        keep_ref,
        send_ref,
        dmixed_ref,
    ) = refs[1 + tensor :]
    wq, wkv, _, wx, _, _ = widths
    t = t_ref[0]
    rows = dparts[0].shape[0]
    length = rows * tensor
    for k in range(tensor):
        dmixed_ref[pl.ds(pl.multiple_of((t ^ k) * rows, rows), rows), :] = dparts[k][...]
    dmixed = dmixed_ref[...]
    lane_lo = lane_ids(length, LANES) < HD
    half = length // BLOCKS
    scale = HD ** (-0.5)

    datt = dot_t(dmixed, att_w_ref[...]).astype(bf16)
    datt_f = datt.astype(f32)
    prod = datt_f * att_ref[...].astype(f32)
    query = qkv_ref[:, 0:wq]
    keys2 = qkv_ref[:, wq : wq + LANES]
    values2 = qkv_ref[:, wq + LANES :]
    dq = [jnp.zeros((half, LANES), f32) for _ in range(BLOCKS)]
    dk = [jnp.zeros((half, LANES), f32) for _ in range(BLOCKS)]
    dv = [jnp.zeros((half, LANES), f32) for _ in range(BLOCKS)]
    for head in range(2):
        keep = lane_lo if head == 0 else ~lane_lo
        q_m = jnp.where(keep, query.astype(f32), 0.0).astype(bf16)
        k_m = jnp.where(keep, keys2.astype(f32), 0.0).astype(bf16)
        d_m = jnp.where(keep, datt_f, 0.0).astype(bf16)
        delta = jnp.sum(jnp.where(keep, prod, 0.0), axis=-1, keepdims=True)
        for block in range(BLOCKS):
            lo, hi = block * half, (block + 1) * half
            probs = probs_ref[head, lo:hi, 0:hi]
            dprob = dot_t(d_m[lo:hi], values2[:hi])
            dscore = (probs * (dprob - delta[lo:hi]) * scale).astype(bf16)
            dq[block] = dq[block] + dot(dscore, k_m[:hi])
            dk_add = tdot(dscore, q_m[lo:hi])
            dv_add = tdot(probs.astype(bf16), d_m[lo:hi])
            for part in range(block + 1):
                dk[part] = dk[part] + dk_add[part * half : (part + 1) * half]
                dv[part] = dv[part] + dv_add[part * half : (part + 1) * half]
    for block in range(BLOCKS):
        lo, hi = block * half, (block + 1) * half
        d_ref[lo:hi, 0:wq] = dq[block].astype(bf16)
        dk_sum = dk[block] + pltpu.roll(dk[block], HD, 1)
        dv_sum = dv[block] + pltpu.roll(dv[block], HD, 1)
        d_ref[lo:hi, wq : wq + wkv] = jnp.where(lane_lo[:half], dk_sum, dv_sum).astype(bf16)

    base = wq + wkv
    for pair in range(heads // 2):
        cols = slice(pair * LANES, (pair + 1) * LANES)
        xc = xc_ref[:, cols]
        z = z_ref[:, cols]
        zs = sigmoid(z)
        dgated = dot_t(dmixed, mam_w_ref[cols, :])
        dssm_ref[:, cols] = dgated * z * zs
        y = ysum_ref[:, cols] + skip_ref[0:1, cols] * xc
        dz = dgated * y * zs * (1.0 + z * (1.0 - zs))
        d_ref[:, base + pair * LANES : base + (pair + 1) * LANES] = dz.astype(bf16)
    upper = t_ref[1] % 2
    n1 = n1_ref[...]
    gz = tdot(d_ref[:, base:], n1)
    split_store(upper, tdot(att_ref[...], dmixed), gz[wx - wq :], keep_ref, send_ref, 0)
    second = jnp.concatenate([gz[: wx - wq], tdot(d_ref[:, :wq], n1)], 0)
    split_store(upper, tdot(gated_ref[...], dmixed), second, keep_ref, send_ref, wq)


def state_bwd_body(widths, taps_count, heads, tensor, *refs):
    (
        t_ref,
        gain_ref,
        query_w_ref,
        kv_w_ref,
        gate_w_ref,
        input_w_ref,
        state_w_ref,
        step_w_ref,
        taps_ref,
        nega_ref,
        skip_ref,
        weight_ref,
        mixing_ref,
        slope_ref,
        xc_ref,
        ub_ref,
        moved_ref,
        linked_ref,
        dt_ref,
        link_ref,
        n1_ref,
        u_ref,
        acc_ref,
        ysum_ref,
        raw_ref,
        d1_ref,
        dssm_ref,
        gfeed_ref,
    ) = refs[:28]
    (
        keep_ref,
        send_ref,
        *dn1_refs,
        d2_ref,
        small_ref,
        dn1_ref,
        dg_ref,
        dact_ref,
        rows_ref,
    ) = refs[28:]
    wq, wkv, _, wx, wbc, _ = widths
    t = t_ref[0]
    length = n1_ref.shape[0]
    rows = length // tensor
    state = wbc // 2
    lanes = lane_ids(length, LANES)
    lane_lo = lanes < HD
    half = length // BLOCKS

    raw = raw_ref[...]
    dt = dt_ref[...]
    ld = dt * nega_ref[...]
    bc_acc = acc_ref[:, wx:]
    bc = (bc_acc * sigmoid(bc_acc)).astype(bf16)
    dg_ref[...] = jnp.zeros((length, length), f32)
    drun = jnp.zeros((length, LANES), f32)
    ddt = jnp.zeros((length, LANES), f32)
    skip_row = jnp.zeros((1, LANES), f32)
    small_ref[...] = jnp.zeros(small_ref.shape, f32)
    for pair in range(heads // 2):
        cols = slice(pair * LANES, (pair + 1) * LANES)
        xc = xc_ref[:, cols]
        skip = skip_ref[0:1, cols]
        ysum = ysum_ref[:, cols]
        dssm = dssm_ref[:, cols]
        dskip = jnp.sum(dssm * xc, axis=0, keepdims=True)
        for side in range(2):
            keep = lane_lo[0:1] if side == 0 else ~lane_lo[0:1]
            head_sum = jnp.sum(jnp.where(keep, dskip, 0.0), axis=-1, keepdims=True)
            skip_row = jnp.where(lanes[0:1] == 2 * pair + side, head_sum, skip_row)
        dt_pair = pair_columns(dt, pair, lanes)
        u_b = ub_ref[:, cols]
        dy_b = dssm.astype(bf16)
        u_f = u_b.astype(f32)
        dy_f = dy_b.astype(f32)
        du = [jnp.zeros((half, LANES), f32) for _ in range(BLOCKS)]
        for side in range(2):
            head = 2 * pair + side
            keep = lane_lo if side == 0 else ~lane_lo
            dy_m = jnp.where(keep, dy_f, 0.0).astype(bf16)
            for block in range(BLOCKS):
                lo, hi = block * half, (block + 1) * half
                weight = weight_ref[head, lo:hi, 0:hi]
                mixing = mixing_ref[head, lo:hi, 0:hi]
                dmix = dot_t(dy_m[lo:hi], u_b[:hi])
                dg_ref[lo:hi, 0:hi] += weight * dmix
                du_add = tdot(mixing, dy_m[lo:hi])
                for part in range(block + 1):
                    du[part] = du[part] + du_add[part * half : (part + 1) * half]
        du = jnp.concatenate(du, 0)
        balance = dy_f * ysum - u_f * du
        weighted = du * xc
        for side in range(2):
            head = 2 * pair + side
            keep = lane_lo if side == 0 else ~lane_lo
            here = lanes == head
            drun = jnp.where(
                here, jnp.sum(jnp.where(keep, balance, 0.0), axis=-1, keepdims=True), drun
            )
            ddt = jnp.where(
                here, jnp.sum(jnp.where(keep, weighted, 0.0), axis=-1, keepdims=True), ddt
            )
        dact_ref[:, cols] = du * dt_pair + skip * dssm
    dg = dg_ref[...].astype(bf16)
    dact_ref[:, wx : wx + state] = tdot(dg, bc[:, state:])
    dact_ref[:, wx + state :] = dot(dg, bc[:, :state])
    linked = linked_ref[...]
    high, mid, low = split3(drun)
    dld = tdot(linked, high) + (tdot(linked, mid) + tdot(linked, low))
    ddt = ddt + dld * nega_ref[...]
    dstep = ddt * sigmoid(raw)
    d2_ref[:, wx + wbc :] = dstep.astype(bf16)

    dconv = dact_ref[...] * slope_ref[...]
    u = u_ref[...]
    small_ref[0:1, :] = jnp.sum(dconv * u, axis=0, keepdims=True)
    small_ref[taps_count : taps_count + 1, :] = jnp.sum(dconv, axis=0, keepdims=True)
    du_in = dconv * taps_ref[0:1, :]
    for shift_by in range(1, taps_count):
        masked = dconv * link_ref[shift_by - 1, :, 0:1]
        small_ref[shift_by : shift_by + 1, :] = jnp.sum(
            dconv * moved_ref[shift_by - 1], axis=0, keepdims=True
        )
        du_in = du_in + taps_ref[shift_by : shift_by + 1, :] * pltpu.roll(
            masked, length - shift_by, 0
        )
    d2_ref[:, 0 : wx + wbc] = du_in.astype(bf16)
    small_ref[taps_count + 1 : taps_count + 2, 0:LANES] = skip_row
    small_ref[taps_count + 2 : taps_count + 3, 0:LANES] = jnp.sum(dstep, axis=0, keepdims=True)
    small_ref[taps_count + 3 : taps_count + 4, 0:LANES] = jnp.sum(dld * ld, axis=0, keepdims=True)
    dn1 = dot_t(d1_ref[:, :wq], query_w_ref[...]) + dot_t(d1_ref[:, wq : wq + wkv], kv_w_ref[...])
    dn1 = dn1 + dot_t(d1_ref[:, wq + wkv :], gate_w_ref[...])
    dn1 = dn1 + dot_t(d2_ref[:, :wx], input_w_ref[...])
    dn1 = dn1 + dot_t(d2_ref[:, wx : wx + wbc], state_w_ref[...])
    dn1 = dn1 + dot(d2_ref[:, wx + wbc :], step_w_ref[...])
    dn1_ref[...] = dn1.astype(bf16)
    for k in range(tensor):
        dn1_refs[k][...] = dn1_ref[pl.ds(pl.multiple_of((t ^ k) * rows, rows), rows), :]
    gmix = jnp.sum(dn1 * n1_ref[...].astype(f32), axis=0, keepdims=True) / gain_ref[...]
    late_grads(
        widths, heads, t_ref[1] % 2, n1_ref, d1_ref, d2_ref, small_ref, gmix, gfeed_ref[...],
        keep_ref, send_ref, rows_ref,
    )


def feed_body(count, *refs):
    parts = refs[:count]
    dhidden_ref, gate_ref, up_ref, n2_ref, hidden_ref, dgu_ref = refs[count : count + 6]
    dn2_refs = refs[count + 6 :]
    rows = parts[0].shape[0]
    units = gate_ref.shape[1]
    for k in range(count):
        n2_ref[k * rows : (k + 1) * rows, :] = parts[k][...]
    n2 = n2_ref[...]
    gate_pre = dot(n2, gate_ref[...])
    up_pre = dot(n2, up_ref[...])
    gsig = sigmoid(gate_pre)
    gate_act = gate_pre * gsig
    dhidden = dhidden_ref[...]
    dgate = (dhidden * up_pre * gsig * (1.0 + gate_pre * (1.0 - gsig))).astype(bf16)
    dup = (dhidden * gate_act).astype(bf16)
    dn2 = (dot_t(dgate, gate_ref[...]) + dot_t(dup, up_ref[...])).astype(bf16)
    for k in range(count):
        dn2_refs[k][...] = dn2[k * rows : (k + 1) * rows]
    hidden_ref[...] = (gate_act * up_pre).astype(bf16)
    dgu_ref[:, :units] = dgate
    dgu_ref[:, units:] = dup


def split_store(upper, first, second, keep_ref, send_ref, at):
    size = first.shape[0]
    low = upper == 0
    keep_ref[at : at + size, :] = jnp.where(low, first, second).astype(bf16)
    send_ref[at : at + size, :] = jnp.where(low, second, first).astype(bf16)


def feed_grads_body(groups, u_ref, *refs):
    n2_refs, dgu_refs, hidden_refs, cot_refs = refs[0:2], refs[2:4], refs[4:6], refs[6:8]
    keep_ref, send_ref = refs[8:]
    half_wide = n2_refs[0].shape[1] // 2
    half_tall = hidden_refs[0].shape[1] // 2
    wide, tall = half_wide // groups, half_tall // groups
    low = u_ref[1] % 2 == 0
    for sources, others, half, size, skip in (
        (n2_refs, dgu_refs, half_wide, wide, 0),
        (hidden_refs, cot_refs, half_tall, tall, wide),
    ):
        first, second = (
            sum(
                tdot(source[:, side * half : (side + 1) * half], other[...])
                for source, other in zip(sources, others)
            )
            for side in range(2)
        )
        keep = jnp.where(low, first, second).astype(bf16)
        send = jnp.where(low, second, first).astype(bf16)
        for q in range(groups):
            at = q * (wide + tall) + skip
            keep_ref[at : at + size, :] = keep[q * size : (q + 1) * size]
            send_ref[at : at + size, :] = send[q * size : (q + 1) * size]


def late_grads(
    widths, heads, upper, n1_ref, d1_ref, d2_ref, small_ref, gmix, gfeed,
    keep_ref, send_ref, rows_ref,
):
    wq, wkv, _, wx, wbc, wst = widths
    count = small_ref.shape[0]
    width = n1_ref.shape[1]
    half = width // 2
    rows_ref[...] = jnp.zeros(rows_ref.shape, f32)
    at = heads
    rows_ref[at : at + count, 0:wx] = small_ref[:, :wx]
    at += count
    rows_ref[at : at + 1, :] = gmix
    rows_ref[at + 1 : at + 2, :] = gfeed
    at += 2
    rows_ref[at : at + count, 0:wbc] = small_ref[:, wx:]
    extra = rows_ref[...].T
    low = upper == 0
    for source, columns, where_to in (
        (d1_ref, (wq, wq + wkv), 0),
        (d2_ref, (wx, wx + wbc), wkv),
        (d2_ref, (wx + wbc, wx + wbc + wst), wkv + wbc),
        (d2_ref, (0, wx), wkv + wbc + wst),
    ):
        grads = tdot(n1_ref[...], source[:, columns[0] : columns[1]])
        if columns[0] == wx + wbc:
            grads = grads + extra
        first, second = grads[:half], grads[half:]
        span = slice(where_to, where_to + columns[1] - columns[0])
        keep_ref[:, span] = jnp.where(low, first, second).astype(bf16)
        send_ref[:, span] = jnp.where(low, second, first).astype(bf16)


def combine_body(widths, heads, counts, local_heads, t_ref, own_ref, sum_ref, other_ref, out_ref):
    _, wkv, _, _, wbc, wst = widths
    t = t_ref[0]
    group = QH // KVH
    picked = wkv + wbc + wst
    lanes = lane_ids(own_ref.shape[0], LANES)
    first = t * local_heads // group == 0
    own = own_ref[:, :picked].astype(f32)
    mine = sum_ref[...].astype(f32)
    other = other_ref[...].astype(f32)
    low = jnp.where(first, mine[:, :wkv], other[:, :wkv])
    high = jnp.where(first, other[:, :wkv], mine[:, :wkv])
    out_ref[:, :LANES] = jnp.where(lanes < HD, low, pltpu.roll(high, HD, 1)).astype(bf16)
    out_ref[:, LANES : 2 * LANES] = jnp.where(lanes < HD, pltpu.roll(low, HD, 1), high).astype(
        bf16
    )
    total = mine[:, wkv:] + other[:, wkv:]
    at = 2 * LANES
    out_ref[:, at : at + wbc] = total[:, :wbc].astype(bf16)
    at += wbc
    extra = jnp.where(lanes < heads + counts, own[:, wkv + wbc :], total[:, wbc:])
    out_ref[:, at : at + wst] = extra.astype(bf16)
    at += wst
    out_ref[:, at:] = own_ref[:, picked:]


def input_grad_body(t_ref, *refs):
    *hops, inputs_ref, dhidden_ref, gain_ref, out_ref = refs
    xf = inputs_ref[...].astype(f32)
    recip = rms_recip(xf)
    unit = xf * recip
    scaled = sum_of([hop[...] for hop in hops]) * gain_ref[...]
    mean = jnp.mean(scaled * unit, axis=-1, keepdims=True)
    out_ref[...] = dhidden_ref[...] + recip * (scaled - unit * mean)


def piece_places(d, groups):
    for side in range(2):
        half = d % 2 if side == 0 else 1 - d % 2
        for j in range(groups):
            yield side * groups + j, half, (d // 2) ^ j


def merge_rows(d, groups, pieces, full_ref):
    rows = pieces[0].shape[0]
    for at, half, group in piece_places(d, groups):
        where_to = pl.multiple_of((half * groups + group) * rows, rows)
        full_ref[pl.ds(where_to, rows), :] = pieces[at][...]


def feed_out_body(groups, d_ref, *refs):
    pieces = refs[: 2 * groups]
    gate_ref, up_ref, down_ref, gate_stage, up_stage, down_stage, sems = refs[2 * groups :]
    width, units = gate_ref.shape
    wide, tall = width // (2 * groups), units // (2 * groups)
    copies = Copies(sems)
    for at, half, group in piece_places(d_ref[1], groups):
        piece = pieces[at]
        place = half * groups + group
        rows = pl.ds(pl.multiple_of(place * wide, wide), wide)
        gate_stage[rows, :] = piece[:wide, :units].astype(f32)
        copies.start(gate_stage.at[rows, :], gate_ref.at[rows, :])
        up_stage[rows, :] = piece[:wide, units:].astype(f32)
        copies.start(up_stage.at[rows, :], up_ref.at[rows, :])
        rows = pl.ds(pl.multiple_of(place * tall, tall), tall)
        down_stage[rows, :] = piece[wide:, :].astype(f32)
        copies.start(down_stage.at[rows, :], down_ref.at[rows, :])
    copies.wait()


def mid_out_body(widths, groups, d_ref, *refs):
    wq, _, _, wx, _, _ = widths
    outs = refs[2 * groups : 2 * groups + 4]
    stages = refs[2 * groups + 4 : 2 * groups + 8]
    full_ref, sems = refs[2 * groups + 8 :]
    att_stage, mam_stage, gate_stage, query_stage = stages
    merge_rows(d_ref[1], groups, refs[: 2 * groups], full_ref)
    copies = Copies(sems)
    mam_stage[...] = full_ref[wq : wq + wx, :].astype(f32)
    copies.start(mam_stage, outs[1])
    att_stage[...] = full_ref[:wq, :].astype(f32)
    copies.start(att_stage, outs[0])
    at = wq + wx
    gate_stage[:, wx - wq :] = full_ref[at : at + wq, :].astype(f32).T
    gate_stage[:, : wx - wq] = full_ref[at + wq : at + wx, :].astype(f32).T
    copies.start(gate_stage, outs[2])
    query_stage[...] = full_ref[at + wx :, :].astype(f32).T
    copies.start(query_stage, outs[3])
    copies.wait()


def late_out_body(widths, heads, taps_count, groups, d_ref, *refs):
    _, _, _, wx, wbc, wst = widths
    big = refs[2 * groups : 2 * groups + 4]
    (
        step_ref, tap_in_ref, off_in_ref, skip_ref, bias_ref, decay_ref,
        mix_ref, feed_ref, tap_st_ref, off_st_ref,
    ) = refs[2 * groups + 4 : 2 * groups + 14]
    *stages, full_ref, rows_ref, sems = refs[2 * groups + 14 :]
    merge_rows(d_ref[1], groups, refs[: 2 * groups], full_ref)
    copies = Copies(sems)
    sizes = (KVH * HD, KVH * HD, wbc, wx)
    starts = (0, KVH * HD, 2 * KVH * HD, 2 * KVH * HD + wbc + wst)
    for out_ref, stage, size, at in zip(big, stages, sizes, starts):
        stage[...] = full_ref[:, at : at + size].astype(f32)
        copies.start(stage, out_ref)
    at = 2 * KVH * HD + wbc
    rows_ref[...] = full_ref[:, at : at + wst].astype(f32).T
    step_ref[...] = rows_ref[:heads, :]
    at = heads
    tap_in_ref[...] = rows_ref[at : at + taps_count, :wx]
    at += taps_count
    off_in_ref[...] = rows_ref[at : at + 1, :wx]
    skip_ref[...] = rows_ref[at + 1 : at + 2, :heads]
    bias_ref[...] = rows_ref[at + 2 : at + 3, :heads]
    decay_ref[...] = rows_ref[at + 3 : at + 4, :heads]
    at += taps_count
    mix_ref[...] = rows_ref[at : at + 1, :]
    feed_ref[...] = rows_ref[at + 1 : at + 2, :]
    at += 2
    tap_st_ref[...] = rows_ref[at : at + taps_count, :wbc]
    off_st_ref[...] = rows_ref[at + taps_count : at + taps_count + 1, :wbc]
    copies.wait()


def add_split_body(groups, d_ref, keep_ref, came_ref, *outs):
    group = d_ref[1] // 2
    rows = keep_ref.shape[0] // groups
    for j in range(groups):
        at = pl.ds(pl.multiple_of((group ^ j) * rows, rows), rows)
        outs[j][...] = (keep_ref[at, :].astype(f32) + came_ref[at, :].astype(f32)).astype(bf16)


def add_body(groups, picked, d_ref, *refs):
    total = refs[0][...].astype(f32)
    for j in range(1, groups):
        total = total + refs[j][...].astype(f32)
    total = total.astype(bf16)
    refs[groups][...] = total
    if picked:
        refs[groups + 1][...] = total[:, :picked]


def call_kernel(body, scalar, operands, out_shapes, scratch=(), leaves=False, far=(), far_outs=0):
    spec = pl.BlockSpec(memory_space=pltpu.VMEM)
    hbm = pl.BlockSpec(memory_space=pltpu.HBM)
    shape_of = jax.ShapeDtypeStruct if leaves else pltpu.VMEM
    placed = [
        pltpu.with_memory_space_constraint(value, pltpu.HBM if at in far else pltpu.VMEM)
        for at, value in enumerate(operands)
    ]
    return pl.pallas_call(
        body,
        in_specs=[pl.BlockSpec(memory_space=pltpu.SMEM)]
        + [hbm if at in far else spec for at in range(len(operands))],
        out_specs=[hbm if at < far_outs else spec for at in range(len(out_shapes))],
        out_shape=[shape_of(shape, kind) for shape, kind in out_shapes],
        scratch_shapes=[
            shape if kind is None else pltpu.VMEM(shape, kind) for shape, kind in scratch
        ],
        compiler_params=pltpu.CompilerParams(vmem_limit_bytes=16 * 1024 * 1024),
    )(scalar, *placed)


class Copies:
    def __init__(self, sems):
        self.sems = sems
        self.started = []

    def start(self, source, target):
        copy = pltpu.make_async_copy(source, target, self.sems.at[len(self.started)])
        copy.start()
        self.started.append(copy)

    def wait(self, first=0, last=None):
        for copy in self.started[first:last]:
            copy.wait()


def xor_pairs(size, bit):
    return [(at, at ^ bit) for at in range(size)]


def swap(value, axis, size, bit):
    return lax.ppermute(value, axis, xor_pairs(size, bit))


def lowest_bit(number):
    return number & -number


def gather_parts(value, size):
    got = {0: value}
    for k in range(size - 1, 0, -1):
        if lowest_bit(k) == k:
            got[k] = swap(value, TP, size, k)
    for k in range(1, size):
        low = lowest_bit(k)
        if k != low:
            got[k] = swap(got[k ^ low], TP, size, low)
    return [got[k] for k in range(size)]


def scatter_parts(blocks, size, total=True):
    held = list(blocks)
    for k in range(size - 1, 0, -1):
        low = lowest_bit(k)
        if k != low:
            came = swap(held[k], TP, size, low)
            held[k ^ low] = (held[k ^ low].astype(f32) + came.astype(f32)).astype(bf16)
    hops = [held[0]]
    for k in range(size - 1, 0, -1):
        if lowest_bit(k) == k:
            hops.append(swap(held[k], TP, size, k))
    return sum_of(hops) if total else hops


def sum_of(arrays):
    total = arrays[0].astype(f32)
    for value in arrays[1:]:
        total = total + value.astype(f32)
    return total


def sum_over_dp(keep, send, size, index, between=None, picked=0):
    groups = size // 2
    rows, width = keep.shape[0] // groups, keep.shape[1]
    came = swap(send, DP, size, 1)
    pieces = call_kernel(
        functools.partial(add_split_body, groups),
        index,
        (keep, came),
        [((rows, width), bf16)] * groups,
    )
    came = [swap(pieces[j], DP, size, 2 * j) for j in range(1, groups)]
    outs = [((rows, width), bf16)]
    if picked:
        outs = outs + [((rows, picked), bf16)]
    total, *rest = call_kernel(
        functools.partial(add_body, groups, picked), index, (pieces[0], *came), outs
    )
    if between is not None:
        total = between(total, *rest)
    mine = [total]
    mine = mine + [swap(total, DP, size, 2 * j) for j in range(1, groups)]
    return mine + [swap(piece, DP, size, 1) for piece in mine]


def block(
    inputs,
    segments,
    mixers_norm_gain,
    query_weight,
    key_weight,
    value_weight,
    attention_out,
    mamba_gate,
    mamba_input,
    state_weight,
    step_weight,
    kernel_input,
    kernel_state,
    offset_input,
    offset_state,
    step_bias,
    decay_log,
    skip_gain,
    mamba_out,
    feedforward_norm_gain,
    gate_weight,
    up_weight,
    down_weight,
    cotangent,
    *,
    dp,
    tensor,
):
    local_heads = query_weight.shape[1] // HD
    group = QH // KVH
    assert tensor == 4 and KVH * HD == LANES and 2 * local_heads == group
    rows, width = inputs.shape
    length = rows * tensor
    heads = step_weight.shape[1]
    wq = query_weight.shape[1]
    wkv = 2 * HD
    wx = mamba_input.shape[1]
    wbc = state_weight.shape[1]
    wst = LANES
    units = gate_weight.shape[1]
    kc = kernel_input.shape[0]
    widths = (wq, wkv, wx, wx, wbc, wst)
    t_index = lax.axis_index(TP)
    t_array = jnp.where(
        lax.iota(jnp.int32, 2) == 0, t_index, lax.axis_index(DP)
    ).astype(jnp.int32)

    parts = gather_parts(inputs, tensor)
    cot_parts = gather_parts(cotangent, tensor)

    kv_index = t_index * local_heads // group
    key_slice = lax.dynamic_slice_in_dim(key_weight, kv_index * HD, HD, 1)
    value_slice = lax.dynamic_slice_in_dim(value_weight, kv_index * HD, HD, 1)
    step_pad = jnp.pad(step_weight.T, ((0, LANES - heads), (0, 0)))
    kv_weight = jnp.concatenate([key_slice, value_slice], 1)
    weights = (query_weight, kv_weight, mamba_gate, mamba_input, state_weight, step_pad)
    taps = jnp.concatenate([kernel_input, kernel_state], 1)
    offs = jnp.concatenate([offset_input, offset_state], 0)[None, :]
    bias = jnp.pad(step_bias, (0, LANES - heads))[None, :]
    nega = jnp.pad(-jnp.exp(decay_log), (0, LANES - heads))[None, :]
    skip = jnp.repeat(skip_gain, wx // heads)[None, :]
    square = ((length, length), f32)
    wide_bits = ((length, length), bf16)
    mask, tri, link = call_kernel(
        functools.partial(masks_body, kc),
        t_array,
        (segments[None, :],),
        [square, wide_bits, ((kc - 1, length, LANES), f32)],
    )
    gain1 = mixers_norm_gain[None, :]

    full = (length, width)
    blocks = [((rows, width), bf16)] * tensor
    (n1, qkv, att, stat, z, u, acc, ysum, gated, raw, *held) = call_kernel(
        functools.partial(fwd_body, widths, kc, heads, tensor),
        t_array,
        (*parts, mask, tri, link, gain1, *weights, taps, offs, bias, nega, skip, attention_out, mamba_out),
        [
            (full, bf16),
            ((length, wq + 2 * LANES), bf16),
            ((length, LANES), bf16),
            ((length, LANES), f32),
            ((length, wx), f32),
            ((length, wx + wbc), f32),
            ((length, wx + wbc), f32),
            ((length, wx), f32),
            ((length, wx), bf16),
            ((length, wst), f32),
            square,
            ((length, wst), f32),
            ((wst, length), f32),
            ((length, wst), f32),
            *blocks,
        ],
        [
            (full, bf16),
            (query_weight.shape, bf16),
            (state_weight.shape, bf16),
            (attention_out.shape, bf16),
            (mamba_out.shape, bf16),
            (pltpu.SemaphoreType.DMA((4,)), None),
        ],
        far=(tensor + 4, tensor + 8, tensor + 15, tensor + 16),
    )
    g, run, run_t, dt, *mixed_blocks = held
    probs, weight, mixing, slope, xc, ub, moved, linked = call_kernel(
        functools.partial(ahead_body, widths, kc, heads),
        t_array,
        (mask, link, qkv, stat, u, acc, g, run, run_t, dt),
        [
            ((2, length, length), f32),
            ((heads, length, length), f32),
            ((heads, length, length), bf16),
            ((length, wx + wbc), f32),
            ((length, wx), f32),
            ((length, wx), bf16),
            ((kc - 1, length, wx + wbc), f32),
            wide_bits,
        ],
    )

    inputs_float = inputs.astype(f32)
    hidden_first = inputs_float + scatter_parts(mixed_blocks, tensor)
    reciprocal_second = rms_recip(hidden_first)
    unit_second = hidden_first * reciprocal_second
    local_normed_second = (unit_second * feedforward_norm_gain[None, :]).astype(bf16)
    n2_parts = gather_parts(local_normed_second, tensor)

    stages = (range(tensor - 1), range(tensor - 1, tensor))
    cots = [jnp.concatenate([cot_parts[k] for k in stage], 0) for stage in stages]
    n2s, hiddens, dgus, dn2_blocks = [], [], [], []
    for at, stage in enumerate(stages):
        dhidden = dot_t(cots[at], down_weight)
        span = rows * len(stage)
        n2, hidden, dgu, *dn2_stage = call_kernel(
            lambda scalar, *refs, count=len(stage): feed_body(count, *refs),
            t_array,
            (*[n2_parts[k] for k in stage], dhidden, gate_weight, up_weight),
            [
                ((span, width), bf16),
                ((span, units), bf16),
                ((span, 2 * units), bf16),
                *blocks[: len(stage)],
            ],
        )
        n2s.append(n2)
        hiddens.append(hidden)
        dgus.append(dgu)
        dn2_blocks.extend(dn2_stage)
    dn2 = scatter_parts(dn2_blocks, tensor)
    scaled_second = dn2 * feedforward_norm_gain[None, :]
    grad_hidden = cotangent.astype(f32) + reciprocal_second * (
        scaled_second - unit_second * jnp.mean(scaled_second * unit_second, axis=-1, keepdims=True)
    )
    feed_grad = jnp.sum(dn2 * unit_second, axis=0)
    dparts = gather_parts(grad_hidden.astype(bf16), tensor)

    span = width // 2 + units // 2
    feed_keep, feed_send = call_kernel(
        functools.partial(feed_grads_body, dp // 2),
        t_array,
        (*n2s, *dgus, *hiddens, *cots),
        [((span, width), bf16)] * 2,
    )
    feed_sum = sum_over_dp(feed_keep, feed_send, dp, t_array)

    mid_rows = wq + wx
    d1, dssm, mid_keep, mid_send = call_kernel(
        functools.partial(attention_bwd_body, widths, heads, tensor),
        t_array,
        (
            *dparts, skip, attention_out, mamba_out, probs, xc,
            qkv, att, z, ysum, gated, n1,
        ),
        [
            ((length, wq + wkv + wx), bf16),
            ((length, wx), f32),
            ((mid_rows, width), bf16),
            ((mid_rows, width), bf16),
        ],
        [(full, bf16)],
    )
    mid_sum = sum_over_dp(mid_keep, mid_send, dp, t_array)

    feed_blocks = []
    for hidden, stage in zip(hiddens, stages):
        feed_part = dot(hidden, down_weight).astype(bf16)
        feed_blocks += [feed_part[k * rows : (k + 1) * rows] for k in range(len(stage))]
    feed_total = scatter_parts(feed_blocks, tensor)
    hidden_held, feed_total = lax.optimization_barrier((hidden_first, feed_total))
    output = (hidden_held + feed_total).astype(bf16)

    wl = wkv + wbc + wst + wx
    late_keep, late_send, *dn1_blocks = call_kernel(
        functools.partial(state_bwd_body, widths, kc, heads, tensor),
        t_array,
        (
            gain1, *weights, taps, nega, skip, weight, mixing, slope, xc, ub, moved, linked, dt, link,
            n1, u, acc, ysum, raw, d1, dssm, feed_grad[None, :],
        ),
        [((width // 2, wl), bf16), ((width // 2, wl), bf16), *blocks],
        [
            ((length, wx + wbc + wst), bf16),
            ((2 * kc, wx + wbc), f32),
            (full, bf16),
            square,
            ((length, wx + wbc), f32),
            ((LANES, width), f32),
        ],
    )
    dn1_hops = scatter_parts(dn1_blocks, tensor, total=False)
    picked = wkv + wbc + wst
    wide = 2 * KVH * HD + wbc + wst + wx

    def combine(own, shared):
        pair = shared + swap(shared, TP, tensor, 1)
        (out,) = call_kernel(
            functools.partial(combine_body, widths, heads, 2 * kc, local_heads),
            t_array,
            (own, pair, swap(pair, TP, tensor, 2)),
            [((own.shape[0], wide), bf16)],
        )
        return out

    late_sum = sum_over_dp(late_keep, late_send, dp, t_array, combine, picked)

    (dn1_hops, _) = lax.optimization_barrier((dn1_hops, late_sum[len(late_sum) // 2 :]))
    (block_input_gradient,) = call_kernel(
        input_grad_body,
        t_array,
        (*dn1_hops, inputs, grad_hidden, gain1),
        [((rows, width), f32)],
        leaves=True,
    )
    groups = dp // 2
    feed_shapes = [((width, units), f32), ((width, units), f32), ((units, width), f32)]
    grad_gate, grad_up, grad_down = call_kernel(
        functools.partial(feed_out_body, groups),
        t_array,
        feed_sum,
        feed_shapes,
        [*feed_shapes, (pltpu.SemaphoreType.DMA((6 * groups,)), None)],
        leaves=True,
        far_outs=3,
    )
    mid_shapes = [((wq, width), f32), ((wx, width), f32), ((width, wx), f32), ((width, wq), f32)]
    grad_attn_out, grad_mamba_out, grad_mgate, grad_query = call_kernel(
        functools.partial(mid_out_body, widths, groups),
        t_array,
        mid_sum,
        mid_shapes,
        [*mid_shapes, ((2 * (wq + wx), width), bf16), (pltpu.SemaphoreType.DMA((4,)), None)],
        leaves=True,
        far_outs=4,
    )
    late_shapes = [
        ((width, KVH * HD), f32),
        ((width, KVH * HD), f32),
        ((width, wbc), f32),
        ((width, wx), f32),
    ]
    (
        grad_key,
        grad_value,
        grad_state,
        grad_minput,
        grad_step,
        grad_kinput,
        grad_oinput,
        grad_skip,
        grad_sbias,
        grad_dlog,
        mixers_grad,
        feedforward_grad,
        grad_kstate,
        grad_ostate,
    ) = call_kernel(
        functools.partial(late_out_body, widths, heads, kc, groups),
        t_array,
        late_sum,
        [
            *late_shapes,
            ((heads, width), f32),
            ((kc, wx), f32),
            ((1, wx), f32),
            ((1, heads), f32),
            ((1, heads), f32),
            ((1, heads), f32),
            ((1, width), f32),
            ((1, width), f32),
            ((kc, wbc), f32),
            ((1, wbc), f32),
        ],
        [
            *late_shapes,
            ((width, wide), bf16),
            ((LANES, width), f32),
            (pltpu.SemaphoreType.DMA((4,)), None),
        ],
        leaves=True,
        far_outs=4,
    )
    grad_step = grad_step.T
    grad_oinput, grad_skip, grad_sbias, grad_dlog, mixers_grad, feedforward_grad, grad_ostate = (
        value[0]
        for value in (
            grad_oinput, grad_skip, grad_sbias, grad_dlog, mixers_grad, feedforward_grad, grad_ostate
        )
    )
    return (
        output,
        block_input_gradient,
        mixers_grad,
        grad_query,
        grad_key,
        grad_value,
        grad_attn_out,
        grad_mgate,
        grad_minput,
        grad_state,
        grad_step,
        grad_kinput,
        grad_kstate,
        grad_oinput,
        grad_ostate,
        grad_sbias,
        grad_dlog,
        grad_skip,
        grad_mamba_out,
        feedforward_grad,
        grad_gate,
        grad_up,
        grad_down,
    )


def solution(mesh):
    in_specs = (
        P((DP, TP), None),
        P(DP),
        P(),
        P(None, TP),
        P(),
        P(),
        P(TP, None),
        P(None, TP),
        P(None, TP),
        P(),
        P(None, TP),
        P(None, TP),
        P(),
        P(TP),
        P(),
        P(TP),
        P(TP),
        P(TP),
        P(TP, None),
        P(),
        P(None, TP),
        P(None, TP),
        P(TP, None),
        P((DP, TP), None),
    )
    out_specs = (
        P((DP, TP), None),
        P((DP, TP), None),
        P(),
        P(None, TP),
        P(),
        P(),
        P(TP, None),
        P(None, TP),
        P(None, TP),
        P(),
        P(None, TP),
        P(None, TP),
        P(),
        P(TP),
        P(),
        P(TP),
        P(TP),
        P(TP),
        P(TP, None),
        P(),
        P(None, TP),
        P(None, TP),
        P(TP, None),
    )
    body = functools.partial(block, dp=mesh.shape[DP], tensor=mesh.shape[TP])
    return jax.shard_map(body, mesh=mesh, in_specs=in_specs, out_specs=out_specs, check_vma=False)
```

```python
import functools

import jax
import jax.numpy as jnp
from jax import lax
from jax.experimental import pallas as pl
from jax.experimental.pallas import tpu as pltpu
from jax.sharding import PartitionSpec as P


QH = 8
KVH = 2
HD = 64
LANES = 128
BLOCKS = 4
FWD_BLOCKS = 2

eps = 1e-05
big_negative = -1e30
f32 = jnp.float32
bf16 = jnp.bfloat16

DP = "dp"
TP = "tensor"


def dot(left, right):
    return jnp.dot(left, right, preferred_element_type=f32)


def tdot(left, right):
    return lax.dot_general(left, right, (((0,), (0,)), ((), ())), preferred_element_type=f32)


def dot_t(left, right):
    return lax.dot_general(left, right, (((1,), (1,)), ((), ())), preferred_element_type=f32)


def split3(value):
    high = value.astype(bf16)
    rest = value - high.astype(f32)
    mid = rest.astype(bf16)
    return high, mid, (rest - mid.astype(f32)).astype(bf16)


def exact_left(mask, value):
    high, mid, low = split3(value)
    return dot(mask, high) + (dot(mask, mid) + dot(mask, low))


def rms_recip(values):
    return lax.rsqrt(jnp.mean(values * values, axis=-1, keepdims=True) + eps)


def sigmoid(value):
    return 1.0 / (1.0 + jnp.exp(-value))


def lane_ids(rows, width):
    return lax.broadcasted_iota(jnp.int32, (rows, width), 1)


def pair_columns(values, pair, lanes):
    first = values[:, 2 * pair : 2 * pair + 1]
    second = values[:, 2 * pair + 1 : 2 * pair + 2]
    return jnp.where(lanes < HD, first, second)


def masks_body(taps_count, t_ref, seg_ref, mask_ref, tri_ref, link_ref):
    length = mask_ref.shape[0]
    seg_row = seg_ref[0:1, :].astype(f32)
    seg_col = jnp.broadcast_to(seg_row, (LANES, length)).T
    row_pos = lax.broadcasted_iota(jnp.int32, (length, length), 0)
    col_pos = lax.broadcasted_iota(jnp.int32, (length, length), 1)
    allowed = (row_pos >= col_pos) & (seg_col[:, 0:1] == seg_row)
    mask_ref[...] = jnp.where(allowed, 0.0, big_negative)
    tri_ref[...] = (row_pos >= col_pos).astype(f32).astype(bf16)
    spots = lax.broadcasted_iota(jnp.int32, (length, LANES), 0)
    for shift_by in range(1, taps_count):
        linked = (pltpu.roll(seg_col, shift_by, 0) == seg_col) & (spots >= shift_by)
        link_ref[shift_by - 1] = jnp.where(linked, 1.0, 0.0)


def ahead_body(
    widths, taps_count, heads, t_ref, mask_ref, link_ref, qkv_ref, stat_ref, u_ref, acc_ref,
    g_ref, run_ref, run_t_ref, dt_ref,
    probs_ref, weight_ref, mixing_ref, slope_ref, xc_ref, ub_ref, moved_ref, linked_ref,
):
    wq, _, _, _, _, _ = widths
    length = acc_ref.shape[0]
    lanes = lane_ids(length, LANES)
    lane_lo = lanes < HD
    half = length // BLOCKS
    scale = HD ** (-0.5)
    keys2 = qkv_ref[:, wq : wq + LANES]
    for head in range(2):
        keep = lane_lo if head == 0 else ~lane_lo
        q_m = jnp.where(keep, qkv_ref[:, 0:wq].astype(f32), 0.0).astype(bf16)
        logsum = stat_ref[:, head * HD : head * HD + 1]
        for block in range(BLOCKS):
            lo, hi = block * half, (block + 1) * half
            scores = dot_t(q_m[lo:hi], keys2[:hi]) * scale + mask_ref[lo:hi, 0:hi]
            probs_ref[head, lo:hi, 0:hi] = jnp.exp(scores - logsum[lo:hi])
    run = run_ref[...]
    run_t = run_t_ref[...]
    for head in range(heads):
        for block in range(BLOCKS):
            lo, hi = block * half, (block + 1) * half
            spread = run[lo:hi, head : head + 1] - run_t[head : head + 1, 0:hi]
            weight = jnp.exp(spread + mask_ref[lo:hi, 0:hi])
            weight_ref[head, lo:hi, 0:hi] = weight
            mixing_ref[head, lo:hi, 0:hi] = (weight * g_ref[lo:hi, 0:hi]).astype(bf16)
    acc = acc_ref[...]
    sig = sigmoid(acc)
    slope_ref[...] = sig * (1.0 + acc * (1.0 - sig))
    for pair in range(heads // 2):
        cols = slice(pair * LANES, (pair + 1) * LANES)
        xc = acc[:, cols] * sig[:, cols]
        xc_ref[:, cols] = xc
        ub_ref[:, cols] = (xc * pair_columns(dt_ref[...], pair, lanes)).astype(bf16)
    u = u_ref[...]
    for shift_by in range(1, taps_count):
        moved_ref[shift_by - 1] = link_ref[shift_by - 1, :, 0:1] * pltpu.roll(u, shift_by, 0)
    linked_ref[...] = jnp.where(mask_ref[...] == 0.0, 1.0, 0.0).astype(bf16)


def fwd_body(widths, taps_count, heads, tensor, *refs):
    (t_ref,) = refs[:1]
    parts = refs[1 : 1 + tensor]
    (
        mask_ref,
        tri_ref,
        link_ref,
        gain_ref,
        query_w_ref,
        kv_w_ref,
        gate_w_ref,
        input_w_ref,
        state_w_ref,
        step_w_ref,
        taps_ref,
        offs_ref,
        bias_ref,
        nega_ref,
        skip_ref,
        att_w_ref,
        mam_w_ref,
        n1_ref,
        qkv_ref,
        att_ref,
        stat_ref,
        z_ref,
        u_ref,
        acc_ref,
        ysum_ref,
        gated_ref,
        raw_ref,
        g_ref,
        run_ref,
        run_t_ref,
        dt_ref,
        *mixed_refs,
        mixed_ref,
        query_v,
        state_v,
        att_v,
        mam_v,
        sems,
    ) = refs[1 + tensor :]
    wq, _, _, wx, wbc, _ = widths
    copies = Copies(sems)
    for source, target in (
        (query_w_ref, query_v),
        (state_w_ref, state_v),
        (att_w_ref, att_v),
        (mam_w_ref, mam_v),
    ):
        copies.start(source, target)
    t = t_ref[0]
    rows = parts[0].shape[0]
    length = rows * tensor
    state = wbc // 2
    for k in range(tensor):
        xf = parts[k][...].astype(f32)
        normed = (xf * rms_recip(xf) * gain_ref[...]).astype(bf16)
        n1_ref[pl.ds(pl.multiple_of((t ^ k) * rows, rows), rows), :] = normed
    n1 = n1_ref[...]
    copies.wait(0, 1)
    query = dot(n1, query_v[...]).astype(bf16)
    kv = dot(n1, kv_w_ref[...])
    lanes = lane_ids(length, LANES)
    kv_swap = pltpu.roll(kv, HD, 1)
    keys2 = jnp.where(lanes < HD, kv, kv_swap).astype(bf16)
    values2 = jnp.where(lanes < HD, kv_swap, kv).astype(bf16)
    qkv_ref[:, 0:wq] = query
    qkv_ref[:, wq : wq + LANES] = keys2
    qkv_ref[:, wq + LANES :] = values2
    z_ref[...] = dot(n1, gate_w_ref[...])
    u_ref[:, :wx] = dot(n1, input_w_ref[...])
    copies.wait(1, 2)
    u_ref[:, wx:] = dot(n1, state_v[...])
    raw = dot_t(n1, step_w_ref[...]) + bias_ref[...]
    raw_ref[...] = raw

    lane_lo = lanes < HD
    scale = HD ** (-0.5)
    half = length // FWD_BLOCKS
    for block in range(FWD_BLOCKS):
        lo, hi = block * half, (block + 1) * half
        out = jnp.zeros((half, LANES), f32)
        stats = []
        for head in range(2):
            keep = lane_lo[:half] if head == 0 else ~lane_lo[:half]
            keep_v = lane_lo[:hi] if head == 0 else ~lane_lo[:hi]
            q_rows = jnp.where(keep, query[lo:hi].astype(f32), 0.0).astype(bf16)
            scores = dot_t(q_rows, keys2[:hi]) * scale + mask_ref[lo:hi, 0:hi]
            top = jnp.max(scores, axis=-1, keepdims=True)
            expo = jnp.exp(scores - top)
            total = jnp.sum(expo, axis=-1, keepdims=True)
            probs = (expo / total).astype(bf16)
            v_rows = jnp.where(keep_v, values2[:hi].astype(f32), 0.0).astype(bf16)
            out = out + dot(probs, v_rows)
            stats.append(top + jnp.log(total))
        att_ref[lo:hi, :] = out.astype(bf16)
        stat_ref[lo:hi, :] = jnp.where(lane_lo[:half], stats[0], stats[1])

    u = u_ref[...]
    acc = offs_ref[...] + taps_ref[0:1, :] * u
    for shift_by in range(1, taps_count):
        acc = acc + taps_ref[shift_by : shift_by + 1, :] * (
            link_ref[shift_by - 1, :, 0:1] * pltpu.roll(u, shift_by, 0)
        )
    acc_ref[...] = acc

    dt = jnp.maximum(raw, 0.0) + jnp.log1p(jnp.exp(-jnp.abs(raw)))
    run = exact_left(tri_ref[...], dt * nega_ref[...])
    run_t = run.T
    dt_ref[...] = dt
    run_ref[...] = run
    run_t_ref[...] = run_t
    bc = acc_ref[:, wx:]
    bc = (bc * sigmoid(bc)).astype(bf16)
    g_ref[...] = dot_t(bc[:, state:], bc[:, :state])
    for pair in range(heads // 2):
        cols = slice(pair * LANES, (pair + 1) * LANES)
        xa = acc_ref[:, cols]
        xc = xa * sigmoid(xa)
        uu = xc * pair_columns(dt, pair, lanes)
        u_lo = jnp.where(lane_lo, uu, 0.0).astype(bf16)
        u_hi = jnp.where(lane_lo, 0.0, uu).astype(bf16)
        for block in range(FWD_BLOCKS):
            lo, hi = block * half, (block + 1) * half
            total = jnp.zeros((half, LANES), f32)
            for side, masked in ((0, u_lo), (1, u_hi)):
                head = 2 * pair + side
                spread = run[lo:hi, head : head + 1] - run_t[head : head + 1, 0:hi]
                weight = jnp.exp(spread + mask_ref[lo:hi, 0:hi])
                mixing = (weight * g_ref[lo:hi, 0:hi]).astype(bf16)
                total = total + dot(mixing, masked[:hi])
            ysum_ref[lo:hi, cols] = total
        y = ysum_ref[:, cols] + skip_ref[0:1, cols] * xc
        z = z_ref[:, cols]
        gated_ref[:, cols] = (y * z * sigmoid(z)).astype(bf16)
    copies.wait(2)
    mixed = dot(att_ref[...], att_v[...]) + dot(gated_ref[...], mam_v[...])
    mixed_ref[...] = mixed.astype(bf16)
    for k in range(tensor):
        mixed_refs[k][...] = mixed_ref[pl.ds(pl.multiple_of((t ^ k) * rows, rows), rows), :]


def attention_bwd_body(widths, heads, tensor, *refs):
    t_ref = refs[0]
    dparts = refs[1 : 1 + tensor]
    (
        skip_ref,
        att_w_ref,
        mam_w_ref,
        probs_ref,
        xc_ref,
        qkv_ref,
        att_ref,
        z_ref,
        ysum_ref,
        gated_ref,
        n1_ref,
        d_ref,
        dssm_ref,
        keep_ref,
        send_ref,
        dmixed_ref,
    ) = refs[1 + tensor :]
    wq, wkv, _, wx, _, _ = widths
    t = t_ref[0]
    rows = dparts[0].shape[0]
    length = rows * tensor
    for k in range(tensor):
        dmixed_ref[pl.ds(pl.multiple_of((t ^ k) * rows, rows), rows), :] = dparts[k][...]
    dmixed = dmixed_ref[...]
    lane_lo = lane_ids(length, LANES) < HD
    half = length // BLOCKS
    scale = HD ** (-0.5)

    datt = dot_t(dmixed, att_w_ref[...]).astype(bf16)
    datt_f = datt.astype(f32)
    prod = datt_f * att_ref[...].astype(f32)
    query = qkv_ref[:, 0:wq]
    keys2 = qkv_ref[:, wq : wq + LANES]
    values2 = qkv_ref[:, wq + LANES :]
    dq = [jnp.zeros((half, LANES), f32) for _ in range(BLOCKS)]
    dk = [jnp.zeros((half, LANES), f32) for _ in range(BLOCKS)]
    dv = [jnp.zeros((half, LANES), f32) for _ in range(BLOCKS)]
    for head in range(2):
        keep = lane_lo if head == 0 else ~lane_lo
        q_m = jnp.where(keep, query.astype(f32), 0.0).astype(bf16)
        k_m = jnp.where(keep, keys2.astype(f32), 0.0).astype(bf16)
        d_m = jnp.where(keep, datt_f, 0.0).astype(bf16)
        delta = jnp.sum(jnp.where(keep, prod, 0.0), axis=-1, keepdims=True)
        for block in range(BLOCKS):
            lo, hi = block * half, (block + 1) * half
            probs = probs_ref[head, lo:hi, 0:hi]
            dprob = dot_t(d_m[lo:hi], values2[:hi])
            dscore = (probs * (dprob - delta[lo:hi]) * scale).astype(bf16)
            dq[block] = dq[block] + dot(dscore, k_m[:hi])
            dk_add = tdot(dscore, q_m[lo:hi])
            dv_add = tdot(probs.astype(bf16), d_m[lo:hi])
            for part in range(block + 1):
                dk[part] = dk[part] + dk_add[part * half : (part + 1) * half]
                dv[part] = dv[part] + dv_add[part * half : (part + 1) * half]
    for block in range(BLOCKS):
        lo, hi = block * half, (block + 1) * half
        d_ref[lo:hi, 0:wq] = dq[block].astype(bf16)
        dk_sum = dk[block] + pltpu.roll(dk[block], HD, 1)
        dv_sum = dv[block] + pltpu.roll(dv[block], HD, 1)
        d_ref[lo:hi, wq : wq + wkv] = jnp.where(lane_lo[:half], dk_sum, dv_sum).astype(bf16)

    base = wq + wkv
    for pair in range(heads // 2):
        cols = slice(pair * LANES, (pair + 1) * LANES)
        xc = xc_ref[:, cols]
        z = z_ref[:, cols]
        zs = sigmoid(z)
        dgated = dot_t(dmixed, mam_w_ref[cols, :])
        dssm_ref[:, cols] = dgated * z * zs
        y = ysum_ref[:, cols] + skip_ref[0:1, cols] * xc
        dz = dgated * y * zs * (1.0 + z * (1.0 - zs))
        d_ref[:, base + pair * LANES : base + (pair + 1) * LANES] = dz.astype(bf16)
    upper = t_ref[1] % 2
    n1 = n1_ref[...]
    gz = tdot(d_ref[:, base:], n1)
    split_store(upper, tdot(att_ref[...], dmixed), gz[wx - wq :], keep_ref, send_ref, 0)
    second = jnp.concatenate([gz[: wx - wq], tdot(d_ref[:, :wq], n1)], 0)
    split_store(upper, tdot(gated_ref[...], dmixed), second, keep_ref, send_ref, wq)


def state_bwd_body(widths, taps_count, heads, tensor, *refs):
    (
        t_ref,
        gain_ref,
        query_w_ref,
        kv_w_ref,
        gate_w_ref,
        input_w_ref,
        state_w_ref,
        step_w_ref,
        taps_ref,
        nega_ref,
        skip_ref,
        weight_ref,
        mixing_ref,
        slope_ref,
        xc_ref,
        ub_ref,
        moved_ref,
        linked_ref,
        dt_ref,
        link_ref,
        n1_ref,
        u_ref,
        acc_ref,
        ysum_ref,
        raw_ref,
        d1_ref,
        dssm_ref,
        gfeed_ref,
    ) = refs[:28]
    (
        keep_ref,
        send_ref,
        *dn1_refs,
        d2_ref,
        small_ref,
        dn1_ref,
        dg_ref,
        dact_ref,
        rows_ref,
    ) = refs[28:]
    wq, wkv, _, wx, wbc, _ = widths
    t = t_ref[0]
    length = n1_ref.shape[0]
    rows = length // tensor
    state = wbc // 2
    lanes = lane_ids(length, LANES)
    lane_lo = lanes < HD
    half = length // BLOCKS

    raw = raw_ref[...]
    dt = dt_ref[...]
    ld = dt * nega_ref[...]
    bc_acc = acc_ref[:, wx:]
    bc = (bc_acc * sigmoid(bc_acc)).astype(bf16)
    dg_ref[...] = jnp.zeros((length, length), f32)
    drun = jnp.zeros((length, LANES), f32)
    ddt = jnp.zeros((length, LANES), f32)
    skip_row = jnp.zeros((1, LANES), f32)
    small_ref[...] = jnp.zeros(small_ref.shape, f32)
    for pair in range(heads // 2):
        cols = slice(pair * LANES, (pair + 1) * LANES)
        xc = xc_ref[:, cols]
        skip = skip_ref[0:1, cols]
        ysum = ysum_ref[:, cols]
        dssm = dssm_ref[:, cols]
        dskip = jnp.sum(dssm * xc, axis=0, keepdims=True)
        for side in range(2):
            keep = lane_lo[0:1] if side == 0 else ~lane_lo[0:1]
            head_sum = jnp.sum(jnp.where(keep, dskip, 0.0), axis=-1, keepdims=True)
            skip_row = jnp.where(lanes[0:1] == 2 * pair + side, head_sum, skip_row)
        dt_pair = pair_columns(dt, pair, lanes)
        u_b = ub_ref[:, cols]
        dy_b = dssm.astype(bf16)
        u_f = u_b.astype(f32)
        dy_f = dy_b.astype(f32)
        du = [jnp.zeros((half, LANES), f32) for _ in range(BLOCKS)]
        for side in range(2):
            head = 2 * pair + side
            keep = lane_lo if side == 0 else ~lane_lo
            dy_m = jnp.where(keep, dy_f, 0.0).astype(bf16)
            for block in range(BLOCKS):
                lo, hi = block * half, (block + 1) * half
                weight = weight_ref[head, lo:hi, 0:hi]
                mixing = mixing_ref[head, lo:hi, 0:hi]
                dmix = dot_t(dy_m[lo:hi], u_b[:hi])
                dg_ref[lo:hi, 0:hi] += weight * dmix
                du_add = tdot(mixing, dy_m[lo:hi])
                for part in range(block + 1):
                    du[part] = du[part] + du_add[part * half : (part + 1) * half]
        du = jnp.concatenate(du, 0)
        balance = dy_f * ysum - u_f * du
        weighted = du * xc
        for side in range(2):
            head = 2 * pair + side
            keep = lane_lo if side == 0 else ~lane_lo
            here = lanes == head
            drun = jnp.where(
                here, jnp.sum(jnp.where(keep, balance, 0.0), axis=-1, keepdims=True), drun
            )
            ddt = jnp.where(
                here, jnp.sum(jnp.where(keep, weighted, 0.0), axis=-1, keepdims=True), ddt
            )
        dact_ref[:, cols] = du * dt_pair + skip * dssm
    dg = dg_ref[...].astype(bf16)
    dact_ref[:, wx : wx + state] = tdot(dg, bc[:, state:])
    dact_ref[:, wx + state :] = dot(dg, bc[:, :state])
    linked = linked_ref[...]
    high, mid, low = split3(drun)
    dld = tdot(linked, high) + (tdot(linked, mid) + tdot(linked, low))
    ddt = ddt + dld * nega_ref[...]
    dstep = ddt * sigmoid(raw)
    d2_ref[:, wx + wbc :] = dstep.astype(bf16)

    dconv = dact_ref[...] * slope_ref[...]
    u = u_ref[...]
    small_ref[0:1, :] = jnp.sum(dconv * u, axis=0, keepdims=True)
    small_ref[taps_count : taps_count + 1, :] = jnp.sum(dconv, axis=0, keepdims=True)
    du_in = dconv * taps_ref[0:1, :]
    for shift_by in range(1, taps_count):
        masked = dconv * link_ref[shift_by - 1, :, 0:1]
        small_ref[shift_by : shift_by + 1, :] = jnp.sum(
            dconv * moved_ref[shift_by - 1], axis=0, keepdims=True
        )
        du_in = du_in + taps_ref[shift_by : shift_by + 1, :] * pltpu.roll(
            masked, length - shift_by, 0
        )
    d2_ref[:, 0 : wx + wbc] = du_in.astype(bf16)
    small_ref[taps_count + 1 : taps_count + 2, 0:LANES] = skip_row
    small_ref[taps_count + 2 : taps_count + 3, 0:LANES] = jnp.sum(dstep, axis=0, keepdims=True)
    small_ref[taps_count + 3 : taps_count + 4, 0:LANES] = jnp.sum(dld * ld, axis=0, keepdims=True)
    dn1 = dot_t(d1_ref[:, :wq], query_w_ref[...]) + dot_t(d1_ref[:, wq : wq + wkv], kv_w_ref[...])
    dn1 = dn1 + dot_t(d1_ref[:, wq + wkv :], gate_w_ref[...])
    dn1 = dn1 + dot_t(d2_ref[:, :wx], input_w_ref[...])
    dn1 = dn1 + dot_t(d2_ref[:, wx : wx + wbc], state_w_ref[...])
    dn1 = dn1 + dot(d2_ref[:, wx + wbc :], step_w_ref[...])
    dn1_ref[...] = dn1.astype(bf16)
    for k in range(tensor):
        dn1_refs[k][...] = dn1_ref[pl.ds(pl.multiple_of((t ^ k) * rows, rows), rows), :]
    gmix = jnp.sum(dn1 * n1_ref[...].astype(f32), axis=0, keepdims=True) / gain_ref[...]
    late_grads(
        widths, heads, t_ref[1] % 2, n1_ref, d1_ref, d2_ref, small_ref, gmix, gfeed_ref[...],
        keep_ref, send_ref, rows_ref,
    )


def feed_body(count, *refs):
    parts = refs[:count]
    dhidden_ref, gate_ref, up_ref, n2_ref, hidden_ref, dgu_ref = refs[count : count + 6]
    dn2_refs = refs[count + 6 :]
    rows = parts[0].shape[0]
    units = gate_ref.shape[1]
    for k in range(count):
        n2_ref[k * rows : (k + 1) * rows, :] = parts[k][...]
    n2 = n2_ref[...]
    gate_pre = dot(n2, gate_ref[...])
    up_pre = dot(n2, up_ref[...])
    gsig = sigmoid(gate_pre)
    gate_act = gate_pre * gsig
    dhidden = dhidden_ref[...]
    dgate = (dhidden * up_pre * gsig * (1.0 + gate_pre * (1.0 - gsig))).astype(bf16)
    dup = (dhidden * gate_act).astype(bf16)
    dn2 = (dot_t(dgate, gate_ref[...]) + dot_t(dup, up_ref[...])).astype(bf16)
    for k in range(count):
        dn2_refs[k][...] = dn2[k * rows : (k + 1) * rows]
    hidden_ref[...] = (gate_act * up_pre).astype(bf16)
    dgu_ref[:, :units] = dgate
    dgu_ref[:, units:] = dup


def split_store(upper, first, second, keep_ref, send_ref, at):
    size = first.shape[0]
    low = upper == 0
    keep_ref[at : at + size, :] = jnp.where(low, first, second).astype(bf16)
    send_ref[at : at + size, :] = jnp.where(low, second, first).astype(bf16)


def feed_grads_body(groups, u_ref, *refs):
    n2_refs, dgu_refs, hidden_refs, cot_refs = refs[0:2], refs[2:4], refs[4:6], refs[6:8]
    keep_ref, send_ref = refs[8:]
    half_wide = n2_refs[0].shape[1] // 2
    half_tall = hidden_refs[0].shape[1] // 2
    wide, tall = half_wide // groups, half_tall // groups
    low = u_ref[1] % 2 == 0
    for sources, others, half, size, skip in (
        (n2_refs, dgu_refs, half_wide, wide, 0),
        (hidden_refs, cot_refs, half_tall, tall, wide),
    ):
        first, second = (
            sum(
                tdot(source[:, side * half : (side + 1) * half], other[...])
                for source, other in zip(sources, others)
            )
            for side in range(2)
        )
        keep = jnp.where(low, first, second).astype(bf16)
        send = jnp.where(low, second, first).astype(bf16)
        for q in range(groups):
            at = q * (wide + tall) + skip
            keep_ref[at : at + size, :] = keep[q * size : (q + 1) * size]
            send_ref[at : at + size, :] = send[q * size : (q + 1) * size]


def late_grads(
    widths, heads, upper, n1_ref, d1_ref, d2_ref, small_ref, gmix, gfeed,
    keep_ref, send_ref, rows_ref,
):
    wq, wkv, _, wx, wbc, wst = widths
    count = small_ref.shape[0]
    width = n1_ref.shape[1]
    half = width // 2
    rows_ref[...] = jnp.zeros(rows_ref.shape, f32)
    at = heads
    rows_ref[at : at + count, 0:wx] = small_ref[:, :wx]
    at += count
    rows_ref[at : at + 1, :] = gmix
    rows_ref[at + 1 : at + 2, :] = gfeed
    at += 2
    rows_ref[at : at + count, 0:wbc] = small_ref[:, wx:]
    extra = rows_ref[...].T
    low = upper == 0
    for source, columns, where_to in (
        (d1_ref, (wq, wq + wkv), 0),
        (d2_ref, (wx, wx + wbc), wkv),
        (d2_ref, (wx + wbc, wx + wbc + wst), wkv + wbc),
        (d2_ref, (0, wx), wkv + wbc + wst),
    ):
        grads = tdot(n1_ref[...], source[:, columns[0] : columns[1]])
        if columns[0] == wx + wbc:
            grads = grads + extra
        first, second = grads[:half], grads[half:]
        span = slice(where_to, where_to + columns[1] - columns[0])
        keep_ref[:, span] = jnp.where(low, first, second).astype(bf16)
        send_ref[:, span] = jnp.where(low, second, first).astype(bf16)


def combine_body(widths, heads, counts, local_heads, t_ref, own_ref, sum_ref, other_ref, out_ref):
    _, wkv, _, _, wbc, wst = widths
    t = t_ref[0]
    group = QH // KVH
    picked = wkv + wbc + wst
    lanes = lane_ids(own_ref.shape[0], LANES)
    first = t * local_heads // group == 0
    own = own_ref[:, :picked].astype(f32)
    mine = sum_ref[...].astype(f32)
    other = other_ref[...].astype(f32)
    low = jnp.where(first, mine[:, :wkv], other[:, :wkv])
    high = jnp.where(first, other[:, :wkv], mine[:, :wkv])
    out_ref[:, :LANES] = jnp.where(lanes < HD, low, pltpu.roll(high, HD, 1)).astype(bf16)
    out_ref[:, LANES : 2 * LANES] = jnp.where(lanes < HD, pltpu.roll(low, HD, 1), high).astype(
        bf16
    )
    total = mine[:, wkv:] + other[:, wkv:]
    at = 2 * LANES
    out_ref[:, at : at + wbc] = total[:, :wbc].astype(bf16)
    at += wbc
    extra = jnp.where(lanes < heads + counts, own[:, wkv + wbc :], total[:, wbc:])
    out_ref[:, at : at + wst] = extra.astype(bf16)
    at += wst
    out_ref[:, at:] = own_ref[:, picked:]


def input_grad_body(t_ref, *refs):
    *hops, inputs_ref, dhidden_ref, gain_ref, out_ref = refs
    xf = inputs_ref[...].astype(f32)
    recip = rms_recip(xf)
    unit = xf * recip
    scaled = sum_of([hop[...] for hop in hops]) * gain_ref[...]
    mean = jnp.mean(scaled * unit, axis=-1, keepdims=True)
    out_ref[...] = dhidden_ref[...] + recip * (scaled - unit * mean)


def piece_places(d, groups):
    for side in range(2):
        half = d % 2 if side == 0 else 1 - d % 2
        for j in range(groups):
            yield side * groups + j, half, (d // 2) ^ j


def merge_rows(d, groups, pieces, full_ref):
    rows = pieces[0].shape[0]
    for at, half, group in piece_places(d, groups):
        where_to = pl.multiple_of((half * groups + group) * rows, rows)
        full_ref[pl.ds(where_to, rows), :] = pieces[at][...]


def feed_out_body(groups, d_ref, *refs):
    pieces = refs[: 2 * groups]
    gate_ref, up_ref, down_ref, gate_stage, up_stage, down_stage, sems = refs[2 * groups :]
    width, units = gate_ref.shape
    wide, tall = width // (2 * groups), units // (2 * groups)
    copies = Copies(sems)
    for at, half, group in piece_places(d_ref[1], groups):
        piece = pieces[at]
        place = half * groups + group
        rows = pl.ds(pl.multiple_of(place * wide, wide), wide)
        gate_stage[rows, :] = piece[:wide, :units].astype(f32)
        copies.start(gate_stage.at[rows, :], gate_ref.at[rows, :])
        up_stage[rows, :] = piece[:wide, units:].astype(f32)
        copies.start(up_stage.at[rows, :], up_ref.at[rows, :])
        rows = pl.ds(pl.multiple_of(place * tall, tall), tall)
        down_stage[rows, :] = piece[wide:, :].astype(f32)
        copies.start(down_stage.at[rows, :], down_ref.at[rows, :])
    copies.wait()


def mid_out_body(widths, groups, d_ref, *refs):
    wq, _, _, wx, _, _ = widths
    outs = refs[2 * groups : 2 * groups + 4]
    stages = refs[2 * groups + 4 : 2 * groups + 8]
    full_ref, sems = refs[2 * groups + 8 :]
    att_stage, mam_stage, gate_stage, query_stage = stages
    merge_rows(d_ref[1], groups, refs[: 2 * groups], full_ref)
    copies = Copies(sems)
    mam_stage[...] = full_ref[wq : wq + wx, :].astype(f32)
    copies.start(mam_stage, outs[1])
    att_stage[...] = full_ref[:wq, :].astype(f32)
    copies.start(att_stage, outs[0])
    at = wq + wx
    gate_stage[:, wx - wq :] = full_ref[at : at + wq, :].astype(f32).T
    gate_stage[:, : wx - wq] = full_ref[at + wq : at + wx, :].astype(f32).T
    copies.start(gate_stage, outs[2])
    query_stage[...] = full_ref[at + wx :, :].astype(f32).T
    copies.start(query_stage, outs[3])
    copies.wait()


def late_out_body(widths, heads, taps_count, groups, d_ref, *refs):
    _, _, _, wx, wbc, wst = widths
    big = refs[2 * groups : 2 * groups + 4]
    (
        step_ref, tap_in_ref, off_in_ref, skip_ref, bias_ref, decay_ref,
        mix_ref, feed_ref, tap_st_ref, off_st_ref,
    ) = refs[2 * groups + 4 : 2 * groups + 14]
    *stages, full_ref, rows_ref, sems = refs[2 * groups + 14 :]
    merge_rows(d_ref[1], groups, refs[: 2 * groups], full_ref)
    copies = Copies(sems)
    sizes = (KVH * HD, KVH * HD, wbc, wx)
    starts = (0, KVH * HD, 2 * KVH * HD, 2 * KVH * HD + wbc + wst)
    for out_ref, stage, size, at in zip(big, stages, sizes, starts):
        stage[...] = full_ref[:, at : at + size].astype(f32)
        copies.start(stage, out_ref)
    at = 2 * KVH * HD + wbc
    rows_ref[...] = full_ref[:, at : at + wst].astype(f32).T
    step_ref[...] = rows_ref[:heads, :]
    at = heads
    tap_in_ref[...] = rows_ref[at : at + taps_count, :wx]
    at += taps_count
    off_in_ref[...] = rows_ref[at : at + 1, :wx]
    skip_ref[...] = rows_ref[at + 1 : at + 2, :heads]
    bias_ref[...] = rows_ref[at + 2 : at + 3, :heads]
    decay_ref[...] = rows_ref[at + 3 : at + 4, :heads]
    at += taps_count
    mix_ref[...] = rows_ref[at : at + 1, :]
    feed_ref[...] = rows_ref[at + 1 : at + 2, :]
    at += 2
    tap_st_ref[...] = rows_ref[at : at + taps_count, :wbc]
    off_st_ref[...] = rows_ref[at + taps_count : at + taps_count + 1, :wbc]
    copies.wait()


def add_split_body(groups, d_ref, keep_ref, came_ref, *outs):
    group = d_ref[1] // 2
    rows = keep_ref.shape[0] // groups
    for j in range(groups):
        at = pl.ds(pl.multiple_of((group ^ j) * rows, rows), rows)
        outs[j][...] = (keep_ref[at, :].astype(f32) + came_ref[at, :].astype(f32)).astype(bf16)


def add_body(groups, picked, d_ref, *refs):
    total = refs[0][...].astype(f32)
    for j in range(1, groups):
        total = total + refs[j][...].astype(f32)
    total = total.astype(bf16)
    refs[groups][...] = total
    if picked:
        refs[groups + 1][...] = total[:, :picked]


def call_kernel(body, scalar, operands, out_shapes, scratch=(), leaves=False, far=(), far_outs=0):
    spec = pl.BlockSpec(memory_space=pltpu.VMEM)
    hbm = pl.BlockSpec(memory_space=pltpu.HBM)
    shape_of = jax.ShapeDtypeStruct if leaves else pltpu.VMEM
    placed = [
        pltpu.with_memory_space_constraint(value, pltpu.HBM if at in far else pltpu.VMEM)
        for at, value in enumerate(operands)
    ]
    return pl.pallas_call(
        body,
        in_specs=[pl.BlockSpec(memory_space=pltpu.SMEM)]
        + [hbm if at in far else spec for at in range(len(operands))],
        out_specs=[hbm if at < far_outs else spec for at in range(len(out_shapes))],
        out_shape=[shape_of(shape, kind) for shape, kind in out_shapes],
        scratch_shapes=[
            shape if kind is None else pltpu.VMEM(shape, kind) for shape, kind in scratch
        ],
        compiler_params=pltpu.CompilerParams(vmem_limit_bytes=16 * 1024 * 1024),
    )(scalar, *placed)


class Copies:
    def __init__(self, sems):
        self.sems = sems
        self.started = []

    def start(self, source, target):
        copy = pltpu.make_async_copy(source, target, self.sems.at[len(self.started)])
        copy.start()
        self.started.append(copy)

    def wait(self, first=0, last=None):
        for copy in self.started[first:last]:
            copy.wait()


def xor_pairs(size, bit):
    return [(at, at ^ bit) for at in range(size)]


def swap(value, axis, size, bit):
    return lax.ppermute(value, axis, xor_pairs(size, bit))


def lowest_bit(number):
    return number & -number


def gather_parts(value, size):
    got = {0: value}
    for k in range(size - 1, 0, -1):
        if lowest_bit(k) == k:
            got[k] = swap(value, TP, size, k)
    for k in range(1, size):
        low = lowest_bit(k)
        if k != low:
            got[k] = swap(got[k ^ low], TP, size, low)
    return [got[k] for k in range(size)]


def scatter_parts(blocks, size, total=True):
    held = list(blocks)
    for k in range(size - 1, 0, -1):
        low = lowest_bit(k)
        if k != low:
            came = swap(held[k], TP, size, low)
            held[k ^ low] = (held[k ^ low].astype(f32) + came.astype(f32)).astype(bf16)
    hops = [held[0]]
    for k in range(size - 1, 0, -1):
        if lowest_bit(k) == k:
            hops.append(swap(held[k], TP, size, k))
    return sum_of(hops) if total else hops


def sum_of(arrays):
    total = arrays[0].astype(f32)
    for value in arrays[1:]:
        total = total + value.astype(f32)
    return total


def sum_over_dp(keep, send, size, index, between=None, picked=0):
    groups = size // 2
    rows, width = keep.shape[0] // groups, keep.shape[1]
    came = swap(send, DP, size, 1)
    pieces = call_kernel(
        functools.partial(add_split_body, groups),
        index,
        (keep, came),
        [((rows, width), bf16)] * groups,
    )
    came = [swap(pieces[j], DP, size, 2 * j) for j in range(1, groups)]
    outs = [((rows, width), bf16)]
    if picked:
        outs = outs + [((rows, picked), bf16)]
    total, *rest = call_kernel(
        functools.partial(add_body, groups, picked), index, (pieces[0], *came), outs
    )
    if between is not None:
        total = between(total, *rest)
    mine = [total]
    mine = mine + [swap(total, DP, size, 2 * j) for j in range(1, groups)]
    return mine + [swap(piece, DP, size, 1) for piece in mine]


def block(
    inputs,
    segments,
    mixers_norm_gain,
    query_weight,
    key_weight,
    value_weight,
    attention_out,
    mamba_gate,
    mamba_input,
    state_weight,
    step_weight,
    kernel_input,
    kernel_state,
    offset_input,
    offset_state,
    step_bias,
    decay_log,
    skip_gain,
    mamba_out,
    feedforward_norm_gain,
    gate_weight,
    up_weight,
    down_weight,
    cotangent,
    *,
    dp,
    tensor,
):
    local_heads = query_weight.shape[1] // HD
    group = QH // KVH
    assert tensor == 4 and KVH * HD == LANES and 2 * local_heads == group
    rows, width = inputs.shape
    length = rows * tensor
    heads = step_weight.shape[1]
    wq = query_weight.shape[1]
    wkv = 2 * HD
    wx = mamba_input.shape[1]
    wbc = state_weight.shape[1]
    wst = LANES
    units = gate_weight.shape[1]
    kc = kernel_input.shape[0]
    widths = (wq, wkv, wx, wx, wbc, wst)
    t_index = lax.axis_index(TP)
    t_array = jnp.where(
        lax.iota(jnp.int32, 2) == 0, t_index, lax.axis_index(DP)
    ).astype(jnp.int32)

    parts = gather_parts(inputs, tensor)
    cot_parts = gather_parts(cotangent, tensor)

    kv_index = t_index * local_heads // group
    key_slice = lax.dynamic_slice_in_dim(key_weight, kv_index * HD, HD, 1)
    value_slice = lax.dynamic_slice_in_dim(value_weight, kv_index * HD, HD, 1)
    step_pad = jnp.pad(step_weight.T, ((0, LANES - heads), (0, 0)))
    kv_weight = jnp.concatenate([key_slice, value_slice], 1)
    weights = (query_weight, kv_weight, mamba_gate, mamba_input, state_weight, step_pad)
    taps = jnp.concatenate([kernel_input, kernel_state], 1)
    offs = jnp.concatenate([offset_input, offset_state], 0)[None, :]
    bias = jnp.pad(step_bias, (0, LANES - heads))[None, :]
    nega = jnp.pad(-jnp.exp(decay_log), (0, LANES - heads))[None, :]
    skip = jnp.repeat(skip_gain, wx // heads)[None, :]
    square = ((length, length), f32)
    wide_bits = ((length, length), bf16)
    mask, tri, link = call_kernel(
        functools.partial(masks_body, kc),
        t_array,
        (segments[None, :],),
        [square, wide_bits, ((kc - 1, length, LANES), f32)],
    )
    gain1 = mixers_norm_gain[None, :]

    full = (length, width)
    blocks = [((rows, width), bf16)] * tensor
    (n1, qkv, att, stat, z, u, acc, ysum, gated, raw, *held) = call_kernel(
        functools.partial(fwd_body, widths, kc, heads, tensor),
        t_array,
        (*parts, mask, tri, link, gain1, *weights, taps, offs, bias, nega, skip, attention_out, mamba_out),
        [
            (full, bf16),
            ((length, wq + 2 * LANES), bf16),
            ((length, LANES), bf16),
            ((length, LANES), f32),
            ((length, wx), f32),
            ((length, wx + wbc), f32),
            ((length, wx + wbc), f32),
            ((length, wx), f32),
            ((length, wx), bf16),
            ((length, wst), f32),
            square,
            ((length, wst), f32),
            ((wst, length), f32),
            ((length, wst), f32),
            *blocks,
        ],
        [
            (full, bf16),
            (query_weight.shape, bf16),
            (state_weight.shape, bf16),
            (attention_out.shape, bf16),
            (mamba_out.shape, bf16),
            (pltpu.SemaphoreType.DMA((4,)), None),
        ],
        far=(tensor + 4, tensor + 8, tensor + 15, tensor + 16),
    )
    g, run, run_t, dt, *mixed_blocks = held
    probs, weight, mixing, slope, xc, ub, moved, linked = call_kernel(
        functools.partial(ahead_body, widths, kc, heads),
        t_array,
        (mask, link, qkv, stat, u, acc, g, run, run_t, dt),
        [
            ((2, length, length), f32),
            ((heads, length, length), f32),
            ((heads, length, length), bf16),
            ((length, wx + wbc), f32),
            ((length, wx), f32),
            ((length, wx), bf16),
            ((kc - 1, length, wx + wbc), f32),
            wide_bits,
        ],
    )

    inputs_float = inputs.astype(f32)
    hidden_first = inputs_float + scatter_parts(mixed_blocks, tensor)
    reciprocal_second = rms_recip(hidden_first)
    unit_second = hidden_first * reciprocal_second
    local_normed_second = (unit_second * feedforward_norm_gain[None, :]).astype(bf16)
    n2_parts = gather_parts(local_normed_second, tensor)

    stages = (range(tensor - 1), range(tensor - 1, tensor))
    cots = [jnp.concatenate([cot_parts[k] for k in stage], 0) for stage in stages]
    n2s, hiddens, dgus, dn2_blocks = [], [], [], []
    for at, stage in enumerate(stages):
        dhidden = dot_t(cots[at], down_weight)
        span = rows * len(stage)
        n2, hidden, dgu, *dn2_stage = call_kernel(
            lambda scalar, *refs, count=len(stage): feed_body(count, *refs),
            t_array,
            (*[n2_parts[k] for k in stage], dhidden, gate_weight, up_weight),
            [
                ((span, width), bf16),
                ((span, units), bf16),
                ((span, 2 * units), bf16),
                *blocks[: len(stage)],
            ],
        )
        n2s.append(n2)
        hiddens.append(hidden)
        dgus.append(dgu)
        dn2_blocks.extend(dn2_stage)
    dn2 = scatter_parts(dn2_blocks, tensor)
    scaled_second = dn2 * feedforward_norm_gain[None, :]
    grad_hidden = cotangent.astype(f32) + reciprocal_second * (
        scaled_second - unit_second * jnp.mean(scaled_second * unit_second, axis=-1, keepdims=True)
    )
    feed_grad = jnp.sum(dn2 * unit_second, axis=0)
    dparts = gather_parts(grad_hidden.astype(bf16), tensor)

    span = width // 2 + units // 2
    feed_keep, feed_send = call_kernel(
        functools.partial(feed_grads_body, dp // 2),
        t_array,
        (*n2s, *dgus, *hiddens, *cots),
        [((span, width), bf16)] * 2,
    )
    feed_sum = sum_over_dp(feed_keep, feed_send, dp, t_array)

    mid_rows = wq + wx
    d1, dssm, mid_keep, mid_send = call_kernel(
        functools.partial(attention_bwd_body, widths, heads, tensor),
        t_array,
        (
            *dparts, skip, attention_out, mamba_out, probs, xc,
            qkv, att, z, ysum, gated, n1,
        ),
        [
            ((length, wq + wkv + wx), bf16),
            ((length, wx), f32),
            ((mid_rows, width), bf16),
            ((mid_rows, width), bf16),
        ],
        [(full, bf16)],
    )
    mid_sum = sum_over_dp(mid_keep, mid_send, dp, t_array)

    feed_blocks = []
    for hidden, stage in zip(hiddens, stages):
        feed_part = dot(hidden, down_weight).astype(bf16)
        feed_blocks += [feed_part[k * rows : (k + 1) * rows] for k in range(len(stage))]
    feed_total = scatter_parts(feed_blocks, tensor)
    hidden_held, feed_total = lax.optimization_barrier((hidden_first, feed_total))
    output = (hidden_held + feed_total).astype(bf16)

    wl = wkv + wbc + wst + wx
    late_keep, late_send, *dn1_blocks = call_kernel(
        functools.partial(state_bwd_body, widths, kc, heads, tensor),
        t_array,
        (
            gain1, *weights, taps, nega, skip, weight, mixing, slope, xc, ub, moved, linked, dt, link,
            n1, u, acc, ysum, raw, d1, dssm, feed_grad[None, :],
        ),
        [((width // 2, wl), bf16), ((width // 2, wl), bf16), *blocks],
        [
            ((length, wx + wbc + wst), bf16),
            ((2 * kc, wx + wbc), f32),
            (full, bf16),
            square,
            ((length, wx + wbc), f32),
            ((LANES, width), f32),
        ],
    )
    dn1_hops = scatter_parts(dn1_blocks, tensor, total=False)
    picked = wkv + wbc + wst
    wide = 2 * KVH * HD + wbc + wst + wx

    def combine(own, shared):
        pair = shared + swap(shared, TP, tensor, 1)
        (out,) = call_kernel(
            functools.partial(combine_body, widths, heads, 2 * kc, local_heads),
            t_array,
            (own, pair, swap(pair, TP, tensor, 2)),
            [((own.shape[0], wide), bf16)],
        )
        return out

    late_sum = sum_over_dp(late_keep, late_send, dp, t_array, combine, picked)

    (dn1_hops, _) = lax.optimization_barrier((dn1_hops, late_sum[len(late_sum) // 2 :]))
    (block_input_gradient,) = call_kernel(
        input_grad_body,
        t_array,
        (*dn1_hops, inputs, grad_hidden, gain1),
        [((rows, width), f32)],
        leaves=True,
    )
    groups = dp // 2
    feed_shapes = [((width, units), f32), ((width, units), f32), ((units, width), f32)]
    grad_gate, grad_up, grad_down = call_kernel(
        functools.partial(feed_out_body, groups),
        t_array,
        feed_sum,
        feed_shapes,
        [*feed_shapes, (pltpu.SemaphoreType.DMA((6 * groups,)), None)],
        leaves=True,
        far_outs=3,
    )
    mid_shapes = [((wq, width), f32), ((wx, width), f32), ((width, wx), f32), ((width, wq), f32)]
    grad_attn_out, grad_mamba_out, grad_mgate, grad_query = call_kernel(
        functools.partial(mid_out_body, widths, groups),
        t_array,
        mid_sum,
        mid_shapes,
        [*mid_shapes, ((2 * (wq + wx), width), bf16), (pltpu.SemaphoreType.DMA((4,)), None)],
        leaves=True,
        far_outs=4,
    )
    late_shapes = [
        ((width, KVH * HD), f32),
        ((width, KVH * HD), f32),
        ((width, wbc), f32),
        ((width, wx), f32),
    ]
    (
        grad_key,
        grad_value,
        grad_state,
        grad_minput,
        grad_step,
        grad_kinput,
        grad_oinput,
        grad_skip,
        grad_sbias,
        grad_dlog,
        mixers_grad,
        feedforward_grad,
        grad_kstate,
        grad_ostate,
    ) = call_kernel(
        functools.partial(late_out_body, widths, heads, kc, groups),
        t_array,
        late_sum,
        [
            *late_shapes,
            ((heads, width), f32),
            ((kc, wx), f32),
            ((1, wx), f32),
            ((1, heads), f32),
            ((1, heads), f32),
            ((1, heads), f32),
            ((1, width), f32),
            ((1, width), f32),
            ((kc, wbc), f32),
            ((1, wbc), f32),
        ],
        [
            *late_shapes,
            ((width, wide), bf16),
            ((LANES, width), f32),
            (pltpu.SemaphoreType.DMA((4,)), None),
        ],
        leaves=True,
        far_outs=4,
    )
    grad_step = grad_step.T
    grad_oinput, grad_skip, grad_sbias, grad_dlog, mixers_grad, feedforward_grad, grad_ostate = (
        value.reshape(-1)
        for value in (
            grad_oinput, grad_skip, grad_sbias, grad_dlog, mixers_grad, feedforward_grad, grad_ostate
        )
    )
    return (
        output,
        block_input_gradient,
        mixers_grad,
        grad_query,
        grad_key,
        grad_value,
        grad_attn_out,
        grad_mgate,
        grad_minput,
        grad_state,
        grad_step,
        grad_kinput,
        grad_kstate,
        grad_oinput,
        grad_ostate,
        grad_sbias,
        grad_dlog,
        grad_skip,
        grad_mamba_out,
        feedforward_grad,
        grad_gate,
        grad_up,
        grad_down,
    )


def solution(mesh):
    in_specs = (
        P((DP, TP), None),
        P(DP),
        P(),
        P(None, TP),
        P(),
        P(),
        P(TP, None),
        P(None, TP),
        P(None, TP),
        P(),
        P(None, TP),
        P(None, TP),
        P(),
        P(TP),
        P(),
        P(TP),
        P(TP),
        P(TP),
        P(TP, None),
        P(),
        P(None, TP),
        P(None, TP),
        P(TP, None),
        P((DP, TP), None),
    )
    out_specs = (
        P((DP, TP), None),
        P((DP, TP), None),
        P(),
        P(None, TP),
        P(),
        P(),
        P(TP, None),
        P(None, TP),
        P(None, TP),
        P(),
        P(None, TP),
        P(None, TP),
        P(),
        P(TP),
        P(),
        P(TP),
        P(TP),
        P(TP),
        P(TP, None),
        P(),
        P(None, TP),
        P(None, TP),
        P(TP, None),
    )
    body = functools.partial(block, dp=mesh.shape[DP], tensor=mesh.shape[TP])
    return jax.shard_map(body, mesh=mesh, in_specs=in_specs, out_specs=out_specs, check_vma=False)
```
